32 devices in a mesh: dp: 4 (over z), expert: 2 (over core), hidden: 4 (over y, x).
Axes of the slice: x: 2, y: 2, z: 4, core: 2. Of those that a mesh axis runs over, the one named last changes fastest.
Arguments:
- patches: bfloat16 [8192, 768], P(('dp', 'expert'), 'hidden'), may hold values from -6 to 6
- cond: bfloat16 [256, 768], P(('dp', 'expert')), may hold values from -6 to 6
- seg_ids: int32 [32, 256], P(('dp', 'expert')), may hold values from 0 to 7, never falling along the last dimension, each value on 1 to 64 neighbouring positions
- seg_image: int32 [32, 8], P(('dp', 'expert')), may hold values from 0 to 31
- routes: int32 [8192, 2], P(('dp', 'expert')), may hold values from 0 to 7, all different within a row; in each aligned block of 1024 rows (0 to 1023, 1024 to 2047, ...) at most 384 rows name the same one
- gates: float32 [8192, 2], P(('dp', 'expert')), may hold values from 0.25 to 1
- grad_out: bfloat16 [8192, 768], P(('dp', 'expert'), 'hidden'), may hold values from -6 to 6
- w_ada: bfloat16 [768, 6, 768], P(None, None, 'hidden'), may hold values from -0.21875 to 0.21875
- w_qkv: bfloat16 [768, 3, 768], P(None, None, 'hidden'), may hold values from -0.21875 to 0.21875
- w_out: bfloat16 [768, 768], P('hidden'), may hold values from -1.25 to 1.25
- w_shared_in: bfloat16 [768, 3072], P(None, 'hidden'), may hold values from -0.21875 to 0.21875
- w_shared_out: bfloat16 [3072, 768], P('hidden'), may hold values from -0.109375 to 0.109375
- w_expert_in: bfloat16 [8, 768, 3072], P('expert', None, 'hidden'), may hold values from -0.21875 to 0.21875
- w_expert_out: bfloat16 [8, 3072, 768], P('expert', 'hidden'), may hold values from -0.109375 to 0.109375
Outputs:
- block_out: bfloat16 [8192, 768], P(('dp', 'expert'), 'hidden')
- grad_patches: bfloat16 [8192, 768], P(('dp', 'expert'), 'hidden')
- grad_ada: float32 [768, 6, 768], P(('dp', 'expert'), None, 'hidden')
- grad_qkv: float32 [768, 3, 768], P(('dp', 'expert'), None, 'hidden')
- grad_proj: float32 [768, 768], P('hidden', ('dp', 'expert'))
- grad_shared_in: float32 [768, 3072], P(('dp', 'expert'), 'hidden')
- grad_shared_out: float32 [3072, 768], P('hidden', ('dp', 'expert'))
- grad_expert_in: float32 [8, 768, 3072], P('expert', 'dp', 'hidden')
- grad_expert_out: float32 [8, 3072, 768], P('expert', 'hidden', 'dp')
The draws below stay inside these ranges and needn't reach their ends.
Inputs may be any that keep to these rules, and one draw needn't show every extreme that they name: `routes`: within the rows of one device group no expert is named by more than 384 patches, a bound that some block reaches of them. `seg_ids`: along a row the segment number never falls; a segment has 1 to 64 patches. `seg_image`: A value names one of the 32 conditioning vectors of the same device group.
All inputs are finite; a program needn't handle non-finite values.
Results may differ from the reference program's by a relative error of at most 0.014.
The reference program's roundings to bfloat16 on the way count: a program that leaves them out, or rounds other values in their place, can miss the bound.
Values may be sent and summed in bfloat16 or wider, within the bound.
No kernel may reach another device: no remote copies, remote signals or barrier semaphores. Data moves between devices by JAX's collectives and lax.ppermute only.
A program may use at most 256 MiB of HBM per device.

```python
import math
import jax
import jax.numpy as jnp
import numpy as np
from jax import lax

D = 768
HEADS = 12
HEAD_DIM = 64
FF = 3072
SEQ_LEN = 256
SEGS = 8
SEQ_DEV = 4
TOK_DEV = 1024
CAP = 384
IMG_DEV = 32
SEG_MOST = 64
EXPERTS = 8
TOKENS = 8192
SEQS = 32
IMAGES = 256
N_DP = 4
N_EXPERT = 2


def place_ends(entries, key, least, top_value):
    shape = entries.shape
    place = [jax.random.randint(jax.random.fold_in(key, axis), (), 0, shape[axis]) for axis in range(len(shape))]
    entries = entries.at[tuple(place)].set(least)
    longest = shape.index(max(shape))
    place[longest] = (place[longest] + 1) % shape[longest]
    return entries.at[tuple(place)].set(top_value)


def levels(key, dims, shards, low, largest):
    def one(position, shards_of):
        heights = jax.random.uniform(jax.random.fold_in(jax.random.fold_in(key, 6), position), (shards_of,), jnp.float32, low / len(shards), largest / len(shards))
        return jnp.repeat(jnp.exp(heights), dims[position] // shards_of).reshape((-1,) + (1,) * (len(dims) - position - 1))

    loudness = one(*shards[0])
    for cut in shards[1:]:
        loudness = loudness * one(*cut)
    return loudness


def profile(count, total, most, lean):
    weights = [(1 << 20) // math.isqrt(standing ** lean) + 1 for standing in range(2, count + 1)]
    rest, given = total - most - (count - 1), [1] * (count - 1)
    while rest > 0:
        free = [i for i in range(count - 1) if given[i] < most]
        whole, budget = sum([weights[i] for i in free]), rest
        for i in free:
            more = min(most - given[i], max(1, budget * weights[i] // whole), rest)
            given[i] = given[i] + more
            rest = rest - more
    return np.array([most] + given)


def uneven(own_key, amount, total, most, slope):
    if amount == 2:
        one = jax.random.randint(own_key, (), max(1, total - most), min(most, total - 1) + 1)
        return jnp.stack([one, total - one])
    lengths = jnp.asarray(profile(amount, total, most, slope), jnp.int32)
    pairs = (amount - 1) // 2
    giver, taker = lengths[1:1 + 2 * pairs:2], lengths[2:2 + 2 * pairs:2]
    slack = jnp.minimum(giver - 1, most - taker)
    passed = jax.random.randint(jax.random.fold_in(own_key, 1), (pairs,), 0, 1 << 20) % (slack + 1)
    lengths = lengths.at[1:1 + 2 * pairs:2].set(giver - passed).at[2:2 + 2 * pairs:2].set(taker + passed)
    return lengths[jax.random.permutation(jax.random.fold_in(own_key, 2), amount)]


def deal_out(key, own, number, rows, count, top, limit, slope):
    ranking = jax.random.permutation(key, count)
    crowded, usual = load_shares(count, rows * top, limit, slope, True), load_shares(count, rows * top, limit, slope, False)
    places = jnp.arange(count)

    def named(sizes, turn):
        used = int((sizes > 0).sum())
        fixed = max(1, used // 4)
        moved = fixed + (places - fixed + turn * (used - fixed)) % max(1, count - fixed)
        return jnp.zeros((count,), jnp.int32).at[ranking[jnp.where(places < fixed, places, moved)]].set(jnp.asarray(sizes, jnp.int32))

    sizes = jnp.where(number % 4 == 0, named(crowded, number // 4), named(usual, number - number // 4 - 1))
    mixed = jax.random.permutation(jax.random.fold_in(own, 3), count)
    donor, sink = mixed[0:count // 2 * 2:2], mixed[1:count // 2 * 2:2]
    room = jnp.minimum(sizes[donor] - 1, limit - sizes[sink]) // 2
    room = jnp.where((donor == ranking[0]) | (sink == ranking[0]) | (sizes[sink] == 0), 0, jnp.maximum(room, 0))
    moved = jax.random.randint(jax.random.fold_in(own, 4), (count // 2,), 0, 1 << 20) % (room + 1)
    sizes = sizes.at[donor].add(-moved).at[sink].add(moved)
    members = jnp.searchsorted(jnp.cumsum(sizes), jnp.arange(rows * top), side="right").astype(jnp.int32)
    table = members.reshape(top, rows).T
    table = table[jax.random.permutation(jax.random.fold_in(own, 1), rows)]
    turn = jax.random.randint(jax.random.fold_in(own, 2), (rows, 1), 0, top)
    return jnp.take_along_axis(table, (jnp.arange(top)[None, :] + turn) % top, axis=1)


def load_shares(number_of, total, bound, slope, full):
    loads = [(1 << 20) // math.isqrt(rank ** slope) + 1 for rank in range(1, number_of + 1)]
    largest = bound if full else min(bound, max(-(-total // number_of), total * loads[0] // sum(loads)))
    least = 1 if total - largest >= number_of - 1 else 0
    holding, spare = [largest] + [least] * (number_of - 1), total - largest - least * (number_of - 1)
    while spare > 0:
        candidates = [i for i in range(1, number_of) if holding[i] < largest] or [i for i in range(1, number_of) if holding[i] < bound]
        whole, remaining = sum([loads[i] for i in candidates]), spare
        for i in candidates:
            addition = min(bound - holding[i], max(1, remaining * loads[i] // whole), spare)
            holding[i] = holding[i] + addition
            spare = spare - addition
    return np.array(holding)


def scatter_about(key, extent, width, reach, shards=(), held_as=jnp.bfloat16):
    values = width * jax.random.normal(key, extent, jnp.float32)
    if shards:
        values = values * levels(key, extent, shards, -0.22, 0.18)
    return jnp.clip(values, -reach, reach).astype(held_as)


def setup_inputs(seed: int = 0) -> dict:
    key_of = jax.random.split(jax.random.key(seed), 15)
    patches = scatter_about(key_of[0], (TOKENS, D), 1.0, 6.0, ((0, 8), (1, 4)))
    cond = scatter_about(key_of[1], (IMAGES, D), 1.0, 6.0, ((0, 8),))
    seg_ids = jax.vmap(lambda own: jnp.searchsorted(jnp.cumsum(uneven(own, SEGS, SEQ_LEN, SEG_MOST, 1)), jnp.arange(SEQ_LEN), side="right"))(jax.random.split(key_of[2], SEQS)).reshape((SEQS, SEQ_LEN)).astype(jnp.int32)
    seg_image = place_ends(jax.random.randint(key_of[3], (SEQS, SEGS), 0, IMG_DEV), jax.random.fold_in(key_of[3], 1), 0, IMG_DEV - 1).astype(jnp.int32)
    routes_keys = jax.random.split(jax.random.fold_in(key_of[4], 1), TOKENS // TOK_DEV)
    routes_turns = jax.random.permutation(jax.random.fold_in(key_of[4], 3), TOKENS // TOK_DEV)
    routes = jax.vmap(lambda own, number: deal_out(jax.random.fold_in(key_of[4], 2), own, number, TOK_DEV, EXPERTS, 2, CAP, 1))(routes_keys, routes_turns).reshape((TOKENS, 2))
    gates = jnp.clip(0.25 + 0.75 * jax.random.uniform(key_of[5], (TOKENS, 2), jnp.float32) ** levels(key_of[5], (TOKENS, 2), ((0, 8),), -0.2, 0.2), 0.25, 1.0)
    grad_out = scatter_about(key_of[6], (TOKENS, D), 1.0, 6.0, ((0, 8), (1, 4)))
    w_ada = scatter_about(key_of[7], (D, 6, D), D ** -0.5, 0.21875, ((2, 4),))
    w_qkv = scatter_about(key_of[8], (D, 3, D), D ** -0.5, 0.21875, ((2, 4),))
    w_out = scatter_about(key_of[9], (D, D), (D // 32) ** -0.5, 1.25, ((0, 4),))
    w_shared_in = scatter_about(key_of[10], (D, FF), D ** -0.5, 0.21875, ((1, 4),))
    w_shared_out = scatter_about(key_of[11], (FF, D), FF ** -0.5, 0.109375, ((0, 4),))
    w_expert_in = scatter_about(key_of[12], (EXPERTS, D, FF), D ** -0.5, 0.21875, ((0, 2), (2, 4)))
    w_expert_out = scatter_about(key_of[13], (EXPERTS, FF, D), FF ** -0.5, 0.109375, ((0, 2), (1, 4)))
    return {"patches": patches, "cond": cond, "seg_ids": seg_ids, "seg_image": seg_image, "routes": routes, "gates": gates, "grad_out": grad_out, "w_ada": w_ada, "w_qkv": w_qkv, "w_out": w_out, "w_shared_in": w_shared_in, "w_shared_out": w_shared_out, "w_expert_in": w_expert_in, "w_expert_out": w_expert_out}


EPSILON = 1e-06
NEG_FILL = -1e+30

@jax.custom_vjp
def low(v):
    return lax.optimization_barrier(v.astype(jnp.bfloat16)).astype(jnp.float32)

@jax.custom_vjp
def low_back(v):
    return v

def low_keep(v):
    return (low(v), None)

def low_pass(kept, grad):
    return (grad,)

def back_keep(v):
    return (v, None)

def back_low(kept, grad):
    return (low(grad),)
low.defvjp(low_keep, low_pass)
low_back.defvjp(back_keep, back_low)

def normalize(values):
    centre = values - lax.optimization_barrier(jnp.mean(values, axis=-1, keepdims=True))
    spread = lax.rsqrt(lax.optimization_barrier(jnp.mean(centre * centre, axis=-1, keepdims=True)) + EPSILON)
    return centre * spread

def gelu_tanh(values):
    return jax.nn.gelu(values, approximate=True)

def block_step(weight_set, stream, cond_block, seg_block, image_block, route_block, gate_block):
    w_ada, w_qkv, w_out, w_shared_in, w_shared_out, w_expert_in, w_expert_out = weight_set
    highest = lax.Precision.HIGHEST
    silu_cond = low(jax.nn.silu(cond_block))
    modulation = low(low_back(jnp.einsum('id,dkc->ikc', silu_cond, w_ada, precision=highest)))
    seg_flat = seg_block.reshape(TOK_DEV)
    row_of = jnp.arange(TOK_DEV, dtype=jnp.int32) // SEQ_LEN
    tok_image = image_block[row_of, seg_flat]
    per_token = modulation[tok_image]
    shift_attn = per_token[:, 0]
    scale_attn = per_token[:, 1]
    gate_attn = per_token[:, 2]
    shift_mlp = per_token[:, 3]
    scale_mlp = per_token[:, 4]
    gate_mlp = per_token[:, 5]
    normed_one = low(normalize(stream) * (1.0 + scale_attn) + shift_attn)
    qkv_all = low(low_back(jnp.dot(normed_one, w_qkv.reshape(D, 3 * D), precision=highest)))
    qkv_heads = qkv_all.reshape(SEQ_DEV, SEQ_LEN, 3, HEADS, HEAD_DIM)
    queries = qkv_heads[:, :, 0]
    key_rows = qkv_heads[:, :, 1]
    value_rows = qkv_heads[:, :, 2]
    score_scale = HEAD_DIM ** (-0.5)
    scores = low_back(jnp.einsum('sqhd,skhd->shqk', queries, key_rows, precision=highest) * score_scale)
    same_image = (seg_block[:, :, None] == seg_block[:, None, :])[:, None]
    scores = jnp.where(same_image, scores, NEG_FILL)
    shifted = scores - lax.optimization_barrier(jnp.max(scores, axis=-1, keepdims=True))
    exp_scores = jnp.exp(shifted)
    probs = exp_scores / lax.optimization_barrier(jnp.sum(exp_scores, axis=-1, keepdims=True))
    context = low(low_back(jnp.einsum('shqk,skhd->sqhd', low(probs), value_rows, precision=highest)))
    context = context.reshape(TOK_DEV, D)
    attn_full = low_back(jnp.dot(context, w_out, precision=highest))
    mid_stream = stream + gate_attn * attn_full
    normed_two = low(normalize(mid_stream) * (1.0 + scale_mlp) + shift_mlp)
    shared_pre = low_back(jnp.dot(normed_two, w_shared_in, precision=highest))
    shared_out = low_back(jnp.dot(low(gelu_tanh(shared_pre)), w_shared_out, precision=highest))
    flat_route = route_block.reshape(2 * TOK_DEV)
    route_hot = (flat_route[:, None] == jnp.arange(EXPERTS, dtype=jnp.int32)[None, :]).astype(jnp.int32)
    slot_index = lax.optimization_barrier(jnp.sum((jnp.cumsum(route_hot, axis=0) - 1) * route_hot, axis=1)).astype(jnp.int32)
    target = (flat_route * CAP + slot_index).astype(jnp.int32)
    entry_of = jnp.full((EXPERTS * CAP,), 2 * TOK_DEV, jnp.int32).at[target].set(jnp.arange(2 * TOK_DEV, dtype=jnp.int32))
    padded_rows = jnp.concatenate([normed_two, jnp.zeros((1, D), normed_two.dtype)], axis=0)
    slot_rows = padded_rows[entry_of // 2].reshape(EXPERTS, CAP, D)
    expert_pre = low_back(jnp.einsum('ecd,edf->ecf', slot_rows, w_expert_in, precision=highest))
    expert_res = low_back(jnp.einsum('ecf,efd->ecd', low(gelu_tanh(expert_pre)), w_expert_out, precision=highest))
    picked = expert_res.reshape(EXPERTS * CAP, D)[target].reshape(TOK_DEV, 2, D)
    mixed = lax.optimization_barrier(jnp.sum(picked * gate_block[:, :, None], axis=1))
    mlp = shared_out + mixed
    return mid_stream + gate_mlp * mlp

def reference(patches, cond, seg_ids, seg_image, routes, gates, grad_out, w_ada, w_qkv, w_out, w_shared_in, w_shared_out, w_expert_in, w_expert_out):
    block_count = N_DP * N_EXPERT
    weight_set = tuple((weight_arg.astype(jnp.float32) for weight_arg in (w_ada, w_qkv, w_out, w_shared_in, w_shared_out, w_expert_in, w_expert_out)))
    streams = patches.astype(jnp.float32).reshape(block_count, TOK_DEV, D)
    extras = (cond.astype(jnp.float32).reshape(block_count, IMG_DEV, D), seg_ids.reshape(block_count, SEQ_DEV, SEQ_LEN), seg_image.reshape(block_count, SEQ_DEV, SEGS), routes.reshape(block_count, TOK_DEV, 2), gates.astype(jnp.float32).reshape(block_count, TOK_DEV, 2))
    saved_step = jax.checkpoint(block_step)

    def forward(stream_all, weights_now):

        def visit(carry, items):
            return (carry, saved_step(weights_now, items[0], items[1], items[2], items[3], items[4], items[5]))
        unused, outputs = lax.scan(visit, jnp.zeros((), jnp.float32), (stream_all,) + extras)
        return outputs
    result, pullback = jax.vjp(forward, streams, weight_set)
    grad_stream, grad_weights = pullback(grad_out.astype(jnp.float32).reshape(block_count, TOK_DEV, D))
    return (result.reshape(TOKENS, D).astype(jnp.bfloat16), grad_stream.reshape(TOKENS, D).astype(jnp.bfloat16), grad_weights[0], grad_weights[1], grad_weights[2], grad_weights[3], grad_weights[4], grad_weights[5], grad_weights[6])
```

```python
import jax
import jax.numpy as jnp
from jax import lax
from jax.experimental import pallas as pl
from jax.experimental.pallas import tpu as pltpu
from jax.sharding import PartitionSpec as P

D = 768
HEAD_DIM = 64
EXP_DEV = 4
CAP = 384
EPSILON = 1e-06
NEG_FILL = -1e30
BF = jnp.bfloat16
F32 = jnp.float32
GELU_C = 0.7978845608028654
GELU_A = 0.044715


def kernel_params():
    return pltpu.CompilerParams(vmem_limit_bytes=60 * 1024 * 1024)


def dot(a, b, lhs=1, rhs=0):
    return lax.dot_general(a, b, (((lhs,), (rhs,)), ((), ())), preferred_element_type=F32)


def gelu_pair(values):
    square = values * values
    inner = GELU_C * values * (1.0 + GELU_A * square)
    bent = jnp.tanh(inner)
    half = 0.5 * (1.0 + bent)
    slope = half + (0.5 * values) * (1.0 - bent * bent) * (GELU_C * (1.0 + (3.0 * GELU_A) * square))
    return values * half, slope


def normalize(values):
    centre = values - jnp.mean(values, axis=-1, keepdims=True)
    spread = lax.rsqrt(jnp.mean(centre * centre, axis=-1, keepdims=True) + EPSILON)
    return centre * spread, spread


def norm_back(upstream, unit, spread):
    return spread * (
        upstream
        - jnp.mean(upstream, axis=-1, keepdims=True)
        - unit * jnp.mean(upstream * unit, axis=-1, keepdims=True)
    )


def image_hot(image_col, count):
    lanes = lax.broadcasted_iota(jnp.int32, (image_col.shape[0], count), 1)
    return (image_col == lanes).astype(BF)


def probs_of(queries, keys, same):
    scores = dot(queries, keys, 1, 1) * (HEAD_DIM ** -0.5)
    scores = jnp.where(same, scores, NEG_FILL)
    raised = jnp.exp(scores - jnp.max(scores, axis=-1, keepdims=True))
    return raised * (1.0 / jnp.sum(raised, axis=-1, keepdims=True))


def attn_fwd_kernel(
    x_ref, img_ref, mod_ref, segc_ref, segr_ref, w_ref,
    n1_ref, qkv_ref, ctx_ref, attn_ref, mid_ref, n2_ref,
):
    step = pl.program_id(0)
    feat = ctx_ref.shape[2]
    images = mod_ref.shape[0]

    def mod(k):
        return dot(image_hot(img_ref[...], images), mod_ref[:, k * D:(k + 1) * D])

    @pl.when(step == 0)
    def _():
        unit, _ = normalize(x_ref[...].astype(F32))
        n1_ref[...] = (unit * (1.0 + mod(1)) + mod(0)).astype(BF)
        attn_ref[...] = jnp.zeros_like(attn_ref)

    qkv = dot(n1_ref[...], w_ref[0, :, : 3 * feat]).astype(BF)
    qkv_ref[0] = qkv
    same = segc_ref[...] == segr_ref[...]
    parts = []
    for a in range(feat // HEAD_DIM):
        lo = a * HEAD_DIM
        probs = probs_of(qkv[:, lo:lo + HEAD_DIM], qkv[:, feat + lo:feat + lo + HEAD_DIM], same)
        parts.append(dot(probs.astype(BF), qkv[:, 2 * feat + lo:2 * feat + lo + HEAD_DIM]).astype(BF))
    context = jnp.concatenate(parts, axis=1)
    ctx_ref[0] = context
    attn_ref[...] += dot(context, w_ref[0, :, 3 * feat:], 1, 1)

    @pl.when(step == pl.num_programs(0) - 1)
    def _():
        mid = x_ref[...].astype(F32) + mod(2) * attn_ref[...]
        mid_ref[...] = mid
        unit, _ = normalize(mid)
        n2_ref[...] = (unit * (1.0 + mod(4)) + mod(3)).astype(BF)


def fixed(*shape):
    return pl.BlockSpec(shape, lambda m: (0,) * len(shape))


def stepped(*shape):
    return pl.BlockSpec((1,) + shape, lambda m: (m,) + (0,) * len(shape))


def attn_forward(x_rows, img_col, mod, seg_col, seg_row, weights):
    rows = x_rows.shape[0]
    parts = weights.shape[0]
    feat = D // parts
    return pl.pallas_call(
        attn_fwd_kernel,
        grid=(parts,),
        in_specs=[
            fixed(rows, D), fixed(rows, 1), fixed(*mod.shape), fixed(rows, 1), fixed(1, rows),
            stepped(D, 4 * feat),
        ],
        out_specs=[
            fixed(rows, D), stepped(rows, 3 * feat), stepped(rows, feat),
            fixed(rows, D), fixed(rows, D), fixed(rows, D),
        ],
        out_shape=[
            jax.ShapeDtypeStruct((rows, D), BF),
            jax.ShapeDtypeStruct((parts, rows, 3 * feat), BF),
            jax.ShapeDtypeStruct((parts, rows, feat), BF),
            jax.ShapeDtypeStruct((rows, D), F32),
            jax.ShapeDtypeStruct((rows, D), F32),
            jax.ShapeDtypeStruct((rows, D), BF),
        ],
        compiler_params=kernel_params(),
        name="attn_fwd",
    )(x_rows, img_col, mod, seg_col, seg_row, weights)


def image_sum(hot, values):
    high = values.astype(BF)
    rest = values - high.astype(F32)
    middle = rest.astype(BF)
    low = (rest - middle.astype(F32)).astype(BF)
    return dot(hot, high, 0, 0) + (dot(hot, middle, 0, 0) + dot(hot, low, 0, 0))


def attn_bwd_kernel(
    gn2_ref, mid_ref, attn_ref, go_ref, x_ref, n1_ref, qkv_ref, ctx_ref, img_ref, mod_ref,
    segc_ref, segr_ref, w_ref,
    grad_ref, gpatch_ref, gmod_ref,
    gmid_ref, gattn_ref, gn1_ref,
):
    step = pl.program_id(0)
    feat = ctx_ref.shape[2]
    images = mod_ref.shape[0]
    scale = HEAD_DIM ** -0.5

    def hot():
        return image_hot(img_ref[...], images)

    def mod(k):
        return dot(hot(), mod_ref[:, k * D:(k + 1) * D])

    @pl.when(step == 0)
    def _():
        unit, spread = normalize(mid_ref[...])
        gn2 = gn2_ref[...]
        gmid = go_ref[...].astype(F32) + norm_back(gn2 * (1.0 + mod(4)), unit, spread)
        gmid_ref[...] = gmid
        gattn_ref[...] = (mod(2) * gmid).astype(BF)
        gmod_ref[2] = image_sum(hot(), gmid * attn_ref[...])
        gmod_ref[3] = image_sum(hot(), gn2)
        gmod_ref[4] = image_sum(hot(), gn2 * unit)
        gn1_ref[...] = jnp.zeros_like(gn1_ref)

    gattn = gattn_ref[...]
    gctx = dot(gattn, w_ref[0, :, 3 * feat:]).astype(BF)
    same = segc_ref[...] == segr_ref[...]
    gq, gk, gv = [], [], []
    for a in range(feat // HEAD_DIM):
        lo = a * HEAD_DIM
        queries = qkv_ref[0, :, lo:lo + HEAD_DIM]
        keys = qkv_ref[0, :, feat + lo:feat + lo + HEAD_DIM]
        values = qkv_ref[0, :, 2 * feat + lo:2 * feat + lo + HEAD_DIM]
        gc = gctx[:, lo:lo + HEAD_DIM]
        probs = probs_of(queries, keys, same)
        gv.append(dot(probs.astype(BF), gc, 0, 0).astype(BF))
        gp = dot(gc, values, 1, 1)
        inner = jnp.sum(probs * gp, axis=-1, keepdims=True)
        gs = (probs * (gp - inner)).astype(BF)
        gq.append((dot(gs, keys) * scale).astype(BF))
        gk.append((dot(gs, queries, 0, 0) * scale).astype(BF))
    grows = jnp.concatenate(gq + gk + gv, axis=1)
    grad_ref[0, :, : 3 * feat] = dot(n1_ref[...], grows, 0, 0)
    grad_ref[0, :, 3 * feat:] = dot(gattn, ctx_ref[0], 0, 0)
    gn1_ref[...] += dot(grows, w_ref[0, :, : 3 * feat], 1, 1)

    @pl.when(step == pl.num_programs(0) - 1)
    def _():
        unit, spread = normalize(x_ref[...].astype(F32))
        gn1 = gn1_ref[...]
        back = norm_back(gn1 * (1.0 + mod(1)), unit, spread)
        gpatch_ref[...] = (gmid_ref[...] + back).astype(BF)
        gmod_ref[0] = image_sum(hot(), gn1)
        gmod_ref[1] = image_sum(hot(), gn1 * unit)


def attn_backward(gn2, mid, attn, go, x_rows, n1, qkv, ctx, img_col, mod, seg_col, seg_row, weights):
    rows = x_rows.shape[0]
    parts = weights.shape[0]
    feat = D // parts
    images = mod.shape[0]
    whole = fixed(rows, D)
    return pl.pallas_call(
        attn_bwd_kernel,
        grid=(parts,),
        in_specs=[
            whole, whole, whole, whole, whole, whole,
            stepped(rows, 3 * feat), stepped(rows, feat),
            fixed(rows, 1), fixed(*mod.shape), fixed(rows, 1), fixed(1, rows),
            stepped(D, 4 * feat),
        ],
        out_specs=[stepped(D, 4 * feat), whole, fixed(5, images, D)],
        out_shape=[
            jax.ShapeDtypeStruct((parts, D, 4 * feat), F32),
            jax.ShapeDtypeStruct((rows, D), BF),
            jax.ShapeDtypeStruct((5, images, D), F32),
        ],
        scratch_shapes=[
            pltpu.VMEM((rows, D), F32), pltpu.VMEM((rows, D), BF), pltpu.VMEM((rows, D), F32),
        ],
        compiler_params=kernel_params(),
        name="attn_bwd",
    )(gn2, mid, attn, go, x_rows, n1, qkv, ctx, img_col, mod, seg_col, seg_row, weights)


def finish_kernel(mid_ref, mlp_ref, go_ref, img_ref, gate_ref, out_ref, gmod_ref):
    hot = image_hot(img_ref[...], gate_ref.shape[0])
    mlp = mlp_ref[...]
    out_ref[...] = (mid_ref[...] + dot(hot, gate_ref[...]) * mlp).astype(BF)
    gmod_ref[...] = image_sum(hot, go_ref[...].astype(F32) * mlp)


def finish(mid, mlp, go, img_col, gate):
    return pl.pallas_call(
        finish_kernel,
        out_shape=[
            jax.ShapeDtypeStruct(mid.shape, BF),
            jax.ShapeDtypeStruct(gate.shape, F32),
        ],
        compiler_params=kernel_params(),
        name="finish",
    )(mid, mlp, go, img_col, gate)


def store_split(ref, values):
    pieces, rows = ref.shape[0], ref.shape[2]
    for p in range(pieces):
        ref[p, 0] = values[p * rows:(p + 1) * rows].astype(ref.dtype)


def expert_one_kernel(
    pos_ref, gate_ref, img_ref, n2_ref, go_ref, gm_ref, win_ref,
    rows_ref, act_ref, slope_ref, gslot_ref, gw_ref,
):
    local = pl.program_id(0)
    count = pl.num_programs(0)
    tokens = n2_ref.shape[1]
    images = gm_ref.shape[1]

    def block(j, carry):
        where_ = pos_ref[pl.ds(j * count + local, 1), :]
        mask = lax.broadcasted_iota(jnp.int32, (CAP, tokens), 0) == where_
        pick = mask.astype(BF)
        rows = dot(pick, n2_ref[j]).astype(BF)
        slots = pl.ds(pl.multiple_of(j * CAP, CAP), CAP)
        rows_ref[0, slots, :] = rows
        gate = jnp.sum(jnp.where(mask, gate_ref[pl.ds(j * count + local, 1), :], 0.0), axis=1, keepdims=True)
        image = jnp.sum(jnp.where(mask, img_ref[pl.ds(j, 1), :], 0.0), axis=1, keepdims=True)
        hot = image_hot(image.astype(jnp.int32), images)
        grad = dot(hot, gm_ref[j]) * dot(pick, go_ref[j])
        gslot_ref[0, slots, :] = (gate * grad).astype(BF)
        value, slope = gelu_pair(dot(rows, win_ref[0]))
        act_ref[0, slots, :] = value.astype(BF)
        slope_ref[0, slots, :] = slope
        return carry

    lax.fori_loop(0, 2, block, 0)
    store_split(gw_ref, dot(gslot_ref[0], act_ref[0], 0, 0))


def expert_one(pos, gate, img, n2, go, gate_mlp, w_in, pieces):
    tokens = n2.shape[1]
    slots = 2 * CAP
    ff = w_in.shape[2]
    return pl.pallas_call(
        expert_one_kernel,
        grid=(EXP_DEV,),
        in_specs=[
            fixed(2 * EXP_DEV, tokens), fixed(2 * EXP_DEV, tokens), fixed(2, tokens),
            fixed(2, tokens, D), fixed(2, tokens, D), fixed(*gate_mlp.shape), stepped(D, ff),
        ],
        out_specs=[
            stepped(slots, D), stepped(slots, ff), stepped(slots, ff), stepped(slots, D),
            pl.BlockSpec((pieces, 1, D // pieces, ff), lambda m: (0, m, 0, 0)),
        ],
        out_shape=[
            jax.ShapeDtypeStruct((EXP_DEV, slots, D), BF),
            jax.ShapeDtypeStruct((EXP_DEV, slots, ff), BF),
            jax.ShapeDtypeStruct((EXP_DEV, slots, ff), F32),
            jax.ShapeDtypeStruct((EXP_DEV, slots, D), BF),
            jax.ShapeDtypeStruct((pieces, EXP_DEV, D // pieces, ff), BF),
        ],
        compiler_params=kernel_params(),
        name="expert_one",
    )(pos, gate, img, n2, go, gate_mlp, w_in)


def expert_two_kernel(
    pos_ref, gate_ref, rows_ref, act_ref, slope_ref, gslot_ref, win_ref, wout_ref,
    gw_ref, gn_ref, mix_ref, gn_far_ref, mix_far_ref,
    gpre_ref, gn_acc, mix_acc,
):
    local = pl.program_id(0)
    count = pl.num_programs(0)
    tokens = pos_ref.shape[0]
    lanes = lax.broadcasted_iota(jnp.int32, pos_ref.shape, 1)

    @pl.when(local == 0)
    def _():
        for ref in (gn_ref, mix_ref, gn_acc, mix_acc):
            ref[...] = jnp.zeros_like(ref)

    for j, (gn, mix) in enumerate(((gn_ref, mix_ref), (gn_acc, mix_acc))):
        slots = slice(j * CAP, (j + 1) * CAP)
        grad_pre = (slope_ref[0, slots, :] * dot(gslot_ref[0, slots, :], wout_ref[0], 1, 1)).astype(BF)
        gpre_ref[slots, :] = grad_pre
        grad_in = dot(grad_pre, win_ref[0], 1, 1).astype(BF)
        result = dot(act_ref[0, slots, :], wout_ref[0]).astype(BF)
        here = lanes == j * count + local
        where_ = jnp.sum(jnp.where(here, pos_ref[...], 0), axis=1, keepdims=True)
        gate = jnp.sum(jnp.where(here, gate_ref[...], 0.0), axis=1, keepdims=True)
        pick = (lax.broadcasted_iota(jnp.int32, (tokens, CAP), 1) == where_).astype(BF)
        gn[...] += dot(pick, grad_in)
        mix[...] += gate * dot(pick, result)
    store_split(gw_ref, dot(rows_ref[0], gpre_ref[...], 0, 0))

    @pl.when(local == count - 1)
    def _():
        gn_far_ref[...] = gn_acc[...].astype(BF)
        mix_far_ref[...] = mix_acc[...].astype(BF)


def expert_two(pos, gate, rows, act, slope, gslot, w_in, w_out, pieces):
    tokens = pos.shape[0]
    slots = 2 * CAP
    ff = w_in.shape[2]
    whole = fixed(tokens, D)
    return pl.pallas_call(
        expert_two_kernel,
        grid=(EXP_DEV,),
        in_specs=[
            fixed(tokens, 2 * EXP_DEV), fixed(tokens, 2 * EXP_DEV),
            stepped(slots, D), stepped(slots, ff), stepped(slots, ff), stepped(slots, D),
            stepped(D, ff), stepped(ff, D),
        ],
        out_specs=[
            pl.BlockSpec((pieces, 1, D // pieces, ff), lambda m: (0, m, 0, 0)),
            whole, whole, whole, whole,
        ],
        out_shape=[
            jax.ShapeDtypeStruct((pieces, EXP_DEV, D // pieces, ff), BF),
            jax.ShapeDtypeStruct((tokens, D), F32),
            jax.ShapeDtypeStruct((tokens, D), F32),
            jax.ShapeDtypeStruct((tokens, D), BF),
            jax.ShapeDtypeStruct((tokens, D), BF),
        ],
        scratch_shapes=[
            pltpu.VMEM((slots, ff), BF), pltpu.VMEM((tokens, D), F32), pltpu.VMEM((tokens, D), F32),
        ],
        compiler_params=kernel_params(),
        name="expert_two",
    )(pos, gate, rows, act, slope, gslot, w_in, w_out)


def shared_kernel(
    n2_ref, go_ref, img_ref, gm_ref, win_ref, wout_ref,
    out_ref, gn_ref, gw_ref,
    act_ref, gs_ref, gpre_ref,
):
    step = pl.program_id(0)
    rows, ff = n2_ref.shape[0] // pl.num_programs(0), win_ref.shape[1]
    here = pl.ds(pl.multiple_of(step * rows, rows), rows)
    value, slope = gelu_pair(dot(n2_ref[here, :], win_ref[...]))
    act = value.astype(BF)
    act_ref[here, :] = act
    out_ref[...] = dot(act, wout_ref[...])
    gate = dot(image_hot(img_ref[...], gm_ref.shape[0]), gm_ref[...])
    grad = (gate * go_ref[...].astype(F32)).astype(BF)
    gs_ref[here, :] = grad
    gpre = (slope * dot(grad, wout_ref[...], 1, 1)).astype(BF)
    gpre_ref[here, :] = gpre
    gn_ref[...] = dot(gpre, win_ref[...], 1, 1)

    @pl.when(step == pl.num_programs(0) - 1)
    def _():
        gw_ref[:, :ff] = dot(n2_ref[...], gpre_ref[...], 0, 0)
        gw_ref[:, ff:] = dot(gs_ref[...], act_ref[...], 0, 0)


def shared_both(n2, go, img_col, gate_mlp, w_in, w_out, steps):
    tokens = n2.shape[0]
    rows = tokens // steps
    ff = w_in.shape[1]
    moving = pl.BlockSpec((rows, D), lambda m: (m, 0))
    return pl.pallas_call(
        shared_kernel,
        grid=(steps,),
        in_specs=[
            fixed(tokens, D), moving, pl.BlockSpec((rows, 1), lambda m: (m, 0)),
            fixed(*gate_mlp.shape), fixed(D, ff), fixed(ff, D),
        ],
        out_specs=[moving, moving, fixed(D, 2 * ff)],
        out_shape=[
            jax.ShapeDtypeStruct((tokens, D), F32),
            jax.ShapeDtypeStruct((tokens, D), F32),
            jax.ShapeDtypeStruct((D, 2 * ff), F32),
        ],
        scratch_shapes=[
            pltpu.VMEM((tokens, ff), BF), pltpu.VMEM((tokens, D), BF), pltpu.VMEM((tokens, ff), BF),
        ],
        compiler_params=kernel_params(),
        name="shared_both",
    )(n2, go, img_col, gate_mlp, w_in, w_out)


def on_device(
    patches, cond, seg_ids, seg_image, routes, gates, grad_out,
    w_ada, w_qkv, w_out, w_shared_in, w_shared_out, w_expert_in, w_expert_out,
):
    tokens, feat = patches.shape
    parts = D // feat
    rows = tokens // parts
    image_count = cond.shape[0]
    seq_length = seg_ids.shape[1]
    pieces = lax.axis_size("dp")
    me = lax.axis_index("hidden")
    core = lax.axis_index("expert")
    bit_low = (me & 1) == 1
    bit_high = (me & 2) == 2

    def turned(items):
        a, b, c, d = items
        a, b = jnp.where(bit_low, b, a), jnp.where(bit_low, a, b)
        c, d = jnp.where(bit_low, d, c), jnp.where(bit_low, c, d)
        return [
            jnp.where(bit_high, c, a), jnp.where(bit_high, d, b),
            jnp.where(bit_high, a, c), jnp.where(bit_high, b, d),
        ]

    def across(value, mask):
        return lax.ppermute(value, "hidden", [(i, i ^ mask) for i in range(parts)])

    def other_core(value):
        return lax.ppermute(value, "expert", [(0, 1), (1, 0)])

    def exchanged(items):
        return [items[0]] + [across(items[m], m) for m in range(1, parts)]

    def gathered(value):
        return [value] + [across(value, m) for m in range(1, parts)]

    def blocks(value):
        return [value[i * rows:(i + 1) * rows] for i in range(parts)]

    def to_rows(value):
        return jnp.concatenate(turned(exchanged(turned(blocks(value)))), axis=1)

    def to_cols(value):
        cuts = [value[:, i * feat:(i + 1) * feat] for i in range(parts)]
        return jnp.concatenate(turned(exchanged(turned(cuts))), axis=0)

    packed = jnp.concatenate([w_qkv.reshape(D, 3 * feat), w_out.T], axis=1)
    half = lax.dynamic_slice_in_dim(packed, core * (D // 2), D // 2, axis=0)
    shards = [packed]
    for m in range(1, parts):
        mine = across(half, m)
        theirs = other_core(mine)
        first = core == 0
        shards.append(
            jnp.concatenate([jnp.where(first, mine, theirs), jnp.where(first, theirs, mine)], axis=0)
        )
    weights = jnp.stack(shards)

    x_rows = to_rows(patches)
    silu_cond = jax.nn.silu(cond.astype(F32)).astype(BF)
    mod_own = jnp.einsum("id,dkc->ikc", silu_cond, w_ada, preferred_element_type=F32).astype(BF)
    mod = jnp.concatenate(turned(gathered(mod_own)), axis=2).reshape(image_count, 6 * D)
    gate_own = mod[:, 5 * D:]
    gate_both = jnp.stack([gate_own, other_core(gate_own)])
    go_rows = to_rows(grad_out)
    go_own = jnp.concatenate(gathered(go_rows), axis=0)
    go_both = jnp.stack([go_own, other_core(go_own)])

    seg_turned = jnp.concatenate(turned(jnp.split(seg_ids, parts, axis=0)), axis=0)
    image_turned = jnp.concatenate(turned(jnp.split(seg_image, parts, axis=0)), axis=0)
    seg_hot = seg_turned[:, :, None] == jnp.arange(seg_image.shape[1], dtype=jnp.int32)
    tok_image = jnp.sum(jnp.where(seg_hot, image_turned[:, None, :], 0), axis=2).reshape(tokens)
    routes_turned = jnp.concatenate(turned(blocks(routes)), axis=0).T
    gates_turned = jnp.concatenate(turned(blocks(gates)), axis=0).T
    expert_ids = jnp.arange(2 * EXP_DEV, dtype=jnp.int32)[:, None]
    named = [routes_turned[k][None, :] == expert_ids for k in range(2)]
    hot = named[0] | named[1]
    slot = jnp.cumsum(hot.astype(jnp.int32), axis=1) - 1
    pos_all = jnp.where(hot, slot, -1)
    gate_all = jnp.where(named[0], gates_turned[0][None], jnp.where(named[1], gates_turned[1][None], 0.0))

    def for_experts(table):
        low, high = table[:EXP_DEV], table[EXP_DEV:]
        mine = jnp.where(core == 0, low, high)
        away = jnp.where(core == 0, high, low)
        return mine, away

    pos_mine, pos_away = for_experts(pos_all.astype(F32))
    gate_mine, gate_away = for_experts(gate_all)
    meta = other_core(jnp.concatenate([pos_away, gate_away, tok_image.astype(F32)[None]], axis=0))
    pos = jnp.concatenate([pos_mine, meta[:EXP_DEV]], axis=0).astype(jnp.int32)
    gate_rows = jnp.concatenate([gate_mine, meta[EXP_DEV:2 * EXP_DEV]], axis=0)
    img_rows = jnp.stack([tok_image.astype(F32), meta[2 * EXP_DEV]])
    img_col = tok_image[:, None]
    img_own = img_col[:rows]
    seg_row = seg_turned[:1]
    seg_col = seg_row.reshape(rows, 1)

    n1, qkv, ctx, attn, mid, n2 = attn_forward(x_rows, img_own, mod, seg_col, seg_row, weights)
    n2_own = jnp.concatenate(gathered(n2), axis=0)
    n2_both = jnp.stack([n2_own, other_core(n2_own)])

    slot_rows, act, slope, gslot, gw_out = expert_one(
        pos, gate_rows, img_rows, n2_both, go_both, gate_both, w_expert_in, pieces
    )
    grad_expert_out = lax.psum_scatter(gw_out, "dp", scatter_dimension=0, tiled=False)
    gw_in, gn_near, mix_near, gn_far, mix_far = expert_two(
        pos.T, gate_rows.T, slot_rows, act, slope, gslot, w_expert_in, w_expert_out, pieces
    )
    grad_expert_in = lax.psum_scatter(gw_in, "dp", scatter_dimension=0, tiled=False)
    shared_out, gn_shared, gw_shared = shared_both(
        n2_own, go_own, img_col, gate_own, w_shared_in, w_shared_out, parts
    )

    def row_total(near, far, extra):
        total = near + extra + other_core(far).astype(F32)
        cut = blocks(total)
        out = cut[0]
        for m in range(1, parts):
            out = out + across(cut[m].astype(BF), m).astype(F32)
        return out

    gn2 = row_total(gn_near, gn_far, gn_shared)
    mlp = row_total(mix_near, mix_far, shared_out)

    def core_half(values):
        shape = values.shape[:-2]
        cut = values.reshape(shape + (pieces, 2, D // (2 * pieces), values.shape[-1]))
        low, high = cut[..., 0, :, :], cut[..., 1, :, :]
        return jnp.where(core == 0, low, high) + other_core(jnp.where(core == 0, high, low))

    def over_dp(values):
        return lax.psum_scatter(values.astype(BF), "dp", scatter_dimension=0, tiled=False).astype(F32)

    grad_shared = over_dp(core_half(gw_shared))
    gw_attn, gpatch, gmod_five = attn_backward(
        gn2, mid, attn, go_rows, x_rows, n1, qkv, ctx, img_own, mod, seg_col, seg_row, weights
    )
    out_rows, gmod_last = finish(mid, mlp, go_rows, img_own, gate_own)
    block_out = to_cols(out_rows)
    grad_patches = to_cols(gpatch)

    gmod = jnp.concatenate([gmod_five, gmod_last[None]], axis=0)
    cuts = turned([gmod[:, :, i * feat:(i + 1) * feat] for i in range(parts)])
    got = exchanged(cuts)
    grad_image = (got[0] + got[1] + got[2] + got[3]).astype(BF)
    everyone = ("dp", "expert")
    silu_all = lax.all_gather(silu_cond, everyone, axis=0, tiled=True)
    image_all = lax.all_gather(grad_image, everyone, axis=0, tiled=False)
    ada_rows = D // (2 * pieces)
    place = lax.axis_index("dp") * 2 + core
    silu_mine = lax.dynamic_slice_in_dim(silu_all, place * ada_rows, ada_rows, axis=1)
    grad_ada = jnp.einsum(
        "gid,gkic->dkc",
        silu_mine.reshape(2 * pieces, image_count, ada_rows),
        image_all,
        preferred_element_type=F32,
    )

    attn_half = core_half(gw_attn)
    attn_sum = attn_half[0]
    for m in range(1, parts):
        attn_sum = attn_sum + across(attn_half[m].astype(BF), m).astype(F32)
    grad_attn = over_dp(attn_sum)
    ff = w_shared_in.shape[1]
    return (
        block_out,
        grad_patches,
        grad_ada,
        grad_attn[:, : 3 * feat].reshape(ada_rows, 3, feat),
        grad_attn[:, 3 * feat:].T,
        grad_shared[:, :ff],
        grad_shared[:, ff:].T,
        grad_expert_in.astype(F32),
        jnp.swapaxes(grad_expert_out.astype(F32), 1, 2),
    )


def solution(mesh):
    rows = P(("dp", "expert"), None)
    tiles = P(("dp", "expert"), "hidden")
    return jax.shard_map(
        on_device,
        mesh=mesh,
        in_specs=(
            tiles, rows, rows, rows, rows, rows, tiles,
            P(None, None, "hidden"),
            P(None, None, "hidden"),
            P("hidden", None),
            P(None, "hidden"),
            P("hidden", None),
            P("expert", None, "hidden"),
            P("expert", "hidden", None),
        ),
        out_specs=(
            tiles,
            tiles,
            P(("dp", "expert"), None, "hidden"),
            P(("dp", "expert"), None, "hidden"),
            P("hidden", ("dp", "expert")),
            P(("dp", "expert"), "hidden"),
            P("hidden", ("dp", "expert")),
            P("expert", "dp", "hidden"),
            P("expert", "hidden", "dp"),
        ),
        check_vma=False,
    )
```

```python
import functools

import jax
import jax.numpy as jnp
from jax import lax
from jax.experimental import pallas as pl
from jax.experimental.pallas import tpu as pltpu
from jax.sharding import PartitionSpec as P


D = 768
HEAD_DIM = 64
EXP_DEV = 4
CAP = 384
EPSILON = 1e-06
NEG_FILL = -1e30
BF = jnp.bfloat16
F32 = jnp.float32
GELU_C = 0.7978845608028654
GELU_A = 0.044715


def kernel_params():
    return pltpu.CompilerParams(vmem_limit_bytes=60 * 1024 * 1024)


def dot(a, b, lhs=1, rhs=0):
    return lax.dot_general(a, b, (((lhs,), (rhs,)), ((), ())), preferred_element_type=F32)


def gelu_pair(values):
    square = values * values
    inner = GELU_C * values * (1.0 + GELU_A * square)
    bent = jnp.tanh(inner)
    half = 0.5 * (1.0 + bent)
    slope = half + (0.5 * values) * (1.0 - bent * bent) * (GELU_C * (1.0 + (3.0 * GELU_A) * square))
    return values * half, slope


def normalize(values):
    centre = values - jnp.mean(values, axis=-1, keepdims=True)
    spread = lax.rsqrt(jnp.mean(centre * centre, axis=-1, keepdims=True) + EPSILON)
    return centre * spread, spread


def norm_back(upstream, unit, spread):
    return spread * (
        upstream
        - jnp.mean(upstream, axis=-1, keepdims=True)
        - unit * jnp.mean(upstream * unit, axis=-1, keepdims=True)
    )


def image_hot(image_col, count):
    lanes = lax.broadcasted_iota(jnp.int32, (image_col.shape[0], count), 1)
    return (image_col == lanes).astype(BF)


def probs_of(queries, keys, same):
    scores = dot(queries, keys, 1, 1) * (HEAD_DIM ** -0.5)
    scores = jnp.where(same, scores, NEG_FILL)
    raised = jnp.exp(scores - jnp.max(scores, axis=-1, keepdims=True))
    return raised * (1.0 / jnp.sum(raised, axis=-1, keepdims=True))


def attn_fwd_kernel(
    x_ref, img_ref, mod_ref, segc_ref, segr_ref, w_ref,
    n1_ref, qkv_ref, ctx_ref, attn_ref, mid_ref, n2_ref,
):
    step = pl.program_id(0)
    feat = ctx_ref.shape[2]
    images = mod_ref.shape[0]

    def mod(k):
        return dot(image_hot(img_ref[...], images), mod_ref[:, k * D:(k + 1) * D])

    @pl.when(step == 0)
    def _():
        unit, _ = normalize(x_ref[...].astype(F32))
        n1_ref[...] = (unit * (1.0 + mod(1)) + mod(0)).astype(BF)
        attn_ref[...] = jnp.zeros_like(attn_ref)

    qkv = dot(n1_ref[...], w_ref[0, :, : 3 * feat]).astype(BF)
    qkv_ref[0] = qkv
    same = segc_ref[...] == segr_ref[...]
    parts = []
    for a in range(feat // HEAD_DIM):
        lo = a * HEAD_DIM
        probs = probs_of(qkv[:, lo:lo + HEAD_DIM], qkv[:, feat + lo:feat + lo + HEAD_DIM], same)
        parts.append(dot(probs.astype(BF), qkv[:, 2 * feat + lo:2 * feat + lo + HEAD_DIM]).astype(BF))
    context = jnp.concatenate(parts, axis=1)
    ctx_ref[0] = context
    attn_ref[...] += dot(context, w_ref[0, :, 3 * feat:], 1, 1)

    @pl.when(step == pl.num_programs(0) - 1)
    def _():
        mid = x_ref[...].astype(F32) + mod(2) * attn_ref[...]
        mid_ref[...] = mid
        unit, _ = normalize(mid)
        n2_ref[...] = (unit * (1.0 + mod(4)) + mod(3)).astype(BF)


def fixed(*shape):
    return pl.BlockSpec(shape, lambda m: (0,) * len(shape))


def stepped(*shape):
    return pl.BlockSpec((1,) + shape, lambda m: (m,) + (0,) * len(shape))


def attn_forward(x_rows, img_col, mod, seg_col, seg_row, weights):
    rows = x_rows.shape[0]
    parts = weights.shape[0]
    feat = D // parts
    return pl.pallas_call(
        attn_fwd_kernel,
        grid=(parts,),
        in_specs=[
            fixed(rows, D), fixed(rows, 1), fixed(*mod.shape), fixed(rows, 1), fixed(1, rows),
            stepped(D, 4 * feat),
        ],
        out_specs=[
            fixed(rows, D), stepped(rows, 3 * feat), stepped(rows, feat),
            fixed(rows, D), fixed(rows, D), fixed(rows, D),
        ],
        out_shape=[
            jax.ShapeDtypeStruct((rows, D), BF),
            jax.ShapeDtypeStruct((parts, rows, 3 * feat), BF),
            jax.ShapeDtypeStruct((parts, rows, feat), BF),
            jax.ShapeDtypeStruct((rows, D), F32),
            jax.ShapeDtypeStruct((rows, D), F32),
            jax.ShapeDtypeStruct((rows, D), BF),
        ],
        compiler_params=kernel_params(),
        name="attn_fwd",
    )(x_rows, img_col, mod, seg_col, seg_row, weights)


def image_sum(hot, values):
    high = values.astype(BF)
    rest = values - high.astype(F32)
    middle = rest.astype(BF)
    low = (rest - middle.astype(F32)).astype(BF)
    return dot(hot, high, 0, 0) + (dot(hot, middle, 0, 0) + dot(hot, low, 0, 0))


def attn_bwd_kernel(
    gn2_ref, mid_ref, attn_ref, go_ref, x_ref, n1_ref, qkv_ref, ctx_ref, img_ref, mod_ref,
    segc_ref, segr_ref, w_ref, core_ref,
    gpatch_ref, gmod_ref, *rest,
):
    grad_refs, (gmid_ref, gattn_ref, gn1_ref) = rest[:-3], rest[-3:]
    step = pl.program_id(0)
    feat = ctx_ref.shape[2]
    images = mod_ref.shape[0]
    scale = HEAD_DIM ** -0.5

    def hot():
        return image_hot(img_ref[...], images)

    def mod(k):
        return dot(hot(), mod_ref[:, k * D:(k + 1) * D])

    @pl.when(step == 0)
    def _():
        unit, spread = normalize(mid_ref[...])
        gn2 = gn2_ref[...]
        gmid = go_ref[...].astype(F32) + norm_back(gn2 * (1.0 + mod(4)), unit, spread)
        gmid_ref[...] = gmid
        gattn_ref[...] = (mod(2) * gmid).astype(BF)
        gmod_ref[2] = image_sum(hot(), gmid * attn_ref[...])
        gmod_ref[3] = image_sum(hot(), gn2)
        gmod_ref[4] = image_sum(hot(), gn2 * unit)
        gn1_ref[...] = jnp.zeros_like(gn1_ref)

    gattn = gattn_ref[...]
    gctx = dot(gattn, w_ref[0, :, 3 * feat:]).astype(BF)
    same = segc_ref[...] == segr_ref[...]
    gq, gk, gv = [], [], []
    for a in range(feat // HEAD_DIM):
        lo = a * HEAD_DIM
        queries = qkv_ref[0, :, lo:lo + HEAD_DIM]
        keys = qkv_ref[0, :, feat + lo:feat + lo + HEAD_DIM]
        values = qkv_ref[0, :, 2 * feat + lo:2 * feat + lo + HEAD_DIM]
        gc = gctx[:, lo:lo + HEAD_DIM]
        probs = probs_of(queries, keys, same)
        gv.append(dot(probs.astype(BF), gc, 0, 0).astype(BF))
        gp = dot(gc, values, 1, 1)
        inner = jnp.sum(probs * gp, axis=-1, keepdims=True)
        gs = (probs * (gp - inner)).astype(BF)
        gq.append((dot(gs, keys) * scale).astype(BF))
        gk.append((dot(gs, queries, 0, 0) * scale).astype(BF))
    grows = jnp.concatenate(gq + gk + gv, axis=1)
    store_rows(grad_refs, core_ref[0], dot(n1_ref[...], grows, 0, 0), slice(0, 3 * feat))
    store_rows(grad_refs, core_ref[0], dot(gattn, ctx_ref[0], 0, 0), slice(3 * feat, 4 * feat))
    gn1_ref[...] += dot(grows, w_ref[0, :, : 3 * feat], 1, 1)

    @pl.when(step == pl.num_programs(0) - 1)
    def _():
        unit, spread = normalize(x_ref[...].astype(F32))
        gn1 = gn1_ref[...]
        back = norm_back(gn1 * (1.0 + mod(1)), unit, spread)
        gpatch_ref[...] = (gmid_ref[...] + back).astype(BF)
        gmod_ref[0] = image_sum(hot(), gn1)
        gmod_ref[1] = image_sum(hot(), gn1 * unit)


def store_rows(refs, core, values, cols):
    if len(refs) == 1:
        refs[0][0, :, cols] = values
        return
    mine, theirs = refs
    pieces, rows = mine.shape[1], mine.shape[2]
    for p in range(pieces):
        low = values[2 * p * rows:(2 * p + 1) * rows]
        high = values[(2 * p + 1) * rows:(2 * p + 2) * rows]
        mine[0, p, :, cols] = jnp.where(core == 0, low, high)
        theirs[0, p, :, cols] = jnp.where(core == 0, high, low)


def row_specs(parts, pieces, width, index):
    rows = D // (2 * pieces)
    if rows % 8:
        shape = (D, width)
        count = 1
    else:
        shape = (pieces, rows, width)
        count = 2
    spec = pl.BlockSpec((1,) + shape, lambda m: (index(m),) + (0,) * len(shape))
    return [spec] * count, [jax.ShapeDtypeStruct((parts,) + shape, F32)] * count


def smem():
    return pl.BlockSpec(memory_space=pltpu.SMEM)


def hbm():
    return pl.BlockSpec(memory_space=pl.ANY)


def fetch(refs, targets, sems):
    copies = [pltpu.make_async_copy(refs[i], targets[i], sems.at[i]) for i in range(len(refs))]
    for copy in copies:
        copy.start()
    for copy in copies:
        copy.wait()


def attn_backward(core, pieces, gn2, mid, attn, go, x_rows, n1, qkv, ctx, img_col, mod, seg_col, seg_row, weights):
    rows = x_rows.shape[0]
    parts = weights.shape[0]
    feat = D // parts
    images = mod.shape[0]
    whole = fixed(rows, D)
    specs, shapes = row_specs(parts, pieces, 4 * feat, lambda m: m)
    return pl.pallas_call(
        attn_bwd_kernel,
        grid=(parts,),
        in_specs=[
            whole, whole, whole, whole, whole, whole,
            stepped(rows, 3 * feat), stepped(rows, feat),
            fixed(rows, 1), fixed(*mod.shape), fixed(rows, 1), fixed(1, rows),
            stepped(D, 4 * feat), smem(),
        ],
        out_specs=[whole, fixed(5, images, D)] + specs,
        out_shape=[
            jax.ShapeDtypeStruct((rows, D), BF),
            jax.ShapeDtypeStruct((5, images, D), F32),
        ] + shapes,
        scratch_shapes=[
            pltpu.VMEM((rows, D), F32), pltpu.VMEM((rows, D), BF), pltpu.VMEM((rows, D), F32),
        ],
        compiler_params=kernel_params(),
        name="attn_bwd",
    )(gn2, mid, attn, go, x_rows, n1, qkv, ctx, img_col, mod, seg_col, seg_row, weights, core)


def finish_kernel(mid_ref, mlp_ref, go_ref, img_ref, gate_ref, out_ref, gmod_ref):
    hot = image_hot(img_ref[...], gate_ref.shape[0])
    mlp = mlp_ref[...]
    out_ref[...] = (mid_ref[...] + dot(hot, gate_ref[...]) * mlp).astype(BF)
    gmod_ref[...] = image_sum(hot, go_ref[...].astype(F32) * mlp)


def finish(mid, mlp, go, img_col, gate):
    return pl.pallas_call(
        finish_kernel,
        out_shape=[
            jax.ShapeDtypeStruct(mid.shape, BF),
            jax.ShapeDtypeStruct(gate.shape, F32),
        ],
        compiler_params=kernel_params(),
        name="finish",
    )(mid, mlp, go, img_col, gate)


def store_split(ref, values):
    pieces, rows = ref.shape[0], ref.shape[2]
    for p in range(pieces):
        ref[p, 0] = values[p * rows:(p + 1) * rows].astype(ref.dtype)


def expert_one_kernel(pos_ref, gate_ref, img_ref, gm_ref, win_ref, *rest, tiles, first, kept):
    pieces_in, rest = rest[:tiles], rest[tiles + 1 + kept:]
    rows_ref, act_ref, slope_ref, gslot_ref, gw_ref, n2_ref, go_ref, sems = rest
    local = first + pl.program_id(0)
    tokens = n2_ref.shape[1]
    images = gm_ref.shape[1]
    each = tiles // 4
    size = tokens // each

    @pl.when(pl.program_id(0) == 0)
    def _():
        targets = [
            ref.at[j, pl.ds(i * size, size)] for ref in (n2_ref, go_ref) for j in range(2) for i in range(each)
        ]
        fetch(pieces_in, targets, sems)

    def block(j, carry):
        where_ = pos_ref[pl.ds(j * EXP_DEV + local, 1), :]
        mask = lax.broadcasted_iota(jnp.int32, (CAP, tokens), 0) == where_
        pick = mask.astype(BF)
        rows = dot(pick, n2_ref[j]).astype(BF)
        slots = pl.ds(pl.multiple_of(j * CAP, CAP), CAP)
        rows_ref[0, slots, :] = rows
        gate = jnp.sum(jnp.where(mask, gate_ref[pl.ds(j * EXP_DEV + local, 1), :], 0.0), axis=1, keepdims=True)
        image = jnp.sum(jnp.where(mask, img_ref[pl.ds(j, 1), :], 0.0), axis=1, keepdims=True)
        hot = image_hot(image.astype(jnp.int32), images)
        grad = dot(hot, gm_ref[j]) * dot(pick, go_ref[j])
        gslot_ref[0, slots, :] = (gate * grad).astype(BF)
        value, slope = gelu_pair(dot(rows, win_ref[0]))
        act_ref[0, slots, :] = value.astype(BF)
        slope_ref[0, slots, :] = slope
        return carry

    lax.fori_loop(0, 2, block, 0)
    store_split(gw_ref, dot(gslot_ref[0], act_ref[0], 0, 0))


def expert_one(pos, gate, img, gate_mlp, w_in, tiles, after, pieces, first, kept):
    tokens = pos.shape[1]
    slots = 2 * CAP
    ff = w_in.shape[2]
    count = EXP_DEV // 2

    def shifted(*shape):
        return pl.BlockSpec((1,) + shape, lambda m: (m + first,) + (0,) * len(shape))

    fixed_ins = 5
    return pl.pallas_call(
        functools.partial(expert_one_kernel, tiles=len(tiles), first=first, kept=len(kept)),
        grid=(count,),
        in_specs=[
            fixed(2 * EXP_DEV, tokens), fixed(2 * EXP_DEV, tokens), fixed(2, tokens),
            fixed(*gate_mlp.shape), shifted(D, ff),
        ] + [hbm()] * (len(tiles) + 1 + len(kept)),
        out_specs=[
            shifted(slots, D), shifted(slots, ff), shifted(slots, ff), shifted(slots, D),
            pl.BlockSpec((pieces, 1, D // pieces, ff), lambda m: (0, m, 0, 0)),
        ],
        out_shape=[
            jax.ShapeDtypeStruct((EXP_DEV, slots, D), BF),
            jax.ShapeDtypeStruct((EXP_DEV, slots, ff), BF),
            jax.ShapeDtypeStruct((EXP_DEV, slots, ff), F32),
            jax.ShapeDtypeStruct((EXP_DEV, slots, D), BF),
            jax.ShapeDtypeStruct((pieces, count, D // pieces, ff), BF),
        ],
        scratch_shapes=[
            pltpu.VMEM((2, tokens, D), BF), pltpu.VMEM((2, tokens, D), BF),
            pltpu.SemaphoreType.DMA((len(tiles),)),
        ],
        input_output_aliases={fixed_ins + len(tiles) + 1 + i: i for i in range(len(kept))},
        compiler_params=kernel_params(),
        name="expert_one",
    )(pos, gate, img, gate_mlp, w_in, *tiles, after, *kept)


def expert_two_kernel(
    pos_ref, gate_ref, rows_ref, act_ref, slope_ref, gslot_ref, win_ref, wout_ref,
    gw_ref, gn_ref, mix_ref, gn_far_ref, mix_far_ref,
    gpre_ref, gn_acc, mix_acc,
):
    local = pl.program_id(0)
    count = pl.num_programs(0)
    tokens = pos_ref.shape[0]
    lanes = lax.broadcasted_iota(jnp.int32, pos_ref.shape, 1)

    @pl.when(local == 0)
    def _():
        for ref in (gn_ref, mix_ref, gn_acc, mix_acc):
            ref[...] = jnp.zeros_like(ref)

    for j, (gn, mix) in enumerate(((gn_ref, mix_ref), (gn_acc, mix_acc))):
        slots = slice(j * CAP, (j + 1) * CAP)
        grad_pre = (slope_ref[0, slots, :] * dot(gslot_ref[0, slots, :], wout_ref[0], 1, 1)).astype(BF)
        gpre_ref[slots, :] = grad_pre
        grad_in = dot(grad_pre, win_ref[0], 1, 1).astype(BF)
        result = dot(act_ref[0, slots, :], wout_ref[0]).astype(BF)
        here = lanes == j * count + local
        where_ = jnp.sum(jnp.where(here, pos_ref[...], 0), axis=1, keepdims=True)
        gate = jnp.sum(jnp.where(here, gate_ref[...], 0.0), axis=1, keepdims=True)
        pick = (lax.broadcasted_iota(jnp.int32, (tokens, CAP), 1) == where_).astype(BF)
        gn[...] += dot(pick, grad_in)
        mix[...] += gate * dot(pick, result)
    store_split(gw_ref, dot(rows_ref[0], gpre_ref[...], 0, 0))

    @pl.when(local == count - 1)
    def _():
        gn_far_ref[...] = gn_acc[...].astype(BF)
        mix_far_ref[...] = mix_acc[...].astype(BF)


def expert_two(pos, gate, rows, act, slope, gslot, w_in, w_out, pieces):
    tokens = pos.shape[0]
    slots = 2 * CAP
    ff = w_in.shape[2]
    whole = fixed(tokens, D)
    return pl.pallas_call(
        expert_two_kernel,
        grid=(EXP_DEV,),
        in_specs=[
            fixed(tokens, 2 * EXP_DEV), fixed(tokens, 2 * EXP_DEV),
            stepped(slots, D), stepped(slots, ff), stepped(slots, ff), stepped(slots, D),
            stepped(D, ff), stepped(ff, D),
        ],
        out_specs=[
            pl.BlockSpec((pieces, 1, D // pieces, ff), lambda m: (0, m, 0, 0)),
            whole, whole, whole, whole,
        ],
        out_shape=[
            jax.ShapeDtypeStruct((pieces, EXP_DEV, D // pieces, ff), BF),
            jax.ShapeDtypeStruct((tokens, D), F32),
            jax.ShapeDtypeStruct((tokens, D), F32),
            jax.ShapeDtypeStruct((tokens, D), BF),
            jax.ShapeDtypeStruct((tokens, D), BF),
        ],
        scratch_shapes=[
            pltpu.VMEM((slots, ff), BF), pltpu.VMEM((tokens, D), F32), pltpu.VMEM((tokens, D), F32),
        ],
        compiler_params=kernel_params(),
        name="expert_two",
    )(pos, gate, rows, act, slope, gslot, w_in, w_out)


def shared_kernel(img_ref, gm_ref, win_ref, wout_ref, core_ref, *rest, tiles):
    pieces_in, out_ref, gn_ref = rest[:tiles], rest[tiles], rest[tiles + 1]
    gw_refs, rest = rest[tiles + 2:-6], rest[-6:]
    n2_ref, go_ref, act_ref, gs_ref, gpre_ref, sems = rest
    step = pl.program_id(0)
    ff = win_ref.shape[1]
    rows = out_ref.shape[0]
    here = pl.ds(pl.multiple_of(step * rows, rows), rows)

    @pl.when(step == 0)
    def _():
        each = tiles // 2
        fetch(pieces_in, [ref.at[pl.ds(i * rows, rows)] for ref in (n2_ref, go_ref) for i in range(each)], sems)

    value, slope = gelu_pair(dot(n2_ref[here, :], win_ref[...]))
    act = value.astype(BF)
    act_ref[here, :] = act
    out_ref[...] = dot(act, wout_ref[...])
    gate = dot(image_hot(img_ref[...], gm_ref.shape[0]), gm_ref[...])
    grad = (gate * go_ref[here, :].astype(F32)).astype(BF)
    gs_ref[here, :] = grad
    gpre = (slope * dot(grad, wout_ref[...], 1, 1)).astype(BF)
    gpre_ref[here, :] = gpre
    gn_ref[...] = dot(gpre, win_ref[...], 1, 1)

    @pl.when(step == pl.num_programs(0) - 1)
    def _():
        store_rows(gw_refs, core_ref[0], dot(n2_ref[...], gpre_ref[...], 0, 0), slice(0, ff))
        store_rows(gw_refs, core_ref[0], dot(gs_ref[...], act_ref[...], 0, 0), slice(ff, 2 * ff))


def shared_both(core, pieces, tiles, img_col, gate_mlp, w_in, w_out):
    rows = tiles[0].shape[0]
    steps = len(tiles) // 2
    tokens = rows * steps
    ff = w_in.shape[1]
    moving = pl.BlockSpec((rows, D), lambda m: (m, 0))
    specs, shapes = row_specs(1, pieces, 2 * ff, lambda m: 0)
    return pl.pallas_call(
        functools.partial(shared_kernel, tiles=len(tiles)),
        grid=(steps,),
        in_specs=[
            pl.BlockSpec((rows, 1), lambda m: (m, 0)),
            fixed(*gate_mlp.shape), fixed(D, ff), fixed(ff, D), smem(),
        ] + [hbm()] * len(tiles),
        out_specs=[moving, moving] + specs,
        out_shape=[
            jax.ShapeDtypeStruct((tokens, D), F32),
            jax.ShapeDtypeStruct((tokens, D), F32),
        ] + shapes,
        scratch_shapes=[
            pltpu.VMEM((tokens, D), BF), pltpu.VMEM((tokens, D), BF),
            pltpu.VMEM((tokens, ff), BF), pltpu.VMEM((tokens, D), BF), pltpu.VMEM((tokens, ff), BF),
            pltpu.SemaphoreType.DMA((len(tiles),)),
        ],
        compiler_params=kernel_params(),
        name="shared_both",
    )(img_col, gate_mlp, w_in, w_out, core, *tiles)


def block(
    patches, cond, seg_ids, seg_image, routes, gates, grad_out,
    w_ada, w_qkv, w_out, w_shared_in, w_shared_out, w_expert_in, w_expert_out,
):
    tokens, feat = patches.shape
    parts = D // feat
    rows = tokens // parts
    image_count = cond.shape[0]
    pieces = lax.axis_size("dp")
    me = lax.axis_index("hidden")
    core = lax.axis_index("expert")
    bit_low = (me & 1) == 1
    bit_high = (me & 2) == 2

    def turned(items):
        a, b, c, d = items
        a, b = jnp.where(bit_low, b, a), jnp.where(bit_low, a, b)
        c, d = jnp.where(bit_low, d, c), jnp.where(bit_low, c, d)
        return [
            jnp.where(bit_high, c, a), jnp.where(bit_high, d, b),
            jnp.where(bit_high, a, c), jnp.where(bit_high, b, d),
        ]

    def across(value, mask):
        return lax.ppermute(value, "hidden", [(i, i ^ mask) for i in range(parts)])

    def other_core(value):
        return lax.ppermute(value, "expert", [(0, 1), (1, 0)])

    def exchanged(items):
        return [items[0]] + [across(items[m], m) for m in range(1, parts)]

    def gathered(value):
        return [value] + [across(value, m) for m in range(1, parts)]

    def blocks(value):
        return [value[i * rows:(i + 1) * rows] for i in range(parts)]

    def to_rows(value):
        return jnp.concatenate(turned(exchanged(turned(blocks(value)))), axis=1)

    def to_cols(value):
        cuts = [value[:, i * feat:(i + 1) * feat] for i in range(parts)]
        return jnp.concatenate(turned(exchanged(turned(cuts))), axis=0)

    packed = jnp.concatenate([w_qkv.reshape(D, 3 * feat), w_out.T], axis=1)
    half = lax.dynamic_slice_in_dim(packed, core * (D // 2), D // 2, axis=0)
    shards = [packed]
    for m in range(1, parts):
        mine = across(half, m)
        theirs = other_core(mine)
        first = core == 0
        shards.append(
            jnp.concatenate([jnp.where(first, mine, theirs), jnp.where(first, theirs, mine)], axis=0)
        )
    weights = jnp.stack(shards)

    x_rows = to_rows(patches)
    silu_cond = jax.nn.silu(cond.astype(F32)).astype(BF)
    mod_own = jnp.einsum("id,dkc->ikc", silu_cond, w_ada, preferred_element_type=F32).astype(BF)
    mod = jnp.concatenate(turned(gathered(mod_own)), axis=2).reshape(image_count, 6 * D)
    gate_own = mod[:, 5 * D:]
    gate_both = jnp.stack([gate_own, other_core(gate_own)])
    go_rows = to_rows(grad_out)
    go_own = gathered(go_rows)
    go_far = [other_core(tile) for tile in go_own]

    seg_turned = jnp.concatenate(turned(jnp.split(seg_ids, parts, axis=0)), axis=0)
    image_turned = jnp.concatenate(turned(jnp.split(seg_image, parts, axis=0)), axis=0)
    seg_hot = seg_turned[:, :, None] == jnp.arange(seg_image.shape[1], dtype=jnp.int32)
    tok_image = jnp.sum(jnp.where(seg_hot, image_turned[:, None, :], 0), axis=2).reshape(tokens)
    routes_turned = jnp.concatenate(turned(blocks(routes)), axis=0).T
    gates_turned = jnp.concatenate(turned(blocks(gates)), axis=0).T
    expert_ids = jnp.arange(2 * EXP_DEV, dtype=jnp.int32)[:, None]
    named = [routes_turned[k][None, :] == expert_ids for k in range(2)]
    hot = named[0] | named[1]
    slot = jnp.cumsum(hot.astype(jnp.int32), axis=1) - 1
    pos_all = jnp.where(hot, slot, -1)
    gate_all = jnp.where(named[0], gates_turned[0][None], jnp.where(named[1], gates_turned[1][None], 0.0))

    def for_experts(table):
        low, high = table[:EXP_DEV], table[EXP_DEV:]
        mine = jnp.where(core == 0, low, high)
        away = jnp.where(core == 0, high, low)
        return mine, away

    pos_mine, pos_away = for_experts(pos_all.astype(F32))
    gate_mine, gate_away = for_experts(gate_all)
    meta = other_core(jnp.concatenate([pos_away, gate_away, tok_image.astype(F32)[None]], axis=0))
    pos = jnp.concatenate([pos_mine, meta[:EXP_DEV]], axis=0).astype(jnp.int32)
    gate_rows = jnp.concatenate([gate_mine, meta[EXP_DEV:2 * EXP_DEV]], axis=0)
    img_rows = jnp.stack([tok_image.astype(F32), meta[2 * EXP_DEV]])
    img_col = tok_image[:, None]
    img_own = img_col[:rows]
    seg_row = seg_turned[:1]
    seg_col = seg_row.reshape(rows, 1)

    n1, qkv, ctx, attn, mid, n2 = attn_forward(x_rows, img_own, mod, seg_col, seg_row, weights)
    n2_own = gathered(n2)
    n2_far = [other_core(tile) for tile in n2_own]

    core_id = core.reshape(1).astype(jnp.int32)
    shared_out, gn_shared, *gw_shared = shared_both(
        core_id, pieces, n2_own + go_own, img_col, gate_own, w_shared_in, w_shared_out
    )

    def core_half(parts_of):
        if len(parts_of) == 1:
            values = parts_of[0]
            cut = values.reshape(values.shape[0], pieces, 2, D // (2 * pieces), values.shape[2])
            low, high = cut[:, :, 0], cut[:, :, 1]
            parts_of = jnp.where(core == 0, low, high), jnp.where(core == 0, high, low)
        return parts_of[0] + other_core(parts_of[1])

    def over_dp(values):
        return lax.psum_scatter(values, "dp", scatter_dimension=0, tiled=False).astype(F32)

    half_shared = core_half(gw_shared)[0].astype(BF)
    grad_shared = over_dp(half_shared)

    tiles = n2_own + n2_far + go_own + go_far
    *kept, gw_out_low = expert_one(
        pos, gate_rows, img_rows, gate_both, w_expert_in, tiles, gn_shared, pieces, 0, []
    )
    ge_out_low = over_dp(gw_out_low)
    *kept, gw_out_high = expert_one(
        pos, gate_rows, img_rows, gate_both, w_expert_in, tiles, gn_shared, pieces, EXP_DEV // 2, kept
    )
    ge_out_high = over_dp(gw_out_high)
    gw_in, gn_near, mix_near, gn_far, mix_far = expert_two(
        pos.T, gate_rows.T, *kept, w_expert_in, w_expert_out, pieces
    )
    grad_expert_in = over_dp(gw_in)

    def row_total(near, far, extra):
        from_core = other_core(far).astype(F32)
        cut = blocks(near + extra + from_core)
        out = cut[0]
        for m in range(1, parts):
            moved = across(cut[m].astype(BF), m)
            out = out + moved.astype(F32)
        return out

    gn2 = row_total(gn_near, gn_far, gn_shared)
    mlp = row_total(mix_near, mix_far, shared_out)

    gpatch, gmod_five, *gw_attn = attn_backward(
        core_id, pieces, gn2, mid, attn, go_rows, x_rows, n1, qkv, ctx, img_own, mod, seg_col, seg_row, weights
    )
    out_rows, gmod_last = finish(mid, mlp, go_rows, img_own, gate_own)
    block_out = to_cols(out_rows)
    grad_patches = to_cols(gpatch)

    gmod = jnp.concatenate([gmod_five, gmod_last[None]], axis=0)
    cuts = turned([gmod[:, :, i * feat:(i + 1) * feat] for i in range(parts)])
    got = exchanged(cuts)
    grad_image = (got[0] + got[1] + got[2] + got[3]).astype(BF)
    ada_rows = D // (2 * pieces)
    place = lax.axis_index("dp") * 2 + core

    def everyone(value):
        if pieces > 8 or pieces & (pieces - 1):
            return lax.all_gather(value, ("dp", "expert"), axis=0, tiled=False)
        pair = jnp.stack([value, other_core(value)])
        pairs = [pair]
        for m in range(1, pieces):
            pairs.append(lax.ppermute(pair, "dp", [(i, i ^ m) for i in range(pieces)]))
        return jnp.concatenate(pairs, axis=0)

    silu_mine = lax.dynamic_slice_in_dim(everyone(silu_cond), place * ada_rows, ada_rows, axis=2)
    grad_ada = jnp.einsum("gid,gkic->dkc", silu_mine, everyone(grad_image), preferred_element_type=F32)

    attn_half = core_half(gw_attn)
    attn_sum = attn_half[0]
    for m in range(1, parts):
        attn_sum = attn_sum + across(attn_half[m].astype(BF), m).astype(F32)
    grad_attn = over_dp(attn_sum.astype(BF))
    ff = w_shared_in.shape[1]
    return (
        block_out,
        grad_patches,
        grad_ada,
        grad_attn[:, : 3 * feat].reshape(ada_rows, 3, feat),
        grad_attn[:, 3 * feat:].T,
        grad_shared[:, :ff],
        grad_shared[:, ff:].T,
        grad_expert_in,
        jnp.swapaxes(jnp.concatenate([ge_out_low, ge_out_high], axis=0), 1, 2),
    )


def solution(mesh):
    rows = P(("dp", "expert"), None)
    tiles = P(("dp", "expert"), "hidden")
    return jax.shard_map(
        block,
        mesh=mesh,
        in_specs=(
            tiles, rows, rows, rows, rows, rows, tiles,
            P(None, None, "hidden"),
            P(None, None, "hidden"),
            P("hidden", None),
            P(None, "hidden"),
            P("hidden", None),
            P("expert", None, "hidden"),
            P("expert", "hidden", None),
        ),
        out_specs=(
            tiles,
            tiles,
            P(("dp", "expert"), None, "hidden"),
            P(("dp", "expert"), None, "hidden"),
            P("hidden", ("dp", "expert")),
            P(("dp", "expert"), "hidden"),
            P("hidden", ("dp", "expert")),
            P("expert", "dp", "hidden"),
            P("expert", "hidden", "dp"),
        ),
        check_vma=False,
    )
```

```python
import functools

import jax
import jax.numpy as jnp
from jax import lax
from jax.experimental import pallas as pl
from jax.experimental.pallas import tpu as pltpu
from jax.sharding import PartitionSpec as P


D = 768
HEAD_DIM = 64
EXP_DEV = 4
CAP = 384
EPSILON = 1e-06
NEG_FILL = -1e30
BF = jnp.bfloat16
F32 = jnp.float32
GELU_C = 0.7978845608028654
GELU_A = 0.044715


def kernel_params():
    return pltpu.CompilerParams(vmem_limit_bytes=60 * 1024 * 1024)


def dot(a, b, lhs=1, rhs=0):
    return lax.dot_general(a, b, (((lhs,), (rhs,)), ((), ())), preferred_element_type=F32)


def gelu_pair(values):
    square = values * values
    inner = GELU_C * values * (1.0 + GELU_A * square)
    bent = jnp.tanh(inner)
    half = 0.5 * (1.0 + bent)
    slope = half + (0.5 * values) * (1.0 - bent * bent) * (GELU_C * (1.0 + (3.0 * GELU_A) * square))
    return values * half, slope


def normalize(values):
    centre = values - jnp.mean(values, axis=-1, keepdims=True)
    spread = lax.rsqrt(jnp.mean(centre * centre, axis=-1, keepdims=True) + EPSILON)
    return centre * spread, spread


def norm_back(upstream, unit, spread):
    return spread * (
        upstream
        - jnp.mean(upstream, axis=-1, keepdims=True)
        - unit * jnp.mean(upstream * unit, axis=-1, keepdims=True)
    )


def image_hot(image_col, count):
    lanes = lax.broadcasted_iota(jnp.int32, (image_col.shape[0], count), 1)
    return (image_col == lanes).astype(BF)


def probs_of(queries, keys, same):
    scores = dot(queries, keys, 1, 1) * (HEAD_DIM ** -0.5)
    scores = jnp.where(same, scores, NEG_FILL)
    raised = jnp.exp(scores - jnp.max(scores, axis=-1, keepdims=True))
    return raised * (1.0 / jnp.sum(raised, axis=-1, keepdims=True))


def attn_fwd_kernel(
    x_ref, img_ref, mod_ref, segc_ref, segr_ref, core_ref, *rest, shards, extras,
):
    w_in, rest = rest[:shards], rest[shards + extras:]
    n1_ref, qkv_ref, ctx_ref, attn_ref, mid_ref, n2_ref, w_ref, sems = rest
    step = pl.program_id(0)
    fetch_weights(w_in, w_ref, core_ref[0], sems)
    feat = ctx_ref.shape[2]
    images = mod_ref.shape[0]

    def mod(k):
        return dot(image_hot(img_ref[...], images), mod_ref[:, k * D:(k + 1) * D])

    @pl.when(step == 0)
    def _():
        unit, _ = normalize(x_ref[...].astype(F32))
        n1_ref[...] = (unit * (1.0 + mod(1)) + mod(0)).astype(BF)
        attn_ref[...] = jnp.zeros_like(attn_ref)

    qkv = dot(n1_ref[...], w_ref[step, :, : 3 * feat]).astype(BF)
    qkv_ref[0] = qkv
    same = segc_ref[...] == segr_ref[...]
    parts = []
    for a in range(feat // HEAD_DIM):
        lo = a * HEAD_DIM
        probs = probs_of(qkv[:, lo:lo + HEAD_DIM], qkv[:, feat + lo:feat + lo + HEAD_DIM], same)
        parts.append(dot(probs.astype(BF), qkv[:, 2 * feat + lo:2 * feat + lo + HEAD_DIM]).astype(BF))
    context = jnp.concatenate(parts, axis=1)
    ctx_ref[0] = context
    attn_ref[...] += dot(context, w_ref[step, :, 3 * feat:], 1, 1)

    @pl.when(step == pl.num_programs(0) - 1)
    def _():
        mid = x_ref[...].astype(F32) + mod(2) * attn_ref[...]
        mid_ref[...] = mid
        unit, _ = normalize(mid)
        n2_ref[...] = (unit * (1.0 + mod(4)) + mod(3)).astype(BF)


def fixed(*shape):
    return pl.BlockSpec(shape, lambda m: (0,) * len(shape))


def stepped(*shape):
    return pl.BlockSpec((1,) + shape, lambda m: (m,) + (0,) * len(shape))


def attn_forward(core, x_rows, img_col, mod, seg_col, seg_row, weights, extras, parts):
    rows = x_rows.shape[0]
    feat = D // parts
    return pl.pallas_call(
        functools.partial(attn_fwd_kernel, shards=len(weights), extras=len(extras)),
        grid=(parts,),
        in_specs=[
            fixed(rows, D), fixed(rows, 1), fixed(*mod.shape), fixed(rows, 1), fixed(1, rows), smem(),
        ] + [hbm()] * (len(weights) + len(extras)),
        out_specs=[
            fixed(rows, D), stepped(rows, 3 * feat), stepped(rows, feat),
            fixed(rows, D), fixed(rows, D), fixed(rows, D),
        ],
        out_shape=[
            jax.ShapeDtypeStruct((rows, D), BF),
            jax.ShapeDtypeStruct((parts, rows, 3 * feat), BF),
            jax.ShapeDtypeStruct((parts, rows, feat), BF),
            jax.ShapeDtypeStruct((rows, D), F32),
            jax.ShapeDtypeStruct((rows, D), F32),
            jax.ShapeDtypeStruct((rows, D), BF),
        ],
        scratch_shapes=[pltpu.VMEM((parts, D, 4 * feat), BF), pltpu.SemaphoreType.DMA((len(weights),))],
        compiler_params=kernel_params(),
        name="attn_fwd",
    )(x_rows, img_col, mod, seg_col, seg_row, core, *weights, *extras)


def image_sum(hot, values):
    high = values.astype(BF)
    rest = values - high.astype(F32)
    middle = rest.astype(BF)
    low = (rest - middle.astype(F32)).astype(BF)
    return dot(hot, high, 0, 0) + (dot(hot, middle, 0, 0) + dot(hot, low, 0, 0))


def attn_bwd_kernel(
    gn2_ref, mid_ref, attn_ref, go_ref, x_ref, n1_ref, qkv_ref, ctx_ref, img_ref, mod_ref,
    segc_ref, segr_ref, core_ref, *rest, shards,
):
    w_in, (gpatch_ref, gmod_ref), rest = rest[:shards], rest[shards:shards + 2], rest[shards + 2:]
    grad_refs, (gmid_ref, gattn_ref, gn1_ref, w_ref, sems) = rest[:-5], rest[-5:]
    step = pl.program_id(0)
    fetch_weights(w_in, w_ref, core_ref[0], sems)
    feat = ctx_ref.shape[2]
    images = mod_ref.shape[0]
    scale = HEAD_DIM ** -0.5

    def hot():
        return image_hot(img_ref[...], images)

    def mod(k):
        return dot(hot(), mod_ref[:, k * D:(k + 1) * D])

    @pl.when(step == 0)
    def _():
        unit, spread = normalize(mid_ref[...])
        gn2 = gn2_ref[...]
        gmid = go_ref[...].astype(F32) + norm_back(gn2 * (1.0 + mod(4)), unit, spread)
        gmid_ref[...] = gmid
        gattn_ref[...] = (mod(2) * gmid).astype(BF)
        gmod_ref[2] = image_sum(hot(), gmid * attn_ref[...])
        gmod_ref[3] = image_sum(hot(), gn2)
        gmod_ref[4] = image_sum(hot(), gn2 * unit)
        gn1_ref[...] = jnp.zeros_like(gn1_ref)

    gattn = gattn_ref[...]
    gctx = dot(gattn, w_ref[step, :, 3 * feat:]).astype(BF)
    same = segc_ref[...] == segr_ref[...]
    gq, gk, gv = [], [], []
    for a in range(feat // HEAD_DIM):
        lo = a * HEAD_DIM
        queries = qkv_ref[0, :, lo:lo + HEAD_DIM]
        keys = qkv_ref[0, :, feat + lo:feat + lo + HEAD_DIM]
        values = qkv_ref[0, :, 2 * feat + lo:2 * feat + lo + HEAD_DIM]
        gc = gctx[:, lo:lo + HEAD_DIM]
        probs = probs_of(queries, keys, same)
        gv.append(dot(probs.astype(BF), gc, 0, 0).astype(BF))
        gp = dot(gc, values, 1, 1)
        inner = jnp.sum(probs * gp, axis=-1, keepdims=True)
        gs = (probs * (gp - inner)).astype(BF)
        gq.append((dot(gs, keys) * scale).astype(BF))
        gk.append((dot(gs, queries, 0, 0) * scale).astype(BF))
    grows = jnp.concatenate(gq + gk + gv, axis=1)
    store_rows(grad_refs, core_ref, dot(n1_ref[...], grows, 0, 0), slice(0, 3 * feat))
    store_rows(grad_refs, core_ref, dot(gattn, ctx_ref[0], 0, 0), slice(3 * feat, 4 * feat))
    gn1_ref[...] += dot(grows, w_ref[step, :, : 3 * feat], 1, 1)

    @pl.when(step == pl.num_programs(0) - 1)
    def _():
        unit, spread = normalize(x_ref[...].astype(F32))
        gn1 = gn1_ref[...]
        back = norm_back(gn1 * (1.0 + mod(1)), unit, spread)
        gpatch_ref[...] = (gmid_ref[...] + back).astype(BF)
        gmod_ref[0] = image_sum(hot(), gn1)
        gmod_ref[1] = image_sum(hot(), gn1 * unit)


def store_rows(refs, core_ref, values, cols):
    if len(refs) == 1:
        refs[0][0, :, cols] = values
        return
    mine, theirs = refs
    pieces, rows = mine.shape[1], mine.shape[2]
    for p in range(pieces):
        low = values[2 * p * rows:(2 * p + 1) * rows]
        high = values[(2 * p + 1) * rows:(2 * p + 2) * rows]
        mine[0, p ^ core_ref[1], :, cols] = jnp.where(core_ref[0] == 0, low, high)
        theirs[0, p ^ core_ref[1], :, cols] = jnp.where(core_ref[0] == 0, high, low)


def row_specs(parts, pieces, width, index):
    rows = D // (2 * pieces)
    if rows % 8:
        shape = (D, width)
        count = 1
    else:
        shape = (pieces, rows, width)
        count = 2
    spec = pl.BlockSpec((1,) + shape, lambda m: (index(m),) + (0,) * len(shape))
    return [spec] * count, [jax.ShapeDtypeStruct((parts,) + shape, F32)] * count


def smem():
    return pl.BlockSpec(memory_space=pltpu.SMEM)


def hbm():
    return pl.BlockSpec(memory_space=pl.ANY)


def fetch(refs, targets, sems):
    copies = [pltpu.make_async_copy(refs[i], targets[i], sems.at[i]) for i in range(len(refs))]
    for copy in copies:
        copy.start()
    for copy in copies:
        copy.wait()


def laid_out(refs, target):
    places, start = [], 0
    for ref in refs:
        places.append(target.at[pl.ds(start, ref.shape[0])])
        start += ref.shape[0]
    return places


def weight_copies(refs, w_ref, core, sems):
    half = D // 2
    mine = pl.multiple_of(core * half, half)
    theirs = pl.multiple_of((1 - core) * half, half)
    places = [(0, w_ref.at[0])]
    for base in (mine, theirs):
        for m in (1, 2):
            places.append((m, w_ref.at[m, pl.ds(base, half)]))
        for k in (0, 1):
            places.append((3, w_ref.at[3, pl.ds(pl.multiple_of(base + k * (half // 2), half // 2), half // 2)]))
    return [(m, pltpu.make_async_copy(ref, place, sems.at[i])) for i, (ref, (m, place)) in enumerate(zip(refs, places))]


def fetch_weights(refs, w_ref, core, sems):
    step = pl.program_id(0)
    copies = weight_copies(refs, w_ref, core, sems)

    @pl.when(step == 0)
    def _():
        for _, copy in copies:
            copy.start()

    for shard in range(w_ref.shape[0]):
        @pl.when(step == shard)
        def _():
            for m, copy in copies:
                if m == shard:
                    copy.wait()


def attn_backward(core, pieces, gn2, mid, attn, go, x_rows, n1, qkv, ctx, img_col, mod, seg_col, seg_row, weights):
    rows = x_rows.shape[0]
    parts = qkv.shape[0]
    feat = D // parts
    images = mod.shape[0]
    whole = fixed(rows, D)
    specs, shapes = row_specs(parts, pieces, 4 * feat, lambda m: m)
    return pl.pallas_call(
        functools.partial(attn_bwd_kernel, shards=len(weights)),
        grid=(parts,),
        in_specs=[
            whole, whole, whole, whole, whole, whole,
            stepped(rows, 3 * feat), stepped(rows, feat),
            fixed(rows, 1), fixed(*mod.shape), fixed(rows, 1), fixed(1, rows),
            smem(),
        ] + [hbm()] * len(weights),
        out_specs=[whole, fixed(5, images, D)] + specs,
        out_shape=[
            jax.ShapeDtypeStruct((rows, D), BF),
            jax.ShapeDtypeStruct((5, images, D), F32),
        ] + shapes,
        scratch_shapes=[
            pltpu.VMEM((rows, D), F32), pltpu.VMEM((rows, D), BF), pltpu.VMEM((rows, D), F32),
            pltpu.VMEM((parts, D, 4 * feat), BF), pltpu.SemaphoreType.DMA((len(weights),)),
        ],
        compiler_params=kernel_params(),
        name="attn_bwd",
    )(gn2, mid, attn, go, x_rows, n1, qkv, ctx, img_col, mod, seg_col, seg_row, core, *weights)


def finish_kernel(mid_ref, mlp_ref, go_ref, img_ref, gate_ref, out_ref, gmod_ref):
    hot = image_hot(img_ref[...], gate_ref.shape[0])
    mlp = mlp_ref[...]
    out_ref[...] = (mid_ref[...] + dot(hot, gate_ref[...]) * mlp).astype(BF)
    gmod_ref[...] = image_sum(hot, go_ref[...].astype(F32) * mlp)


def finish(mid, mlp, go, img_col, gate):
    return pl.pallas_call(
        finish_kernel,
        out_shape=[
            jax.ShapeDtypeStruct(mid.shape, BF),
            jax.ShapeDtypeStruct(gate.shape, F32),
        ],
        compiler_params=kernel_params(),
        name="finish",
    )(mid, mlp, go, img_col, gate)


def store_split(ref, values):
    pieces, rows = ref.shape[0], ref.shape[2]
    for p in range(pieces):
        ref[p, 0] = values[p * rows:(p + 1) * rows].astype(ref.dtype)


def expert_one_kernel(pos_ref, gate_ref, img_ref, gm_ref, win_ref, *rest, tiles, first, kept):
    pieces_in, rest = rest[:tiles], rest[tiles + 1 + kept:]
    rows_ref, act_ref, slope_ref, gslot_ref, gw_ref, n2_ref, go_ref, sems = rest
    local = first + pl.program_id(0)
    tokens = n2_ref.shape[1]
    images = gm_ref.shape[1]
    each = tiles // 4

    @pl.when(pl.program_id(0) == 0)
    def _():
        targets = []
        for i, (ref, j) in enumerate(((n2_ref, 0), (n2_ref, 1), (go_ref, 0), (go_ref, 1))):
            targets += laid_out(pieces_in[i * each:(i + 1) * each], ref.at[j])
        fetch(pieces_in, targets, sems)

    def block(j, carry):
        where_ = pos_ref[pl.ds(j * EXP_DEV + local, 1), :]
        mask = lax.broadcasted_iota(jnp.int32, (CAP, tokens), 0) == where_
        pick = mask.astype(BF)
        rows = dot(pick, n2_ref[j]).astype(BF)
        slots = pl.ds(pl.multiple_of(j * CAP, CAP), CAP)
        rows_ref[0, slots, :] = rows
        gate = jnp.sum(jnp.where(mask, gate_ref[pl.ds(j * EXP_DEV + local, 1), :], 0.0), axis=1, keepdims=True)
        image = jnp.sum(jnp.where(mask, img_ref[pl.ds(j, 1), :], 0.0), axis=1, keepdims=True)
        hot = image_hot(image.astype(jnp.int32), images)
        grad = dot(hot, gm_ref[j]) * dot(pick, go_ref[j])
        gslot_ref[0, slots, :] = (gate * grad).astype(BF)
        value, slope = gelu_pair(dot(rows, win_ref[0]))
        act_ref[0, slots, :] = value.astype(BF)
        slope_ref[0, slots, :] = slope
        return carry

    lax.fori_loop(0, 2, block, 0)
    store_split(gw_ref, dot(gslot_ref[0], act_ref[0], 0, 0))


def expert_one(pos, gate, img, gate_mlp, w_in, tiles, after, pieces, first, kept):
    tokens = pos.shape[1]
    slots = 2 * CAP
    ff = w_in.shape[2]
    count = EXP_DEV // 2

    def shifted(*shape):
        return pl.BlockSpec((1,) + shape, lambda m: (m + first,) + (0,) * len(shape))

    fixed_ins = 5
    return pl.pallas_call(
        functools.partial(expert_one_kernel, tiles=len(tiles), first=first, kept=len(kept)),
        grid=(count,),
        in_specs=[
            fixed(2 * EXP_DEV, tokens), fixed(2 * EXP_DEV, tokens), fixed(2, tokens),
            fixed(*gate_mlp.shape), shifted(D, ff),
        ] + [hbm()] * (len(tiles) + 1 + len(kept)),
        out_specs=[
            shifted(slots, D), shifted(slots, ff), shifted(slots, ff), shifted(slots, D),
            pl.BlockSpec((pieces, 1, D // pieces, ff), lambda m: (0, m, 0, 0)),
        ],
        out_shape=[
            jax.ShapeDtypeStruct((EXP_DEV, slots, D), BF),
            jax.ShapeDtypeStruct((EXP_DEV, slots, ff), BF),
            jax.ShapeDtypeStruct((EXP_DEV, slots, ff), F32),
            jax.ShapeDtypeStruct((EXP_DEV, slots, D), BF),
            jax.ShapeDtypeStruct((pieces, count, D // pieces, ff), BF),
        ],
        scratch_shapes=[
            pltpu.VMEM((2, tokens, D), BF), pltpu.VMEM((2, tokens, D), BF),
            pltpu.SemaphoreType.DMA((len(tiles),)),
        ],
        input_output_aliases={fixed_ins + len(tiles) + 1 + i: i for i in range(len(kept))},
        compiler_params=kernel_params(),
        name="expert_one",
    )(pos, gate, img, gate_mlp, w_in, *tiles, after, *kept)


def expert_two_kernel(
    pos_ref, gate_ref, rows_ref, act_ref, slope_ref, gslot_ref, win_ref, wout_ref,
    gw_ref, gn_ref, mix_ref, gn_far_ref, mix_far_ref,
    gpre_ref, gn_acc, mix_acc,
):
    local = pl.program_id(0)
    count = pl.num_programs(0)
    tokens = pos_ref.shape[0]
    lanes = lax.broadcasted_iota(jnp.int32, pos_ref.shape, 1)

    @pl.when(local == 0)
    def _():
        for ref in (gn_ref, mix_ref, gn_acc, mix_acc):
            ref[...] = jnp.zeros_like(ref)

    for j, (gn, mix) in enumerate(((gn_ref, mix_ref), (gn_acc, mix_acc))):
        slots = slice(j * CAP, (j + 1) * CAP)
        grad_pre = (slope_ref[0, slots, :] * dot(gslot_ref[0, slots, :], wout_ref[0], 1, 1)).astype(BF)
        gpre_ref[slots, :] = grad_pre
        grad_in = dot(grad_pre, win_ref[0], 1, 1).astype(BF)
        result = dot(act_ref[0, slots, :], wout_ref[0]).astype(BF)
        here = lanes == j * count + local
        where_ = jnp.sum(jnp.where(here, pos_ref[...], 0), axis=1, keepdims=True)
        gate = jnp.sum(jnp.where(here, gate_ref[...], 0.0), axis=1, keepdims=True)
        pick = (lax.broadcasted_iota(jnp.int32, (tokens, CAP), 1) == where_).astype(BF)
        gn[...] += dot(pick, grad_in)
        mix[...] += gate * dot(pick, result)
    store_split(gw_ref, dot(rows_ref[0], gpre_ref[...], 0, 0))

    @pl.when(local == count - 1)
    def _():
        gn_far_ref[...] = gn_acc[...].astype(BF)
        mix_far_ref[...] = mix_acc[...].astype(BF)


def expert_two(pos, gate, rows, act, slope, gslot, w_in, w_out, pieces):
    tokens = pos.shape[0]
    slots = 2 * CAP
    ff = w_in.shape[2]
    whole = fixed(tokens, D)
    return pl.pallas_call(
        expert_two_kernel,
        grid=(EXP_DEV,),
        in_specs=[
            fixed(tokens, 2 * EXP_DEV), fixed(tokens, 2 * EXP_DEV),
            stepped(slots, D), stepped(slots, ff), stepped(slots, ff), stepped(slots, D),
            stepped(D, ff), stepped(ff, D),
        ],
        out_specs=[
            pl.BlockSpec((pieces, 1, D // pieces, ff), lambda m: (0, m, 0, 0)),
            whole, whole, whole, whole,
        ],
        out_shape=[
            jax.ShapeDtypeStruct((pieces, EXP_DEV, D // pieces, ff), BF),
            jax.ShapeDtypeStruct((tokens, D), F32),
            jax.ShapeDtypeStruct((tokens, D), F32),
            jax.ShapeDtypeStruct((tokens, D), BF),
            jax.ShapeDtypeStruct((tokens, D), BF),
        ],
        scratch_shapes=[
            pltpu.VMEM((slots, ff), BF), pltpu.VMEM((tokens, D), F32), pltpu.VMEM((tokens, D), F32),
        ],
        compiler_params=kernel_params(),
        name="expert_two",
    )(pos, gate, rows, act, slope, gslot, w_in, w_out)


def shared_kernel(img_ref, gm_ref, win_ref, wout_ref, core_ref, *rest, tiles):
    pieces_in, out_ref, gn_ref = rest[:tiles], rest[tiles], rest[tiles + 1]
    gw_refs, rest = rest[tiles + 2:-6], rest[-6:]
    n2_ref, go_ref, act_ref, gs_ref, gpre_ref, sems = rest
    step = pl.program_id(0)
    ff = win_ref.shape[1]
    rows = out_ref.shape[0]
    here = pl.ds(pl.multiple_of(step * rows, rows), rows)

    @pl.when(step == 0)
    def _():
        each = tiles // 2
        fetch(pieces_in, laid_out(pieces_in[:each], n2_ref) + laid_out(pieces_in[each:], go_ref), sems)

    value, slope = gelu_pair(dot(n2_ref[here, :], win_ref[...]))
    act = value.astype(BF)
    act_ref[here, :] = act
    out_ref[...] = dot(act, wout_ref[...])
    gate = dot(image_hot(img_ref[...], gm_ref.shape[0]), gm_ref[...])
    grad = (gate * go_ref[here, :].astype(F32)).astype(BF)
    gs_ref[here, :] = grad
    gpre = (slope * dot(grad, wout_ref[...], 1, 1)).astype(BF)
    gpre_ref[here, :] = gpre
    gn_ref[...] = dot(gpre, win_ref[...], 1, 1)

    @pl.when(step == pl.num_programs(0) - 1)
    def _():
        store_rows(gw_refs, core_ref, dot(n2_ref[...], gpre_ref[...], 0, 0), slice(0, ff))
        store_rows(gw_refs, core_ref, dot(gs_ref[...], act_ref[...], 0, 0), slice(ff, 2 * ff))


def shared_both(core, pieces, tiles, img_col, gate_mlp, w_in, w_out):
    rows = tiles[0].shape[0]
    tokens = img_col.shape[0]
    steps = tokens // rows
    ff = w_in.shape[1]
    moving = pl.BlockSpec((rows, D), lambda m: (m, 0))
    specs, shapes = row_specs(1, pieces, 2 * ff, lambda m: 0)
    return pl.pallas_call(
        functools.partial(shared_kernel, tiles=len(tiles)),
        grid=(steps,),
        in_specs=[
            pl.BlockSpec((rows, 1), lambda m: (m, 0)),
            fixed(*gate_mlp.shape), fixed(D, ff), fixed(ff, D), smem(),
        ] + [hbm()] * len(tiles),
        out_specs=[moving, moving] + specs,
        out_shape=[
            jax.ShapeDtypeStruct((tokens, D), F32),
            jax.ShapeDtypeStruct((tokens, D), F32),
        ] + shapes,
        scratch_shapes=[
            pltpu.VMEM((tokens, D), BF), pltpu.VMEM((tokens, D), BF),
            pltpu.VMEM((tokens, ff), BF), pltpu.VMEM((tokens, D), BF), pltpu.VMEM((tokens, ff), BF),
            pltpu.SemaphoreType.DMA((len(tiles),)),
        ],
        compiler_params=kernel_params(),
        name="shared_both",
    )(img_col, gate_mlp, w_in, w_out, core, *tiles)


def block(
    patches, cond, seg_ids, seg_image, routes, gates, grad_out,
    w_ada, w_qkv, w_out, w_shared_in, w_shared_out, w_expert_in, w_expert_out,
):
    tokens, feat = patches.shape
    parts = D // feat
    rows = tokens // parts
    image_count = cond.shape[0]
    pieces = lax.axis_size("dp")
    me = lax.axis_index("hidden")
    core = lax.axis_index("expert")
    bit_low = (me & 1) == 1
    bit_high = (me & 2) == 2

    def turned(items):
        a, b, c, d = items
        a, b = jnp.where(bit_low, b, a), jnp.where(bit_low, a, b)
        c, d = jnp.where(bit_low, d, c), jnp.where(bit_low, c, d)
        return [
            jnp.where(bit_high, c, a), jnp.where(bit_high, d, b),
            jnp.where(bit_high, a, c), jnp.where(bit_high, b, d),
        ]

    def across(value, mask):
        return lax.ppermute(value, "hidden", [(i, i ^ mask) for i in range(parts)])

    def other_core(value):
        return lax.ppermute(value, "expert", [(0, 1), (1, 0)])

    def exchanged(items):
        return [items[0]] + [across(items[m], m) for m in range(1, parts)]

    def gathered(value):
        return [value] + [across(value, m) for m in range(1, parts)]

    def passed_on(value):
        one, two = across(value, 1), across(value, 2)
        cut = value.shape[0] // 2
        return [one, two, across(one[:cut], 2), across(two[cut:], 1)]

    def blocks(value):
        return [value[i * rows:(i + 1) * rows] for i in range(parts)]

    def to_rows(value):
        return jnp.concatenate(turned(exchanged(turned(blocks(value)))), axis=1)

    def to_cols(value):
        cuts = [value[:, i * feat:(i + 1) * feat] for i in range(parts)]
        return jnp.concatenate(turned(exchanged(turned(cuts))), axis=0)

    packed = jnp.concatenate([w_qkv.reshape(D, 3 * feat), w_out.T], axis=1)
    half = lax.dynamic_slice_in_dim(packed, core * (D // 2), D // 2, axis=0)
    halves = passed_on(half)
    weights = [packed] + halves + [other_core(part) for part in halves]
    flip = lax.axis_index("dp") if pieces == 4 else jnp.zeros((), jnp.int32)
    core_id = jnp.stack([core, flip]).astype(jnp.int32)

    x_rows = to_rows(patches)
    silu_cond = jax.nn.silu(cond.astype(F32)).astype(BF)
    mod_own = jnp.einsum("id,dkc->ikc", silu_cond, w_ada, preferred_element_type=F32).astype(BF)
    mod = jnp.concatenate(turned(gathered(mod_own)), axis=2).reshape(image_count, 6 * D)
    gate_own = mod[:, 5 * D:]
    gate_both = jnp.stack([gate_own, other_core(gate_own)])
    go_rows = to_rows(grad_out)
    go_own = [go_rows] + passed_on(go_rows)
    go_far = [other_core(tile) for tile in go_own]

    seg_turned = jnp.concatenate(turned(jnp.split(seg_ids, parts, axis=0)), axis=0)
    image_turned = jnp.concatenate(turned(jnp.split(seg_image, parts, axis=0)), axis=0)
    seg_hot = seg_turned[:, :, None] == jnp.arange(seg_image.shape[1], dtype=jnp.int32)
    tok_image = jnp.sum(jnp.where(seg_hot, image_turned[:, None, :], 0), axis=2).reshape(tokens)
    routes_turned = jnp.concatenate(turned(blocks(routes)), axis=0).T
    gates_turned = jnp.concatenate(turned(blocks(gates)), axis=0).T
    expert_ids = jnp.arange(2 * EXP_DEV, dtype=jnp.int32)[:, None]
    named = [routes_turned[k][None, :] == expert_ids for k in range(2)]
    hot = named[0] | named[1]
    slot = jnp.cumsum(hot.astype(jnp.int32), axis=1) - 1
    pos_all = jnp.where(hot, slot, -1)
    gate_all = jnp.where(named[0], gates_turned[0][None], jnp.where(named[1], gates_turned[1][None], 0.0))

    def for_experts(table):
        low, high = table[:EXP_DEV], table[EXP_DEV:]
        mine = jnp.where(core == 0, low, high)
        away = jnp.where(core == 0, high, low)
        return mine, away

    pos_mine, pos_away = for_experts(pos_all.astype(F32))
    gate_mine, gate_away = for_experts(gate_all)
    meta = other_core(jnp.concatenate([pos_away, gate_away, tok_image.astype(F32)[None]], axis=0))
    pos = jnp.concatenate([pos_mine, meta[:EXP_DEV]], axis=0).astype(jnp.int32)
    gate_rows = jnp.concatenate([gate_mine, meta[EXP_DEV:2 * EXP_DEV]], axis=0)
    img_rows = jnp.stack([tok_image.astype(F32), meta[2 * EXP_DEV]])
    img_col = tok_image[:, None]
    img_own = img_col[:rows]
    seg_row = seg_turned[:1]
    seg_col = seg_row.reshape(rows, 1)

    ada_rows = D // (2 * pieces)
    place = lax.axis_index("dp") * 2 + core

    def everyone(value):
        if pieces > 8 or pieces & (pieces - 1):
            return lax.all_gather(value, ("dp", "expert"), axis=0, tiled=False)
        own = [value]
        for m in range(1, pieces):
            own.append(lax.ppermute(value, "dp", [(i, i ^ m) for i in range(pieces)]))
        own = jnp.stack(own)
        return jnp.concatenate([own, other_core(own)], axis=0)

    silu_mine = lax.dynamic_slice_in_dim(everyone(silu_cond), place * ada_rows, ada_rows, axis=2)
    pos_cols, gate_cols = pos.T, gate_rows.T
    n1, qkv, ctx, attn, mid, n2 = attn_forward(
        core_id, x_rows, img_own, mod, seg_col, seg_row, weights,
        [pos, gate_rows, img_rows, pos_cols, gate_cols, gate_both, img_col, silu_mine], parts,
    )
    n2_own = [n2] + passed_on(n2)
    n2_far = [other_core(tile) for tile in n2_own]

    shared_out, gn_shared, *gw_shared = shared_both(
        core_id, pieces, n2_own + go_own, img_col, gate_own, w_shared_in, w_shared_out
    )

    def core_half(parts_of):
        if len(parts_of) == 1:
            values = parts_of[0]
            cut = values.reshape(values.shape[0], pieces, 2, D // (2 * pieces), values.shape[2])
            low, high = cut[:, :, 0], cut[:, :, 1]
            parts_of = jnp.where(core == 0, low, high), jnp.where(core == 0, high, low)
        return parts_of[0] + other_core(parts_of[1])

    def over_dp(values):
        return lax.psum_scatter(values, "dp", scatter_dimension=0, tiled=False).astype(F32)

    def pieces_over_dp(values):
        if pieces != 4:
            return over_dp(values.astype(BF))
        total = values[0]
        for m in range(1, pieces):
            moved = lax.ppermute(values[m].astype(BF), "dp", [(i, i ^ m) for i in range(pieces)])
            total = total + moved.astype(F32)
        return total

    half_shared = core_half(gw_shared)[0]
    grad_shared = pieces_over_dp(half_shared)

    tiles = n2_own + n2_far + go_own + go_far
    *kept, gw_out_low = expert_one(pos, gate_rows, img_rows, gate_both, w_expert_in, tiles, gn_shared, pieces, 0, [])
    ge_out_low = over_dp(gw_out_low)
    *kept, gw_out_high = expert_one(
        pos, gate_rows, img_rows, gate_both, w_expert_in, tiles, gn_shared, pieces, EXP_DEV // 2, kept
    )
    ge_out_high = over_dp(gw_out_high)
    gw_in, gn_near, mix_near, gn_far, mix_far = expert_two(
        pos_cols, gate_cols, *kept, w_expert_in, w_expert_out, pieces
    )
    grad_expert_in = over_dp(gw_in)

    def row_total(near, far, extra):
        from_core = other_core(far).astype(F32)
        cut = blocks(near + extra + from_core)
        out = cut[0]
        for m in range(1, parts):
            moved = across(cut[m].astype(BF), m)
            out = out + moved.astype(F32)
        return out

    gn2 = row_total(gn_near, gn_far, gn_shared)
    mlp = row_total(mix_near, mix_far, shared_out)

    gpatch, gmod_five, *gw_attn = attn_backward(
        core_id, pieces, gn2, mid, attn, go_rows, x_rows, n1, qkv, ctx, img_own, mod, seg_col, seg_row, weights
    )
    out_rows, gmod_last = finish(mid, mlp, go_rows, img_own, gate_own)
    block_out = to_cols(out_rows)
    grad_patches = to_cols(gpatch)

    gmod = jnp.concatenate([gmod_five, gmod_last[None]], axis=0)
    cuts = turned([gmod[:, :, i * feat:(i + 1) * feat] for i in range(parts)])
    got = exchanged(cuts)
    grad_image = (got[0] + got[1] + got[2] + got[3]).astype(BF)
    image_all = everyone(grad_image)
    grad_ada = jnp.einsum("gid,gkic->dkc", silu_mine, image_all, preferred_element_type=F32)

    attn_half = core_half(gw_attn)
    attn_sum = attn_half[0]
    for m in range(1, parts):
        moved = across(attn_half[m].astype(BF), m)
        attn_sum = attn_sum + moved.astype(F32)
    grad_attn = pieces_over_dp(attn_sum)
    ff = w_shared_in.shape[1]
    return (
        block_out,
        grad_patches,
        grad_ada,
        grad_attn[:, : 3 * feat].reshape(ada_rows, 3, feat),
        grad_attn[:, 3 * feat:].T,
        grad_shared[:, :ff],
        grad_shared[:, ff:].T,
        grad_expert_in,
        jnp.swapaxes(jnp.concatenate([ge_out_low, ge_out_high], axis=0), 1, 2),
    )


def solution(mesh):
    rows = P(("dp", "expert"), None)
    tiles = P(("dp", "expert"), "hidden")
    return jax.shard_map(
        block,
        mesh=mesh,
        in_specs=(
            tiles, rows, rows, rows, rows, rows, tiles,
            P(None, None, "hidden"),
            P(None, None, "hidden"),
            P("hidden", None),
            P(None, "hidden"),
            P("hidden", None),
            P("expert", None, "hidden"),
            P("expert", "hidden", None),
        ),
        out_specs=(
            tiles,
            tiles,
            P(("dp", "expert"), None, "hidden"),
            P(("dp", "expert"), None, "hidden"),
            P("hidden", ("dp", "expert")),
            P(("dp", "expert"), "hidden"),
            P("hidden", ("dp", "expert")),
            P("expert", "dp", "hidden"),
            P("expert", "hidden", "dp"),
        ),
        check_vma=False,
    )
```

```python
import functools

import jax
import jax.numpy as jnp
from jax import lax
from jax.experimental import pallas as pl
from jax.experimental.pallas import tpu as pltpu
from jax.sharding import PartitionSpec as P


D = 768
HEAD_DIM = 64
EXP_DEV = 4
CAP = 384
EPSILON = 1e-06
NEG_FILL = -1e30
DP, EXP, HID = "dp", "expert", "hidden"
BF = jnp.bfloat16
F32 = jnp.float32
GELU_C = 0.7978845608028654
GELU_A = 0.044715


def kernel_params():
    return pltpu.CompilerParams(vmem_limit_bytes=60 * 1024 * 1024)


def dot(a, b, lhs=1, rhs=0):
    return lax.dot_general(a, b, (((lhs,), (rhs,)), ((), ())), preferred_element_type=F32)


def gelu_pair(values):
    square = values * values
    inner = GELU_C * values * (1.0 + GELU_A * square)
    bent = jnp.tanh(inner)
    half = 0.5 * (1.0 + bent)
    slope = half + (0.5 * values) * (1.0 - bent * bent) * (GELU_C * (1.0 + (3.0 * GELU_A) * square))
    return values * half, slope


def normalize(values):
    centre = values - jnp.mean(values, axis=-1, keepdims=True)
    spread = lax.rsqrt(jnp.mean(centre * centre, axis=-1, keepdims=True) + EPSILON)
    return centre * spread, spread


def norm_back(upstream, unit, spread):
    return spread * (
        upstream
        - jnp.mean(upstream, axis=-1, keepdims=True)
        - unit * jnp.mean(upstream * unit, axis=-1, keepdims=True)
    )


def image_hot(image_col, count):
    lanes = lax.broadcasted_iota(jnp.int32, (image_col.shape[0], count), 1)
    return (image_col == lanes).astype(BF)


def probs_of(queries, keys, same):
    scores = dot(queries, keys, 1, 1) * (HEAD_DIM ** -0.5)
    scores = jnp.where(same, scores, NEG_FILL)
    raised = jnp.exp(scores - jnp.max(scores, axis=-1, keepdims=True))
    return raised * (1.0 / jnp.sum(raised, axis=-1, keepdims=True))


def attn_fwd_kernel(
    x_ref, img_ref, mod_ref, segc_ref, segr_ref, core_ref, *rest, shards, extras,
):
    w_in, rest = rest[:shards], rest[shards + extras:]
    n1_ref, qkv_ref, ctx_ref, attn_ref, mid_ref, n2_ref, w_ref, sems = rest
    step = pl.program_id(0)
    fetch_weights(w_in, w_ref, core_ref[0], sems)
    feat = ctx_ref.shape[2]
    images = mod_ref.shape[1]

    def mod(k):
        return dot(image_hot(img_ref[...], images), mod_ref[k])

    @pl.when(step == 0)
    def _():
        unit, _ = normalize(x_ref[...].astype(F32))
        n1_ref[...] = (unit * (1.0 + mod(1)) + mod(0)).astype(BF)
        attn_ref[...] = jnp.zeros_like(attn_ref)

    qkv = dot(n1_ref[...], w_ref[step, :, : 3 * feat]).astype(BF)
    qkv_ref[0] = qkv
    same = segc_ref[...] == segr_ref[...]
    parts = []
    for a in range(feat // HEAD_DIM):
        lo = a * HEAD_DIM
        probs = probs_of(qkv[:, lo:lo + HEAD_DIM], qkv[:, feat + lo:feat + lo + HEAD_DIM], same)
        parts.append(dot(probs.astype(BF), qkv[:, 2 * feat + lo:2 * feat + lo + HEAD_DIM]).astype(BF))
    context = jnp.concatenate(parts, axis=1)
    ctx_ref[0] = context
    attn_ref[...] += dot(context, w_ref[step, :, 3 * feat:], 1, 1)

    @pl.when(step == pl.num_programs(0) - 1)
    def _():
        mid = x_ref[...].astype(F32) + mod(2) * attn_ref[...]
        mid_ref[...] = mid
        unit, _ = normalize(mid)
        n2_ref[...] = (unit * (1.0 + mod(4)) + mod(3)).astype(BF)


def fixed(*shape):
    return pl.BlockSpec(shape, lambda m: (0,) * len(shape))


def stepped(*shape):
    return pl.BlockSpec((1,) + shape, lambda m: (m,) + (0,) * len(shape))


def attn_forward(core, x_rows, img_col, mod, seg_col, seg_row, weights, extras, parts):
    rows = x_rows.shape[0]
    feat = D // parts
    return pl.pallas_call(
        functools.partial(attn_fwd_kernel, shards=len(weights), extras=len(extras)),
        grid=(parts,),
        in_specs=[
            fixed(rows, D), fixed(rows, 1), fixed(*mod.shape), fixed(rows, 1), fixed(1, rows), smem(),
        ] + [hbm()] * (len(weights) + len(extras)),
        out_specs=[
            fixed(rows, D), stepped(rows, 3 * feat), stepped(rows, feat),
            fixed(rows, D), fixed(rows, D), fixed(rows, D),
        ],
        out_shape=[
            jax.ShapeDtypeStruct((rows, D), BF),
            jax.ShapeDtypeStruct((parts, rows, 3 * feat), BF),
            jax.ShapeDtypeStruct((parts, rows, feat), BF),
            jax.ShapeDtypeStruct((rows, D), F32),
            jax.ShapeDtypeStruct((rows, D), F32),
            jax.ShapeDtypeStruct((rows, D), BF),
        ],
        scratch_shapes=[pltpu.VMEM((parts, D, 4 * feat), BF), pltpu.SemaphoreType.DMA((len(weights),))],
        compiler_params=kernel_params(),
    )(x_rows, img_col, mod, seg_col, seg_row, core, *weights, *extras)


def image_sum(hot, values):
    high = values.astype(BF)
    rest = values - high.astype(F32)
    middle = rest.astype(BF)
    low = (rest - middle.astype(F32)).astype(BF)
    return dot(hot, high, 0, 0) + (dot(hot, middle, 0, 0) + dot(hot, low, 0, 0))


def attn_bwd_kernel(
    gn2_ref, mid_ref, attn_ref, go_ref, x_ref, n1_ref, qkv_ref, ctx_ref, img_ref, mod_ref,
    segc_ref, segr_ref, core_ref, *rest, shards,
):
    w_in, (gpatch_ref, gmod_ref), rest = rest[:shards], rest[shards:shards + 2], rest[shards + 2:]
    grad_refs, (gmid_ref, gattn_ref, gn1_ref, w_ref, sems) = rest[:-5], rest[-5:]
    step = pl.program_id(0)
    fetch_weights(w_in, w_ref, core_ref[0], sems)
    feat = ctx_ref.shape[2]
    images = mod_ref.shape[1]
    scale = HEAD_DIM ** -0.5

    def hot():
        return image_hot(img_ref[...], images)

    def mod(k):
        return dot(hot(), mod_ref[k])

    @pl.when(step == 0)
    def _():
        unit, spread = normalize(mid_ref[...])
        gn2 = gn2_ref[...]
        gmid = go_ref[...].astype(F32) + norm_back(gn2 * (1.0 + mod(4)), unit, spread)
        gmid_ref[...] = gmid
        gattn_ref[...] = (mod(2) * gmid).astype(BF)
        gmod_ref[2] = image_sum(hot(), gmid * attn_ref[...])
        gmod_ref[3] = image_sum(hot(), gn2)
        gmod_ref[4] = image_sum(hot(), gn2 * unit)
        gn1_ref[...] = jnp.zeros_like(gn1_ref)

    gattn = gattn_ref[...]
    gctx = dot(gattn, w_ref[step, :, 3 * feat:]).astype(BF)
    same = segc_ref[...] == segr_ref[...]
    gq, gk, gv = [], [], []
    for a in range(feat // HEAD_DIM):
        lo = a * HEAD_DIM
        queries = qkv_ref[0, :, lo:lo + HEAD_DIM]
        keys = qkv_ref[0, :, feat + lo:feat + lo + HEAD_DIM]
        values = qkv_ref[0, :, 2 * feat + lo:2 * feat + lo + HEAD_DIM]
        gc = gctx[:, lo:lo + HEAD_DIM]
        probs = probs_of(queries, keys, same)
        gv.append(dot(probs.astype(BF), gc, 0, 0).astype(BF))
        gp = dot(gc, values, 1, 1)
        inner = jnp.sum(probs * gp, axis=-1, keepdims=True)
        gs = (probs * (gp - inner)).astype(BF)
        gq.append((dot(gs, keys) * scale).astype(BF))
        gk.append((dot(gs, queries, 0, 0) * scale).astype(BF))
    grows = jnp.concatenate(gq + gk + gv, axis=1)
    store_rows(grad_refs, core_ref, dot(n1_ref[...], grows, 0, 0), slice(0, 3 * feat))
    store_rows(grad_refs, core_ref, dot(gattn, ctx_ref[0], 0, 0), slice(3 * feat, 4 * feat))
    gn1_ref[...] += dot(grows, w_ref[step, :, : 3 * feat], 1, 1)

    @pl.when(step == pl.num_programs(0) - 1)
    def _():
        unit, spread = normalize(x_ref[...].astype(F32))
        gn1 = gn1_ref[...]
        back = norm_back(gn1 * (1.0 + mod(1)), unit, spread)
        gpatch_ref[...] = (gmid_ref[...] + back).astype(BF)
        gmod_ref[0] = image_sum(hot(), gn1)
        gmod_ref[1] = image_sum(hot(), gn1 * unit)


def store_rows(refs, core_ref, values, cols):
    if len(refs) == 1:
        refs[0][0, :, cols] = values
        return
    mine, theirs = refs
    pieces, rows = mine.shape[1], mine.shape[2]
    for p in range(pieces):
        low = values[2 * p * rows:(2 * p + 1) * rows]
        high = values[(2 * p + 1) * rows:(2 * p + 2) * rows]
        mine[0, p ^ core_ref[1], :, cols] = jnp.where(core_ref[0] == 0, low, high)
        theirs[0, p ^ core_ref[1], :, cols] = jnp.where(core_ref[0] == 0, high, low)


def row_specs(parts, pieces, width, index):
    rows = D // (2 * pieces)
    if rows % 8:
        shape = (D, width)
        count = 1
    else:
        shape = (pieces, rows, width)
        count = 2
    spec = pl.BlockSpec((1,) + shape, lambda m: (index(m),) + (0,) * len(shape))
    return [spec] * count, [jax.ShapeDtypeStruct((parts,) + shape, F32)] * count


def smem():
    return pl.BlockSpec(memory_space=pltpu.SMEM)


def hbm():
    return pl.BlockSpec(memory_space=pl.ANY)


def fetch(refs, targets, sems):
    copies = [pltpu.make_async_copy(refs[i], targets[i], sems.at[i]) for i in range(len(refs))]
    for copy in copies:
        copy.start()
    for copy in copies:
        copy.wait()


def laid_out(refs, target):
    places, start = [], 0
    for ref in refs:
        places.append(target.at[pl.ds(start, ref.shape[0])])
        start += ref.shape[0]
    return places


def weight_copies(refs, w_ref, core, sems):
    half = D // 2
    mine = pl.multiple_of(core * half, half)
    theirs = pl.multiple_of((1 - core) * half, half)
    places = [(0, w_ref.at[0])]
    for base in (mine, theirs):
        for m in (1, 2):
            places.append((m, w_ref.at[m, pl.ds(base, half)]))
        for k in (0, 1):
            places.append((3, w_ref.at[3, pl.ds(pl.multiple_of(base + k * (half // 2), half // 2), half // 2)]))
    return [(m, pltpu.make_async_copy(ref, place, sems.at[i])) for i, (ref, (m, place)) in enumerate(zip(refs, places))]


def fetch_weights(refs, w_ref, core, sems):
    step = pl.program_id(0)
    copies = weight_copies(refs, w_ref, core, sems)

    @pl.when(step == 0)
    def _():
        for _, copy in copies:
            copy.start()

    for shard in range(w_ref.shape[0]):
        @pl.when(step == shard)
        def _():
            for m, copy in copies:
                if m == shard:
                    copy.wait()


def attn_backward(core, pieces, gn2, mid, attn, go, x_rows, n1, qkv, ctx, img_col, mod, seg_col, seg_row, weights):
    rows = x_rows.shape[0]
    parts = qkv.shape[0]
    feat = D // parts
    images = mod.shape[1]
    whole = fixed(rows, D)
    specs, shapes = row_specs(parts, pieces, 4 * feat, lambda m: m)
    return pl.pallas_call(
        functools.partial(attn_bwd_kernel, shards=len(weights)),
        grid=(parts,),
        in_specs=[
            whole, whole, whole, whole, whole, whole,
            stepped(rows, 3 * feat), stepped(rows, feat),
            fixed(rows, 1), fixed(*mod.shape), fixed(rows, 1), fixed(1, rows),
            smem(),
        ] + [hbm()] * len(weights),
        out_specs=[whole, fixed(5, images, D)] + specs,
        out_shape=[
            jax.ShapeDtypeStruct((rows, D), BF),
            jax.ShapeDtypeStruct((5, images, D), F32),
        ] + shapes,
        scratch_shapes=[
            pltpu.VMEM((rows, D), F32), pltpu.VMEM((rows, D), BF), pltpu.VMEM((rows, D), F32),
            pltpu.VMEM((parts, D, 4 * feat), BF), pltpu.SemaphoreType.DMA((len(weights),)),
        ],
        compiler_params=kernel_params(),
    )(gn2, mid, attn, go, x_rows, n1, qkv, ctx, img_col, mod, seg_col, seg_row, core, *weights)


def finish_kernel(mid_ref, mlp_ref, go_ref, img_ref, gate_ref, out_ref, gmod_ref):
    hot = image_hot(img_ref[...], gate_ref.shape[1])
    mlp = mlp_ref[...]
    out_ref[...] = (mid_ref[...] + dot(hot, gate_ref[0]) * mlp).astype(BF)
    gmod_ref[...] = image_sum(hot, go_ref[...].astype(F32) * mlp)


def gate_spec(mod):
    return pl.BlockSpec((1,) + mod.shape[1:], lambda m: (5, 0, 0))


def finish(mid, mlp, go, img_col, mod):
    rows = mid.shape[0]
    whole = fixed(rows, D)
    return pl.pallas_call(
        finish_kernel,
        grid=(1,),
        in_specs=[whole, whole, whole, fixed(rows, 1), gate_spec(mod)],
        out_specs=[whole, fixed(*mod.shape[1:])],
        out_shape=[
            jax.ShapeDtypeStruct(mid.shape, BF),
            jax.ShapeDtypeStruct(mod.shape[1:], F32),
        ],
        compiler_params=kernel_params(),
    )(mid, mlp, go, img_col, mod)


def tables_kernel(own_ref, far_ref, image_ref, ids_ref, row_ref, col_ref):
    core, me = ids_ref[0], ids_ref[2]
    tokens = own_ref.shape[1]
    parts = 4
    size = tokens // parts
    segs = image_ref.shape[1] // parts
    hots, gates, images, seg_rows = [], [], [], []
    for j, ref in enumerate((own_ref, far_ref)):
        tiles, pictures = [], []
        for m in range(parts):
            tile = ref[:, pl.ds(pl.multiple_of((me ^ m) * size, size), size)]
            seg = tile[4:5]
            image = jnp.zeros_like(seg)
            for k in range(segs):
                image = jnp.where(seg == float(k), image_ref[j, (me ^ m) * segs + k].astype(F32), image)
            tiles.append(tile)
            pictures.append(image)
        table = jnp.concatenate(tiles, axis=1)
        images.append(jnp.concatenate(pictures, axis=1))
        seg_rows.append(table[4:5])
        experts = (lax.broadcasted_iota(jnp.int32, (EXP_DEV, tokens), 0) + core * EXP_DEV).astype(F32)
        first, second = table[0:1] == experts, table[1:2] == experts
        hots.append(jnp.where(first | second, 1.0, 0.0))
        gates.append(jnp.where(first, table[2:3], jnp.where(second, table[3:4], 0.0)))
    hot = jnp.concatenate(hots, axis=0)
    before = lax.broadcasted_iota(jnp.int32, (tokens, tokens), 0) <= lax.broadcasted_iota(jnp.int32, (tokens, tokens), 1)
    slot = dot(hot.astype(BF), before.astype(BF))
    pos = jnp.where(hot > 0.5, slot - 1.0, -1.0)
    rest = jnp.concatenate(images + seg_rows + [jnp.zeros((4, tokens), F32)], axis=0)
    rows = jnp.concatenate([pos] + gates + [rest], axis=0)
    row_ref[...] = rows
    col_ref[...] = rows.T


def tables(own, far, images, ids):
    tokens = own.shape[1]
    return pl.pallas_call(
        tables_kernel,
        in_specs=[pl.BlockSpec(own.shape, lambda: (0, 0)), pl.BlockSpec(far.shape, lambda: (0, 0)), smem(), smem()],
        out_shape=[
            jax.ShapeDtypeStruct((24, tokens), F32),
            jax.ShapeDtypeStruct((tokens, 24), F32),
        ],
        compiler_params=kernel_params(),
    )(own, far, images, ids)


def store_split(ref, values):
    pieces, rows = ref.shape[0], ref.shape[2]
    for p in range(pieces):
        ref[p, 0] = values[p * rows:(p + 1) * rows].astype(ref.dtype)


def expert_one_kernel(row_ref, win_ref, mod_ref, gate_far_ref, *rest, tiles, first, kept):
    pieces_in, rest = rest[:tiles], rest[tiles + kept:]
    rows_ref, act_ref, slope_ref, gslot_ref, gw_ref, n2_ref, go_ref, gm_ref, sems = rest
    local = first + pl.program_id(0)
    tokens = n2_ref.shape[1]
    images = gm_ref.shape[1]
    each = tiles // 4

    @pl.when(pl.program_id(0) == 0)
    def _():
        targets = []
        for i, (ref, j) in enumerate(((n2_ref, 0), (n2_ref, 1), (go_ref, 0), (go_ref, 1))):
            targets += laid_out(pieces_in[i * each:(i + 1) * each], ref.at[j])
        sources = list(pieces_in) + [mod_ref.at[5], gate_far_ref]
        fetch(sources, targets + [gm_ref.at[0], gm_ref.at[1]], sems)

    def block(j, carry):
        where_ = row_ref[pl.ds(j * EXP_DEV + local, 1), :].astype(jnp.int32)
        mask = lax.broadcasted_iota(jnp.int32, (CAP, tokens), 0) == where_
        pick = mask.astype(BF)
        rows = dot(pick, n2_ref[j]).astype(BF)
        slots = pl.ds(pl.multiple_of(j * CAP, CAP), CAP)
        rows_ref[0, slots, :] = rows
        gates = row_ref[pl.ds(2 * EXP_DEV + j * EXP_DEV + local, 1), :]
        gate = jnp.sum(jnp.where(mask, gates, 0.0), axis=1, keepdims=True)
        image = jnp.sum(jnp.where(mask, row_ref[pl.ds(4 * EXP_DEV + j, 1), :], 0.0), axis=1, keepdims=True)
        hot = image_hot(image.astype(jnp.int32), images)
        grad = dot(hot, gm_ref[j]) * dot(pick, go_ref[j])
        gslot_ref[0, slots, :] = (gate * grad).astype(BF)
        value, slope = gelu_pair(dot(rows, win_ref[0]))
        act_ref[0, slots, :] = value.astype(BF)
        slope_ref[0, slots, :] = slope
        return carry

    lax.fori_loop(0, 2, block, 0)
    store_split(gw_ref, dot(gslot_ref[0], act_ref[0], 0, 0))


def expert_one(rows, mod, gate_far, w_in, tiles, pieces, first, kept):
    tokens = rows.shape[1]
    slots = 2 * CAP
    ff = w_in.shape[2]
    count = EXP_DEV // 2

    def shifted(*shape):
        return pl.BlockSpec((1,) + shape, lambda m: (m + first,) + (0,) * len(shape))

    fixed_ins = 4
    return pl.pallas_call(
        functools.partial(expert_one_kernel, tiles=len(tiles), first=first, kept=len(kept)),
        grid=(count,),
        in_specs=[fixed(*rows.shape), shifted(D, ff)] + [hbm()] * (2 + len(tiles) + len(kept)),
        out_specs=[
            shifted(slots, D), shifted(slots, ff), shifted(slots, ff), shifted(slots, D),
            pl.BlockSpec((pieces, 1, D // pieces, ff), lambda m: (0, m, 0, 0)),
        ],
        out_shape=[
            jax.ShapeDtypeStruct((EXP_DEV, slots, D), BF),
            jax.ShapeDtypeStruct((EXP_DEV, slots, ff), BF),
            jax.ShapeDtypeStruct((EXP_DEV, slots, ff), F32),
            jax.ShapeDtypeStruct((EXP_DEV, slots, D), BF),
            jax.ShapeDtypeStruct((pieces, count, D // pieces, ff), BF),
        ],
        scratch_shapes=[
            pltpu.VMEM((2, tokens, D), BF), pltpu.VMEM((2, tokens, D), BF), pltpu.VMEM((2,) + mod.shape[1:], BF),
            pltpu.SemaphoreType.DMA((len(tiles) + 2,)),
        ],
        input_output_aliases={fixed_ins + len(tiles) + i: i for i in range(len(kept))},
        compiler_params=kernel_params(),
    )(rows, w_in, mod, gate_far, *tiles, *kept)


def picked(col_ref, j, local):
    lanes = lax.broadcasted_iota(jnp.int32, col_ref.shape, 1)
    place = jnp.sum(jnp.where(lanes == j * EXP_DEV + local, col_ref[...], 0.0), axis=1, keepdims=True)
    slots = lax.broadcasted_iota(jnp.int32, (col_ref.shape[0], CAP), 1)
    return (slots == place.astype(jnp.int32)).astype(BF)


def expert_two_kernel(
    col_ref, rows_ref, slope_ref, gslot_ref, win_ref, wout_ref,
    gw_ref, gn_ref, gn_far_ref, gpre_ref, gn_acc,
):
    local = pl.program_id(0)

    @pl.when(local == 0)
    def _():
        gn_ref[...] = jnp.zeros_like(gn_ref)
        gn_acc[...] = jnp.zeros_like(gn_acc)

    for j, total in enumerate((gn_ref, gn_acc)):
        slots = slice(j * CAP, (j + 1) * CAP)
        grad_pre = (slope_ref[0, slots, :] * dot(gslot_ref[0, slots, :], wout_ref[0], 1, 1)).astype(BF)
        gpre_ref[slots, :] = grad_pre
        grad_in = dot(grad_pre, win_ref[0], 1, 1).astype(BF)
        total[...] += dot(picked(col_ref, j, local), grad_in)
    store_split(gw_ref, dot(rows_ref[0], gpre_ref[...], 0, 0))

    @pl.when(local == pl.num_programs(0) - 1)
    def _():
        gn_far_ref[...] = gn_acc[...].astype(BF)


def expert_two(cols, rows, slope, gslot, w_in, w_out, pieces):
    tokens = cols.shape[0]
    slots = 2 * CAP
    ff = w_in.shape[2]
    whole = fixed(tokens, D)
    return pl.pallas_call(
        expert_two_kernel,
        grid=(EXP_DEV,),
        in_specs=[
            fixed(*cols.shape), stepped(slots, D), stepped(slots, ff), stepped(slots, D),
            stepped(D, ff), stepped(ff, D),
        ],
        out_specs=[pl.BlockSpec((pieces, 1, D // pieces, ff), lambda m: (0, m, 0, 0)), whole, whole],
        out_shape=[
            jax.ShapeDtypeStruct((pieces, EXP_DEV, D // pieces, ff), BF),
            jax.ShapeDtypeStruct((tokens, D), F32),
            jax.ShapeDtypeStruct((tokens, D), BF),
        ],
        scratch_shapes=[pltpu.VMEM((slots, ff), BF), pltpu.VMEM((tokens, D), F32)],
        compiler_params=kernel_params(),
    )(cols, rows, slope, gslot, w_in, w_out)


def expert_mix_kernel(col_ref, act_ref, wout_ref, mix_ref, mix_far_ref, mix_acc):
    local = pl.program_id(0)
    lanes = lax.broadcasted_iota(jnp.int32, col_ref.shape, 1)

    @pl.when(local == 0)
    def _():
        mix_ref[...] = jnp.zeros_like(mix_ref)
        mix_acc[...] = jnp.zeros_like(mix_acc)

    for j, total in enumerate((mix_ref, mix_acc)):
        result = dot(act_ref[0, j * CAP:(j + 1) * CAP, :], wout_ref[0]).astype(BF)
        here = lanes == 2 * EXP_DEV + j * EXP_DEV + local
        gate = jnp.sum(jnp.where(here, col_ref[...], 0.0), axis=1, keepdims=True)
        total[...] += gate * dot(picked(col_ref, j, local), result)

    @pl.when(local == pl.num_programs(0) - 1)
    def _():
        mix_far_ref[...] = mix_acc[...].astype(BF)


def expert_mix(cols, act, w_out):
    tokens = cols.shape[0]
    ff = w_out.shape[1]
    whole = fixed(tokens, D)
    return pl.pallas_call(
        expert_mix_kernel,
        grid=(EXP_DEV,),
        in_specs=[fixed(*cols.shape), stepped(2 * CAP, ff), stepped(ff, D)],
        out_specs=[whole, whole],
        out_shape=[jax.ShapeDtypeStruct((tokens, D), F32), jax.ShapeDtypeStruct((tokens, D), BF)],
        scratch_shapes=[pltpu.VMEM((tokens, D), F32)],
        compiler_params=kernel_params(),
    )(cols, act, w_out)


def shared_kernel(img_ref, gm_ref, win_ref, wout_ref, core_ref, *rest, tiles):
    pieces_in, out_ref, gn_ref = rest[:tiles], rest[tiles + 1], rest[tiles + 2]
    gw_refs, rest = rest[tiles + 3:-6], rest[-6:]
    n2_ref, go_ref, act_ref, gs_ref, gpre_ref, sems = rest
    step = pl.program_id(0)
    ff = win_ref.shape[1]
    rows = out_ref.shape[0]
    here = pl.ds(pl.multiple_of(step * rows, rows), rows)

    @pl.when(step == 0)
    def _():
        each = tiles // 2
        fetch(pieces_in, laid_out(pieces_in[:each], n2_ref) + laid_out(pieces_in[each:], go_ref), sems)

    value, slope = gelu_pair(dot(n2_ref[here, :], win_ref[...]))
    act = value.astype(BF)
    act_ref[here, :] = act
    out_ref[...] = dot(act, wout_ref[...])
    gate = dot(image_hot(img_ref[...], gm_ref.shape[1]), gm_ref[0])
    grad = (gate * go_ref[here, :].astype(F32)).astype(BF)
    gs_ref[here, :] = grad
    gpre = (slope * dot(grad, wout_ref[...], 1, 1)).astype(BF)
    gpre_ref[here, :] = gpre
    gn_ref[...] = dot(gpre, win_ref[...], 1, 1)

    @pl.when(step == pl.num_programs(0) - 1)
    def _():
        store_rows(gw_refs, core_ref, dot(n2_ref[...], gpre_ref[...], 0, 0), slice(0, ff))
        store_rows(gw_refs, core_ref, dot(gs_ref[...], act_ref[...], 0, 0), slice(ff, 2 * ff))


def shared_both(core, pieces, tiles, img_col, mod, w_in, w_out, after):
    rows = tiles[0].shape[0]
    tokens = img_col.shape[0]
    steps = tokens // rows
    ff = w_in.shape[1]
    moving = pl.BlockSpec((rows, D), lambda m: (m, 0))
    specs, shapes = row_specs(1, pieces, 2 * ff, lambda m: 0)
    return pl.pallas_call(
        functools.partial(shared_kernel, tiles=len(tiles)),
        grid=(steps,),
        in_specs=[
            pl.BlockSpec((rows, 1), lambda m: (m, 0)),
            gate_spec(mod), fixed(D, ff), fixed(ff, D), smem(),
        ] + [hbm()] * (len(tiles) + 1),
        out_specs=[moving, moving] + specs,
        out_shape=[
            jax.ShapeDtypeStruct((tokens, D), F32),
            jax.ShapeDtypeStruct((tokens, D), F32),
        ] + shapes,
        scratch_shapes=[
            pltpu.VMEM((tokens, D), BF), pltpu.VMEM((tokens, D), BF),
            pltpu.VMEM((tokens, ff), BF), pltpu.VMEM((tokens, D), BF), pltpu.VMEM((tokens, ff), BF),
            pltpu.SemaphoreType.DMA((len(tiles),)),
        ],
        compiler_params=kernel_params(),
    )(img_col, mod, w_in, w_out, core, *tiles, after)


def block(
    patches, cond, seg_ids, seg_image, routes, gates, grad_out,
    w_ada, w_qkv, w_out, w_shared_in, w_shared_out, w_expert_in, w_expert_out,
):
    tokens, feat = patches.shape
    parts = D // feat
    rows = tokens // parts
    pieces = lax.axis_size(DP)
    me = lax.axis_index(HID)
    core = lax.axis_index(EXP)
    bit_low = (me & 1) == 1
    bit_high = (me & 2) == 2

    def turned(items):
        a, b, c, d = items
        a, b = jnp.where(bit_low, b, a), jnp.where(bit_low, a, b)
        c, d = jnp.where(bit_low, d, c), jnp.where(bit_low, c, d)
        return [
            jnp.where(bit_high, c, a), jnp.where(bit_high, d, b),
            jnp.where(bit_high, a, c), jnp.where(bit_high, b, d),
        ]

    def across(value, mask):
        return lax.ppermute(value, HID, [(i, i ^ mask) for i in range(parts)])

    def other_core(value):
        return lax.ppermute(value, EXP, [(0, 1), (1, 0)])

    def exchanged(items):
        return [items[0]] + [across(items[m], m) for m in range(1, parts)]

    def gathered(value):
        return [value] + [across(value, m) for m in range(1, parts)]

    def passed_on(value):
        one, two = across(value, 1), across(value, 2)
        cut = value.shape[0] // 2
        return [one, two, across(one[:cut], 2), across(two[cut:], 1)]

    def blocks(value):
        return [value[i * rows:(i + 1) * rows] for i in range(parts)]

    def to_cols(value):
        cuts = [value[:, i * feat:(i + 1) * feat] for i in range(parts)]
        return jnp.concatenate(turned(exchanged(turned(cuts))), axis=0)

    packed = jnp.concatenate([w_qkv.reshape(D, 3 * feat), w_out.T], axis=1)
    half = lax.dynamic_slice_in_dim(packed, core * (D // 2), D // 2, axis=0)
    halves = passed_on(half)
    weights = [packed] + halves + [other_core(part) for part in halves]
    flip = lax.axis_index(DP) if pieces == 4 else jnp.zeros((), jnp.int32)
    core_id = jnp.stack([core, flip, me]).astype(jnp.int32)

    def both_rows(left, right):
        cuts = exchanged(turned(blocks(jnp.concatenate([left, right], axis=1))))
        cuts = turned(cuts)
        return [jnp.concatenate([cut[:, i * feat:(i + 1) * feat] for cut in cuts], axis=1) for i in range(2)]

    x_rows, go_rows = both_rows(patches, grad_out)
    silu_cond = jax.nn.silu(cond.astype(F32)).astype(BF)
    mod_own = jnp.einsum("id,dkc->kic", silu_cond, w_ada, preferred_element_type=F32).astype(BF)
    mod = jnp.concatenate(turned(gathered(mod_own)), axis=2)
    go_own = [go_rows] + passed_on(go_rows)
    gate_far = other_core(mod[5])
    go_far = [other_core(tile) for tile in go_own]

    images_flat = seg_image.reshape(1, -1).astype(F32)
    raw = jnp.concatenate(
        [
            routes.T.astype(F32), gates.T, seg_ids.reshape(1, tokens).astype(F32),
            jnp.pad(images_flat, ((0, 0), (0, tokens - images_flat.shape[1]))),
        ],
        axis=0,
    )
    raw_far = other_core(raw)
    image_ids = jnp.concatenate([images_flat, raw_far[5:, : images_flat.shape[1]]], axis=0).astype(jnp.int32)
    table_rows, table_cols = tables(raw, raw_far, image_ids, core_id)
    img_col = table_cols[:, 16:17].astype(jnp.int32)
    seg_col = table_cols[:, 18:19]
    seg_row = table_rows[18:19]

    ada_rows = D // (2 * pieces)
    place = lax.axis_index(DP) * 2 + core

    def everyone(value):
        if pieces > 8 or pieces & (pieces - 1):
            return lax.all_gather(value, (DP, EXP), axis=0, tiled=False)
        own = [value]
        for m in range(1, pieces):
            own.append(lax.ppermute(value, DP, [(i, i ^ m) for i in range(pieces)]))
        own = jnp.stack(own)
        return jnp.concatenate([own, other_core(own)], axis=0)

    n1, qkv, ctx, attn, mid, n2 = attn_forward(
        core_id, x_rows, img_col, mod, seg_col, seg_row, weights, [], parts,
    )
    n2_own = [n2] + passed_on(n2)
    n2_far = [other_core(tile) for tile in n2_own]
    tiles = n2_own + n2_far + go_own + go_far
    *kept, gw_out_low = expert_one(table_rows, mod, gate_far, w_expert_in, tiles, pieces, 0, [])
    shared_out, gn_shared, *gw_shared = shared_both(
        core_id, pieces, n2_own + go_own, img_col, mod, w_shared_in, w_shared_out, gw_out_low
    )

    def core_half(parts_of):
        if len(parts_of) == 1:
            values = parts_of[0]
            cut = values.reshape(values.shape[0], pieces, 2, D // (2 * pieces), values.shape[2])
            low, high = cut[:, :, 0], cut[:, :, 1]
            parts_of = jnp.where(core == 0, low, high), jnp.where(core == 0, high, low)
        return parts_of[0] + other_core(parts_of[1])

    def over_dp(values):
        return lax.psum_scatter(values, DP, scatter_dimension=0, tiled=False).astype(F32)

    def pieces_over_dp(values):
        if pieces != 4:
            return over_dp(values.astype(BF))
        total = values[0]
        for m in range(1, pieces):
            moved = lax.ppermute(values[m].astype(BF), DP, [(i, i ^ m) for i in range(pieces)])
            total = total + moved.astype(F32)
        return total

    half_shared = core_half(gw_shared)[0]
    grad_shared = pieces_over_dp(half_shared)

    ge_out_low = over_dp(gw_out_low)
    *kept, gw_out_high = expert_one(
        table_rows, mod, gate_far, w_expert_in, tiles, pieces, EXP_DEV // 2, kept
    )
    ge_out_high = over_dp(gw_out_high)
    slot_rows, act, slope, gslot = kept
    gw_in, gn_near, gn_far = expert_two(table_cols, slot_rows, slope, gslot, w_expert_in, w_expert_out, pieces)
    grad_expert_in = over_dp(gw_in)
    mix_near, mix_far = expert_mix(table_cols, act, w_expert_out)

    def row_total(near, far, extra):
        from_core = other_core(far).astype(F32)
        cut = blocks(near + extra + from_core)
        out = cut[0]
        for m in range(1, parts):
            moved = across(cut[m].astype(BF), m)
            out = out + moved.astype(F32)
        return out

    gn2 = row_total(gn_near, gn_far, gn_shared)
    mlp = row_total(mix_near, mix_far, shared_out)

    gpatch, gmod_five, *gw_attn = attn_backward(
        core_id, pieces, gn2, mid, attn, go_rows, x_rows, n1, qkv, ctx, img_col, mod, seg_col, seg_row, weights
    )
    out_rows, gmod_last = finish(mid, mlp, go_rows, img_col, mod)
    block_out = to_cols(out_rows)
    grad_patches = to_cols(gpatch)

    gmod = jnp.concatenate([gmod_five, gmod_last[None]], axis=0)
    cuts = turned([gmod[:, :, i * feat:(i + 1) * feat] for i in range(parts)])
    got = exchanged(cuts)
    grad_image = (got[0] + got[1] + got[2] + got[3]).astype(BF)
    image_all = everyone(grad_image)
    silu_all = everyone(silu_cond)
    silu_mine = lax.dynamic_slice_in_dim(silu_all, place * ada_rows, ada_rows, axis=2)
    grad_ada = jnp.einsum("gid,gkic->dkc", silu_mine, image_all, preferred_element_type=F32)

    attn_half = core_half(gw_attn)
    attn_sum = attn_half[0]
    for m in range(1, parts):
        moved = across(attn_half[m].astype(BF), m)
        attn_sum = attn_sum + moved.astype(F32)
    grad_attn = pieces_over_dp(attn_sum)
    ff = w_shared_in.shape[1]
    return (
        block_out,
        grad_patches,
        grad_ada,
        grad_attn[:, : 3 * feat].reshape(ada_rows, 3, feat),
        grad_attn[:, 3 * feat:].T,
        grad_shared[:, :ff],
        grad_shared[:, ff:].T,
        grad_expert_in,
        jnp.swapaxes(jnp.concatenate([ge_out_low, ge_out_high], axis=0), 1, 2),
    )


def solution(mesh):
    rows = P((DP, EXP), None)
    tiles = P((DP, EXP), HID)
    return jax.shard_map(
        block,
        mesh=mesh,
        in_specs=(
            tiles, rows, rows, rows, rows, rows, tiles,
            P(None, None, HID),
            P(None, None, HID),
            P(HID, None),
            P(None, HID),
            P(HID, None),
            P(EXP, None, HID),
            P(EXP, HID, None),
        ),
        out_specs=(
            tiles,
            tiles,
            P((DP, EXP), None, HID),
            P((DP, EXP), None, HID),
            P(HID, (DP, EXP)),
            P((DP, EXP), HID),
            P(HID, (DP, EXP)),
            P(EXP, DP, HID),
            P(EXP, HID, DP),
        ),
        check_vma=False,
    )
```

```python
import functools

import jax
import jax.numpy as jnp
from jax import lax
from jax.experimental import pallas as pl
from jax.experimental.pallas import tpu as pltpu
from jax.sharding import PartitionSpec as P


D = 768
HEAD_DIM = 64
EXP_DEV = 4
CAP = 384
EPSILON = 1e-06
NEG_FILL = -1e30
DP, EXP, HID = "dp", "expert", "hidden"
BF = jnp.bfloat16
F32 = jnp.float32
GELU_C = 0.7978845608028654
GELU_A = 0.044715


def kernel_params():
    return pltpu.CompilerParams(vmem_limit_bytes=60 * 1024 * 1024)


def dot(a, b, lhs=1, rhs=0):
    return lax.dot_general(a, b, (((lhs,), (rhs,)), ((), ())), preferred_element_type=F32)


def gelu_pair(values):
    square = values * values
    inner = GELU_C * values * (1.0 + GELU_A * square)
    bent = jnp.tanh(inner)
    half = 0.5 * (1.0 + bent)
    slope = half + (0.5 * values) * (1.0 - bent * bent) * (GELU_C * (1.0 + (3.0 * GELU_A) * square))
    return values * half, slope


def normalize(values):
    centre = values - jnp.mean(values, axis=-1, keepdims=True)
    spread = lax.rsqrt(jnp.mean(centre * centre, axis=-1, keepdims=True) + EPSILON)
    return centre * spread, spread


def norm_back(upstream, unit, spread):
    return spread * (
        upstream
        - jnp.mean(upstream, axis=-1, keepdims=True)
        - unit * jnp.mean(upstream * unit, axis=-1, keepdims=True)
    )


def image_hot(image_col, count):
    lanes = lax.broadcasted_iota(jnp.int32, (image_col.shape[0], count), 1)
    return (image_col == lanes).astype(BF)


def probs_of(queries, keys, same):
    scores = dot(queries, keys, 1, 1) * (HEAD_DIM ** -0.5)
    scores = jnp.where(same, scores, NEG_FILL)
    raised = jnp.exp(scores - jnp.max(scores, axis=-1, keepdims=True))
    return raised * (1.0 / jnp.sum(raised, axis=-1, keepdims=True))


def attn_fwd_kernel(
    x_ref, img_ref, mod_ref, segc_ref, segr_ref, core_ref, *rest, shards, extras,
):
    w_in, rest = rest[:shards], rest[shards + extras:]
    n1_ref, qkv_ref, ctx_ref, attn_ref, mid_ref, n2_ref, w_ref, sems = rest
    step = pl.program_id(0)
    fetch_weights(w_in, w_ref, core_ref[0], sems)
    feat = ctx_ref.shape[2]
    images = mod_ref.shape[1]

    def mod(k):
        return dot(image_hot(img_ref[...], images), mod_ref[k])

    @pl.when(step == 0)
    def _():
        unit, _ = normalize(x_ref[...].astype(F32))
        n1_ref[...] = (unit * (1.0 + mod(1)) + mod(0)).astype(BF)
        attn_ref[...] = jnp.zeros_like(attn_ref)

    qkv = dot(n1_ref[...], w_ref[step, :, : 3 * feat]).astype(BF)
    qkv_ref[0] = qkv
    same = segc_ref[...] == segr_ref[...]
    parts = []
    for a in range(feat // HEAD_DIM):
        lo = a * HEAD_DIM
        probs = probs_of(qkv[:, lo:lo + HEAD_DIM], qkv[:, feat + lo:feat + lo + HEAD_DIM], same)
        parts.append(dot(probs.astype(BF), qkv[:, 2 * feat + lo:2 * feat + lo + HEAD_DIM]).astype(BF))
    context = jnp.concatenate(parts, axis=1)
    ctx_ref[0] = context
    attn_ref[...] += dot(context, w_ref[step, :, 3 * feat:], 1, 1)

    @pl.when(step == pl.num_programs(0) - 1)
    def _():
        mid = x_ref[...].astype(F32) + mod(2) * attn_ref[...]
        mid_ref[...] = mid
        unit, _ = normalize(mid)
        n2_ref[...] = (unit * (1.0 + mod(4)) + mod(3)).astype(BF)


def fixed(*shape):
    return pl.BlockSpec(shape, lambda m: (0,) * len(shape))


def stepped(*shape):
    return pl.BlockSpec((1,) + shape, lambda m: (m,) + (0,) * len(shape))


def attn_forward(core, x_rows, img_col, mod, seg_col, seg_row, weights, extras, parts):
    rows = x_rows.shape[0]
    feat = D // parts
    return pl.pallas_call(
        functools.partial(attn_fwd_kernel, shards=len(weights), extras=len(extras)),
        grid=(parts,),
        in_specs=[
            fixed(rows, D), fixed(rows, 1), fixed(*mod.shape), fixed(rows, 1), fixed(1, rows), smem(),
        ] + [hbm()] * (len(weights) + len(extras)),
        out_specs=[
            fixed(rows, D), stepped(rows, 3 * feat), stepped(rows, feat),
            fixed(rows, D), fixed(rows, D), fixed(rows, D),
        ],
        out_shape=[
            jax.ShapeDtypeStruct((rows, D), BF),
            jax.ShapeDtypeStruct((parts, rows, 3 * feat), BF),
            jax.ShapeDtypeStruct((parts, rows, feat), BF),
            jax.ShapeDtypeStruct((rows, D), F32),
            jax.ShapeDtypeStruct((rows, D), F32),
            jax.ShapeDtypeStruct((rows, D), BF),
        ],
        scratch_shapes=[pltpu.VMEM((parts, D, 4 * feat), BF), pltpu.SemaphoreType.DMA((len(weights),))],
        compiler_params=kernel_params(),
    )(x_rows, img_col, mod, seg_col, seg_row, core, *weights, *extras)


def image_sum(hot, values):
    high = values.astype(BF)
    rest = values - high.astype(F32)
    middle = rest.astype(BF)
    low = (rest - middle.astype(F32)).astype(BF)
    return dot(hot, high, 0, 0) + (dot(hot, middle, 0, 0) + dot(hot, low, 0, 0))


def attn_bwd_kernel(
    gn2_ref, mid_ref, attn_ref, go_ref, x_ref, n1_ref, qkv_ref, ctx_ref, img_ref, mod_ref,
    segc_ref, segr_ref, core_ref, *rest, shards,
):
    w_in, (gpatch_ref, gmod_ref), rest = rest[:shards], rest[shards:shards + 2], rest[shards + 2:]
    grad_refs, (gmid_ref, gattn_ref, gn1_ref, w_ref, sems) = rest[:-5], rest[-5:]
    step = pl.program_id(0)
    fetch_weights(w_in, w_ref, core_ref[0], sems)
    feat = ctx_ref.shape[2]
    images = mod_ref.shape[1]
    scale = HEAD_DIM ** -0.5

    def hot():
        return image_hot(img_ref[...], images)

    def mod(k):
        return dot(hot(), mod_ref[k])

    @pl.when(step == 0)
    def _():
        unit, spread = normalize(mid_ref[...])
        gn2 = gn2_ref[...]
        gmid = go_ref[...].astype(F32) + norm_back(gn2 * (1.0 + mod(4)), unit, spread)
        gmid_ref[...] = gmid
        gattn_ref[...] = (mod(2) * gmid).astype(BF)
        gmod_ref[2] = image_sum(hot(), gmid * attn_ref[...])
        gmod_ref[3] = image_sum(hot(), gn2)
        gmod_ref[4] = image_sum(hot(), gn2 * unit)
        gn1_ref[...] = jnp.zeros_like(gn1_ref)

    gattn = gattn_ref[...]
    gctx = dot(gattn, w_ref[step, :, 3 * feat:]).astype(BF)
    same = segc_ref[...] == segr_ref[...]
    gq, gk, gv = [], [], []
    for a in range(feat // HEAD_DIM):
        lo = a * HEAD_DIM
        queries = qkv_ref[0, :, lo:lo + HEAD_DIM]
        keys = qkv_ref[0, :, feat + lo:feat + lo + HEAD_DIM]
        values = qkv_ref[0, :, 2 * feat + lo:2 * feat + lo + HEAD_DIM]
        gc = gctx[:, lo:lo + HEAD_DIM]
        probs = probs_of(queries, keys, same)
        gv.append(dot(probs.astype(BF), gc, 0, 0).astype(BF))
        gp = dot(gc, values, 1, 1)
        inner = jnp.sum(probs * gp, axis=-1, keepdims=True)
        gs = (probs * (gp - inner)).astype(BF)
        gq.append((dot(gs, keys) * scale).astype(BF))
        gk.append((dot(gs, queries, 0, 0) * scale).astype(BF))
    grows = jnp.concatenate(gq + gk + gv, axis=1)
    store_rows(grad_refs, core_ref, dot(n1_ref[...], grows, 0, 0), slice(0, 3 * feat))
    store_rows(grad_refs, core_ref, dot(gattn, ctx_ref[0], 0, 0), slice(3 * feat, 4 * feat))
    gn1_ref[...] += dot(grows, w_ref[step, :, : 3 * feat], 1, 1)

    @pl.when(step == pl.num_programs(0) - 1)
    def _():
        unit, spread = normalize(x_ref[...].astype(F32))
        gn1 = gn1_ref[...]
        back = norm_back(gn1 * (1.0 + mod(1)), unit, spread)
        gpatch_ref[...] = (gmid_ref[...] + back).astype(BF)
        gmod_ref[0] = image_sum(hot(), gn1)
        gmod_ref[1] = image_sum(hot(), gn1 * unit)


def store_rows(refs, core_ref, values, cols):
    if len(refs) == 1:
        refs[0][0, :, cols] = values
        return
    mine, theirs = refs
    pieces, rows = mine.shape[1], mine.shape[2]
    for p in range(pieces):
        low = values[2 * p * rows:(2 * p + 1) * rows]
        high = values[(2 * p + 1) * rows:(2 * p + 2) * rows]
        mine[0, p ^ core_ref[1], :, cols] = jnp.where(core_ref[0] == 0, low, high)
        theirs[0, p ^ core_ref[1], :, cols] = jnp.where(core_ref[0] == 0, high, low).astype(theirs.dtype)


def row_specs(parts, pieces, width, index, away):
    rows = D // (2 * pieces)
    if rows % 8:
        shape = (D, width)
        count = 1
    else:
        shape = (pieces, rows, width)
        count = 2
    spec = pl.BlockSpec((1,) + shape, lambda m: (index(m),) + (0,) * len(shape))
    return [spec] * count, [jax.ShapeDtypeStruct((parts,) + shape, kind) for kind in (F32, away)[:count]]


def smem():
    return pl.BlockSpec(memory_space=pltpu.SMEM)


def hbm():
    return pl.BlockSpec(memory_space=pl.ANY)


def fetch(refs, targets, sems):
    copies = [pltpu.make_async_copy(refs[i], targets[i], sems.at[i]) for i in range(len(refs))]
    for copy in copies:
        copy.start()
    for copy in copies:
        copy.wait()


def laid_out(refs, target):
    places, start = [], 0
    for ref in refs:
        places.append(target.at[pl.ds(start, ref.shape[0])])
        start += ref.shape[0]
    return places


def weight_copies(refs, w_ref, core, sems):
    half = D // 2
    mine = pl.multiple_of(core * half, half)
    theirs = pl.multiple_of((1 - core) * half, half)
    places = [(0, w_ref.at[0])]
    for base in (mine, theirs):
        for m in (1, 2):
            places.append((m, w_ref.at[m, pl.ds(base, half)]))
        for k in (0, 1):
            places.append((3, w_ref.at[3, pl.ds(pl.multiple_of(base + k * (half // 2), half // 2), half // 2)]))
    return [(m, pltpu.make_async_copy(ref, place, sems.at[i])) for i, (ref, (m, place)) in enumerate(zip(refs, places))]


def fetch_weights(refs, w_ref, core, sems):
    step = pl.program_id(0)
    copies = weight_copies(refs, w_ref, core, sems)

    @pl.when(step == 0)
    def _():
        for _, copy in copies:
            copy.start()

    for shard in range(w_ref.shape[0]):
        @pl.when(step == shard)
        def _():
            for m, copy in copies:
                if m == shard:
                    copy.wait()


def attn_backward(core, pieces, gn2, mid, attn, go, x_rows, n1, qkv, ctx, img_col, mod, seg_col, seg_row, weights):
    rows = x_rows.shape[0]
    parts = qkv.shape[0]
    feat = D // parts
    images = mod.shape[1]
    whole = fixed(rows, D)
    specs, shapes = row_specs(parts, pieces, 4 * feat, lambda m: m, BF)
    return pl.pallas_call(
        functools.partial(attn_bwd_kernel, shards=len(weights)),
        grid=(parts,),
        in_specs=[
            whole, whole, whole, whole, whole, whole,
            stepped(rows, 3 * feat), stepped(rows, feat),
            fixed(rows, 1), fixed(*mod.shape), fixed(rows, 1), fixed(1, rows),
            smem(),
        ] + [hbm()] * len(weights),
        out_specs=[whole, fixed(5, images, D)] + specs,
        out_shape=[
            jax.ShapeDtypeStruct((rows, D), BF),
            jax.ShapeDtypeStruct((5, images, D), F32),
        ] + shapes,
        scratch_shapes=[
            pltpu.VMEM((rows, D), F32), pltpu.VMEM((rows, D), BF), pltpu.VMEM((rows, D), F32),
            pltpu.VMEM((parts, D, 4 * feat), BF), pltpu.SemaphoreType.DMA((len(weights),)),
        ],
        compiler_params=kernel_params(),
    )(gn2, mid, attn, go, x_rows, n1, qkv, ctx, img_col, mod, seg_col, seg_row, core, *weights)


def finish_kernel(mid_ref, mlp_ref, go_ref, img_ref, gate_ref, out_ref, gmod_ref):
    hot = image_hot(img_ref[...], gate_ref.shape[1])
    mlp = mlp_ref[...]
    out_ref[...] = (mid_ref[...] + dot(hot, gate_ref[0]) * mlp).astype(BF)
    gmod_ref[...] = image_sum(hot, go_ref[...].astype(F32) * mlp)


def gate_spec(mod):
    return pl.BlockSpec((1,) + mod.shape[1:], lambda m: (5, 0, 0))


def finish(mid, mlp, go, img_col, mod):
    rows = mid.shape[0]
    whole = fixed(rows, D)
    return pl.pallas_call(
        finish_kernel,
        grid=(1,),
        in_specs=[whole, whole, whole, fixed(rows, 1), gate_spec(mod)],
        out_specs=[whole, fixed(*mod.shape[1:])],
        out_shape=[
            jax.ShapeDtypeStruct(mid.shape, BF),
            jax.ShapeDtypeStruct(mod.shape[1:], F32),
        ],
        compiler_params=kernel_params(),
    )(mid, mlp, go, img_col, mod)


def tables_kernel(own_ref, far_ref, image_ref, ids_ref, row_ref, col_ref):
    core, me = ids_ref[0], ids_ref[2]
    tokens = own_ref.shape[1]
    parts = 4
    size = tokens // parts
    segs = image_ref.shape[1] // parts
    hots, gates, images, seg_rows = [], [], [], []
    for j, ref in enumerate((own_ref, far_ref)):
        tiles, pictures = [], []
        for m in range(parts):
            tile = ref[:, pl.ds(pl.multiple_of((me ^ m) * size, size), size)]
            seg = tile[4:5]
            image = jnp.zeros_like(seg)
            for k in range(segs):
                image = jnp.where(seg == float(k), image_ref[j, (me ^ m) * segs + k].astype(F32), image)
            tiles.append(tile)
            pictures.append(image)
        table = jnp.concatenate(tiles, axis=1)
        images.append(jnp.concatenate(pictures, axis=1))
        seg_rows.append(table[4:5])
        experts = (lax.broadcasted_iota(jnp.int32, (EXP_DEV, tokens), 0) + core * EXP_DEV).astype(F32)
        first, second = table[0:1] == experts, table[1:2] == experts
        hots.append(jnp.where(first | second, 1.0, 0.0))
        gates.append(jnp.where(first, table[2:3], jnp.where(second, table[3:4], 0.0)))
    hot = jnp.concatenate(hots, axis=0)
    before = lax.broadcasted_iota(jnp.int32, (tokens, tokens), 0) <= lax.broadcasted_iota(jnp.int32, (tokens, tokens), 1)
    slot = dot(hot.astype(BF), before.astype(BF))
    pos = jnp.where(hot > 0.5, slot - 1.0, -1.0)
    rest = jnp.concatenate(images + seg_rows + [jnp.zeros((4, tokens), F32)], axis=0)
    rows = jnp.concatenate([pos] + gates + [rest], axis=0)
    row_ref[...] = rows
    col_ref[...] = rows.T


def tables(own, far, images, ids):
    tokens = own.shape[1]
    return pl.pallas_call(
        tables_kernel,
        in_specs=[pl.BlockSpec(own.shape, lambda: (0, 0)), pl.BlockSpec(far.shape, lambda: (0, 0)), smem(), smem()],
        out_shape=[
            jax.ShapeDtypeStruct((24, tokens), F32),
            jax.ShapeDtypeStruct((tokens, 24), F32),
        ],
        compiler_params=kernel_params(),
    )(own, far, images, ids)


def store_split(ref, values):
    pieces, rows = ref.shape[0], ref.shape[2]
    for p in range(pieces):
        ref[p, 0] = values[p * rows:(p + 1) * rows].astype(ref.dtype)


def expert_one_kernel(row_ref, win_ref, mod_ref, gate_far_ref, *rest, tiles, first, kept):
    pieces_in, rest = rest[:tiles], rest[tiles + kept:]
    rows_ref, act_ref, slope_ref, gslot_ref, gw_ref, n2_ref, go_ref, gm_ref, sems = rest
    local = first + pl.program_id(0)
    tokens = n2_ref.shape[1]
    images = gm_ref.shape[1]
    each = tiles // 4

    @pl.when(pl.program_id(0) == 0)
    def _():
        targets = []
        for i, (ref, j) in enumerate(((n2_ref, 0), (n2_ref, 1), (go_ref, 0), (go_ref, 1))):
            targets += laid_out(pieces_in[i * each:(i + 1) * each], ref.at[j])
        sources = list(pieces_in) + [mod_ref.at[5], gate_far_ref]
        fetch(sources, targets + [gm_ref.at[0], gm_ref.at[1]], sems)

    def block(j, carry):
        where_ = row_ref[pl.ds(j * EXP_DEV + local, 1), :].astype(jnp.int32)
        mask = lax.broadcasted_iota(jnp.int32, (CAP, tokens), 0) == where_
        pick = mask.astype(BF)
        rows = dot(pick, n2_ref[j]).astype(BF)
        slots = pl.ds(pl.multiple_of(j * CAP, CAP), CAP)
        rows_ref[0, slots, :] = rows
        gates = row_ref[pl.ds(2 * EXP_DEV + j * EXP_DEV + local, 1), :]
        gate = jnp.sum(jnp.where(mask, gates, 0.0), axis=1, keepdims=True)
        image = jnp.sum(jnp.where(mask, row_ref[pl.ds(4 * EXP_DEV + j, 1), :], 0.0), axis=1, keepdims=True)
        hot = image_hot(image.astype(jnp.int32), images)
        grad = dot(hot, gm_ref[j]) * dot(pick, go_ref[j])
        gslot_ref[0, slots, :] = (gate * grad).astype(BF)
        value, slope = gelu_pair(dot(rows, win_ref[0]))
        act_ref[0, slots, :] = value.astype(BF)
        slope_ref[0, slots, :] = slope
        return carry

    lax.fori_loop(0, 2, block, 0)
    store_split(gw_ref, dot(gslot_ref[0], act_ref[0], 0, 0))


def expert_one(rows, mod, gate_far, w_in, tiles, pieces, first, kept):
    tokens = rows.shape[1]
    slots = 2 * CAP
    ff = w_in.shape[2]
    count = EXP_DEV // 2

    def shifted(*shape):
        return pl.BlockSpec((1,) + shape, lambda m: (m + first,) + (0,) * len(shape))

    fixed_ins = 4
    return pl.pallas_call(
        functools.partial(expert_one_kernel, tiles=len(tiles), first=first, kept=len(kept)),
        grid=(count,),
        in_specs=[fixed(*rows.shape), shifted(D, ff)] + [hbm()] * (2 + len(tiles) + len(kept)),
        out_specs=[
            shifted(slots, D), shifted(slots, ff), shifted(slots, ff), shifted(slots, D),
            pl.BlockSpec((pieces, 1, D // pieces, ff), lambda m: (0, m, 0, 0)),
        ],
        out_shape=[
            jax.ShapeDtypeStruct((EXP_DEV, slots, D), BF),
            jax.ShapeDtypeStruct((EXP_DEV, slots, ff), BF),
            jax.ShapeDtypeStruct((EXP_DEV, slots, ff), F32),
            jax.ShapeDtypeStruct((EXP_DEV, slots, D), BF),
            jax.ShapeDtypeStruct((pieces, count, D // pieces, ff), BF),
        ],
        scratch_shapes=[
            pltpu.VMEM((2, tokens, D), BF), pltpu.VMEM((2, tokens, D), BF), pltpu.VMEM((2,) + mod.shape[1:], BF),
            pltpu.SemaphoreType.DMA((len(tiles) + 2,)),
        ],
        input_output_aliases={fixed_ins + len(tiles) + i: i for i in range(len(kept))},
        compiler_params=kernel_params(),
    )(rows, w_in, mod, gate_far, *tiles, *kept)


def picked(col_ref, j, local):
    lanes = lax.broadcasted_iota(jnp.int32, col_ref.shape, 1)
    place = jnp.sum(jnp.where(lanes == j * EXP_DEV + local, col_ref[...], 0.0), axis=1, keepdims=True)
    slots = lax.broadcasted_iota(jnp.int32, (col_ref.shape[0], CAP), 1)
    return (slots == place.astype(jnp.int32)).astype(BF)


def expert_two_kernel(
    col_ref, rows_ref, slope_ref, gslot_ref, win_ref, wout_ref,
    gw_ref, gn_ref, gn_far_ref, gpre_ref, gn_acc,
):
    local = pl.program_id(0)

    @pl.when(local == 0)
    def _():
        gn_ref[...] = jnp.zeros_like(gn_ref)
        gn_acc[...] = jnp.zeros_like(gn_acc)

    for j, total in enumerate((gn_ref, gn_acc)):
        slots = slice(j * CAP, (j + 1) * CAP)
        grad_pre = (slope_ref[0, slots, :] * dot(gslot_ref[0, slots, :], wout_ref[0], 1, 1)).astype(BF)
        gpre_ref[slots, :] = grad_pre
        grad_in = dot(grad_pre, win_ref[0], 1, 1).astype(BF)
        total[...] += dot(picked(col_ref, j, local), grad_in)
    store_split(gw_ref, dot(rows_ref[0], gpre_ref[...], 0, 0))

    @pl.when(local == pl.num_programs(0) - 1)
    def _():
        gn_far_ref[...] = gn_acc[...].astype(BF)


def expert_two(cols, rows, slope, gslot, w_in, w_out, pieces):
    tokens = cols.shape[0]
    slots = 2 * CAP
    ff = w_in.shape[2]
    whole = fixed(tokens, D)
    return pl.pallas_call(
        expert_two_kernel,
        grid=(EXP_DEV,),
        in_specs=[
            fixed(*cols.shape), stepped(slots, D), stepped(slots, ff), stepped(slots, D),
            stepped(D, ff), stepped(ff, D),
        ],
        out_specs=[pl.BlockSpec((pieces, 1, D // pieces, ff), lambda m: (0, m, 0, 0)), whole, whole],
        out_shape=[
            jax.ShapeDtypeStruct((pieces, EXP_DEV, D // pieces, ff), BF),
            jax.ShapeDtypeStruct((tokens, D), F32),
            jax.ShapeDtypeStruct((tokens, D), BF),
        ],
        scratch_shapes=[pltpu.VMEM((slots, ff), BF), pltpu.VMEM((tokens, D), F32)],
        compiler_params=kernel_params(),
    )(cols, rows, slope, gslot, w_in, w_out)


def expert_mix_kernel(col_ref, act_ref, wout_ref, mix_ref, mix_far_ref, mix_acc):
    local = pl.program_id(0)
    lanes = lax.broadcasted_iota(jnp.int32, col_ref.shape, 1)

    @pl.when(local == 0)
    def _():
        mix_ref[...] = jnp.zeros_like(mix_ref)
        mix_acc[...] = jnp.zeros_like(mix_acc)

    for j, total in enumerate((mix_ref, mix_acc)):
        result = dot(act_ref[0, j * CAP:(j + 1) * CAP, :], wout_ref[0]).astype(BF)
        here = lanes == 2 * EXP_DEV + j * EXP_DEV + local
        gate = jnp.sum(jnp.where(here, col_ref[...], 0.0), axis=1, keepdims=True)
        total[...] += gate * dot(picked(col_ref, j, local), result)

    @pl.when(local == pl.num_programs(0) - 1)
    def _():
        mix_far_ref[...] = mix_acc[...].astype(BF)


def expert_mix(cols, act, w_out):
    tokens = cols.shape[0]
    ff = w_out.shape[1]
    whole = fixed(tokens, D)
    return pl.pallas_call(
        expert_mix_kernel,
        grid=(EXP_DEV,),
        in_specs=[fixed(*cols.shape), stepped(2 * CAP, ff), stepped(ff, D)],
        out_specs=[whole, whole],
        out_shape=[jax.ShapeDtypeStruct((tokens, D), F32), jax.ShapeDtypeStruct((tokens, D), BF)],
        scratch_shapes=[pltpu.VMEM((tokens, D), F32)],
        compiler_params=kernel_params(),
    )(cols, act, w_out)


def shared_kernel(img_ref, gm_ref, win_ref, wout_ref, core_ref, *rest, tiles):
    pieces_in, out_ref, gn_ref = rest[:tiles], rest[tiles + 1], rest[tiles + 2]
    gw_refs, rest = rest[tiles + 3:-6], rest[-6:]
    n2_ref, go_ref, act_ref, gs_ref, gpre_ref, sems = rest
    step = pl.program_id(0)
    ff = win_ref.shape[1]
    rows = out_ref.shape[0]
    here = pl.ds(pl.multiple_of(step * rows, rows), rows)

    @pl.when(step == 0)
    def _():
        each = tiles // 2
        fetch(pieces_in, laid_out(pieces_in[:each], n2_ref) + laid_out(pieces_in[each:], go_ref), sems)

    value, slope = gelu_pair(dot(n2_ref[here, :], win_ref[...]))
    act = value.astype(BF)
    act_ref[here, :] = act
    out_ref[...] = dot(act, wout_ref[...])
    gate = dot(image_hot(img_ref[...], gm_ref.shape[1]), gm_ref[0])
    grad = (gate * go_ref[here, :].astype(F32)).astype(BF)
    gs_ref[here, :] = grad
    gpre = (slope * dot(grad, wout_ref[...], 1, 1)).astype(BF)
    gpre_ref[here, :] = gpre
    gn_ref[...] = dot(gpre, win_ref[...], 1, 1)

    @pl.when(step == pl.num_programs(0) - 1)
    def _():
        store_rows(gw_refs, core_ref, dot(n2_ref[...], gpre_ref[...], 0, 0), slice(0, ff))
        store_rows(gw_refs, core_ref, dot(gs_ref[...], act_ref[...], 0, 0), slice(ff, 2 * ff))


def shared_both(core, pieces, tiles, img_col, mod, w_in, w_out, after):
    rows = tiles[0].shape[0]
    tokens = img_col.shape[0]
    steps = tokens // rows
    ff = w_in.shape[1]
    moving = pl.BlockSpec((rows, D), lambda m: (m, 0))
    specs, shapes = row_specs(1, pieces, 2 * ff, lambda m: 0, F32)
    return pl.pallas_call(
        functools.partial(shared_kernel, tiles=len(tiles)),
        grid=(steps,),
        in_specs=[
            pl.BlockSpec((rows, 1), lambda m: (m, 0)),
            gate_spec(mod), fixed(D, ff), fixed(ff, D), smem(),
        ] + [hbm()] * (len(tiles) + 1),
        out_specs=[moving, moving] + specs,
        out_shape=[
            jax.ShapeDtypeStruct((tokens, D), F32),
            jax.ShapeDtypeStruct((tokens, D), F32),
        ] + shapes,
        scratch_shapes=[
            pltpu.VMEM((tokens, D), BF), pltpu.VMEM((tokens, D), BF),
            pltpu.VMEM((tokens, ff), BF), pltpu.VMEM((tokens, D), BF), pltpu.VMEM((tokens, ff), BF),
            pltpu.SemaphoreType.DMA((len(tiles),)),
        ],
        compiler_params=kernel_params(),
    )(img_col, mod, w_in, w_out, core, *tiles, after)


def block(
    patches, cond, seg_ids, seg_image, routes, gates, grad_out,
    w_ada, w_qkv, w_out, w_shared_in, w_shared_out, w_expert_in, w_expert_out,
):
    tokens, feat = patches.shape
    parts = D // feat
    rows = tokens // parts
    pieces = lax.axis_size(DP)
    me = lax.axis_index(HID)
    core = lax.axis_index(EXP)
    bit_low = (me & 1) == 1
    bit_high = (me & 2) == 2

    def turned(items):
        a, b, c, d = items
        a, b = jnp.where(bit_low, b, a), jnp.where(bit_low, a, b)
        c, d = jnp.where(bit_low, d, c), jnp.where(bit_low, c, d)
        return [
            jnp.where(bit_high, c, a), jnp.where(bit_high, d, b),
            jnp.where(bit_high, a, c), jnp.where(bit_high, b, d),
        ]

    def across(value, mask):
        return lax.ppermute(value, HID, [(i, i ^ mask) for i in range(parts)])

    def other_core(value):
        return lax.ppermute(value, EXP, [(0, 1), (1, 0)])

    def exchanged(items):
        return [items[0]] + [across(items[m], m) for m in range(1, parts)]

    def gathered(value):
        return [value] + [across(value, m) for m in range(1, parts)]

    def passed_on(value):
        one, two = across(value, 1), across(value, 2)
        cut = value.shape[0] // 2
        return [one, two, across(one[:cut], 2), across(two[cut:], 1)]

    def blocks(value):
        return [value[i * rows:(i + 1) * rows] for i in range(parts)]

    def to_cols(value):
        cuts = [value[:, i * feat:(i + 1) * feat] for i in range(parts)]
        return jnp.concatenate(turned(exchanged(turned(cuts))), axis=0)

    packed = jnp.concatenate([w_qkv.reshape(D, 3 * feat), w_out.T], axis=1)
    half = lax.dynamic_slice_in_dim(packed, core * (D // 2), D // 2, axis=0)
    halves = passed_on(half)
    weights = [packed] + halves + [other_core(part) for part in halves]
    flip = lax.axis_index(DP) if pieces == 4 else jnp.zeros((), jnp.int32)
    core_id = jnp.stack([core, flip, me]).astype(jnp.int32)

    def both_rows(left, right):
        cuts = exchanged(turned(blocks(jnp.concatenate([left, right], axis=1))))
        cuts = turned(cuts)
        return [jnp.concatenate([cut[:, i * feat:(i + 1) * feat] for cut in cuts], axis=1) for i in range(2)]

    x_rows, go_rows = both_rows(patches, grad_out)
    silu_cond = jax.nn.silu(cond.astype(F32)).astype(BF)
    mod_own = jnp.einsum("id,dkc->kic", silu_cond, w_ada, preferred_element_type=F32).astype(BF)
    mod = jnp.concatenate(turned(gathered(mod_own)), axis=2)
    go_own = [go_rows] + passed_on(go_rows)
    gate_far = other_core(mod[5])
    go_far = [other_core(tile) for tile in go_own]

    images_flat = seg_image.reshape(1, -1).astype(F32)
    raw = jnp.concatenate(
        [
            routes.T.astype(F32), gates.T, seg_ids.reshape(1, tokens).astype(F32),
            jnp.pad(images_flat, ((0, 0), (0, tokens - images_flat.shape[1]))),
        ],
        axis=0,
    )
    raw_far = other_core(raw)
    image_ids = jnp.concatenate([images_flat, raw_far[5:, : images_flat.shape[1]]], axis=0).astype(jnp.int32)
    table_rows, table_cols = tables(raw, raw_far, image_ids, core_id)
    img_col = table_cols[:, 16:17].astype(jnp.int32)
    seg_col = table_cols[:, 18:19]
    seg_row = table_rows[18:19]

    ada_rows = D // (2 * pieces)
    place = lax.axis_index(DP) * 2 + core

    def images_and_silu(grads, silu):
        if pieces != 4:
            images = lax.all_gather(grads, (DP, EXP), axis=0, tiled=False)
            silu = lax.all_gather(silu, (DP, EXP), axis=0, tiled=False)
            return images, lax.dynamic_slice_in_dim(silu, place * ada_rows, ada_rows, axis=2)
        count, feat_own = grads.shape[1:]
        wide = 2 * ada_rows
        own = []
        for m in range(pieces):
            cols = lax.dynamic_slice_in_dim(silu, (flip ^ m) * wide, wide, axis=1)
            part = jnp.concatenate([grads.reshape(6 * count, feat_own), cols], axis=0)
            own.append(lax.ppermute(part, DP, [(i, i ^ m) for i in range(pieces)]) if m else part)
        own = jnp.stack(own)
        every = jnp.concatenate([own, other_core(own)], axis=0)
        cols = every[:, 6 * count:]
        cols = jnp.where(core == 0, cols[..., :ada_rows], cols[..., ada_rows:])
        return every[:, :6 * count].reshape(2 * pieces, 6, count, feat_own), cols

    n1, qkv, ctx, attn, mid, n2 = attn_forward(
        core_id, x_rows, img_col, mod, seg_col, seg_row, weights, [], parts,
    )
    n2_own = [n2] + passed_on(n2)
    n2_far = [other_core(tile) for tile in n2_own]
    tiles = n2_own + n2_far + go_own + go_far
    *kept, gw_out_low = expert_one(table_rows, mod, gate_far, w_expert_in, tiles, pieces, 0, [])
    shared_out, gn_shared, *gw_shared = shared_both(
        core_id, pieces, n2_own + go_own, img_col, mod, w_shared_in, w_shared_out, gw_out_low
    )

    def core_half(parts_of):
        if len(parts_of) == 1:
            values = parts_of[0]
            cut = values.reshape(values.shape[0], pieces, 2, D // (2 * pieces), values.shape[2])
            low, high = cut[:, :, 0], cut[:, :, 1]
            parts_of = jnp.where(core == 0, low, high), jnp.where(core == 0, high, low)
        return parts_of[0], other_core(parts_of[1])

    def over_dp(values):
        return lax.psum_scatter(values, DP, scatter_dimension=0, tiled=False).astype(F32)

    def pieces_over_dp(values):
        if pieces != 4:
            return over_dp(values.astype(BF))
        total = values[0]
        for m in range(1, pieces):
            moved = lax.ppermute(values[m].astype(BF), DP, [(i, i ^ m) for i in range(pieces)])
            total = total + moved.astype(F32)
        return total

    mine, theirs = core_half(gw_shared)
    half_shared = mine[0] + theirs[0]
    grad_shared = pieces_over_dp(half_shared)

    ge_out_low = over_dp(gw_out_low)
    *kept, gw_out_high = expert_one(
        table_rows, mod, gate_far, w_expert_in, tiles, pieces, EXP_DEV // 2, kept
    )
    ge_out_high = over_dp(gw_out_high)
    slot_rows, act, slope, gslot = kept
    gw_in, gn_near, gn_far = expert_two(table_cols, slot_rows, slope, gslot, w_expert_in, w_expert_out, pieces)
    grad_expert_in = over_dp(gw_in)
    mix_near, mix_far = expert_mix(table_cols, act, w_expert_out)

    def row_total(near, far, extra):
        from_core = other_core(far).astype(F32)
        cut = blocks(near + extra + from_core)
        out = cut[0]
        for m in range(1, parts):
            moved = across(cut[m].astype(BF), m)
            out = out + moved.astype(F32)
        return out

    gn2 = row_total(gn_near, gn_far, gn_shared)
    mlp = row_total(mix_near, mix_far, shared_out)

    gpatch, gmod_five, *gw_attn = attn_backward(
        core_id, pieces, gn2, mid, attn, go_rows, x_rows, n1, qkv, ctx, img_col, mod, seg_col, seg_row, weights
    )
    out_rows, gmod_last = finish(mid, mlp, go_rows, img_col, mod)
    block_out = to_cols(out_rows)
    grad_patches = to_cols(gpatch)

    gmod = jnp.concatenate([gmod_five, gmod_last[None]], axis=0)
    cuts = turned([gmod[:, :, i * feat:(i + 1) * feat] for i in range(parts)])
    got = exchanged(cuts)
    grad_image = (got[0] + got[1] + got[2] + got[3]).astype(BF)
    image_all, silu_mine = images_and_silu(grad_image, silu_cond)
    grad_ada = jnp.einsum("gid,gkic->dkc", silu_mine, image_all, preferred_element_type=F32)

    mine, theirs = core_half(gw_attn)
    attn_half = mine + theirs.astype(F32)
    attn_sum = attn_half[0]
    for m in range(1, parts):
        moved = across(attn_half[m].astype(BF), m)
        attn_sum = attn_sum + moved.astype(F32)
    grad_attn = pieces_over_dp(attn_sum)
    ff = w_shared_in.shape[1]
    return (
        block_out,
        grad_patches,
        grad_ada,
        grad_attn[:, : 3 * feat].reshape(ada_rows, 3, feat),
        grad_attn[:, 3 * feat:].T,
        grad_shared[:, :ff],
        grad_shared[:, ff:].T,
        grad_expert_in,
        jnp.swapaxes(jnp.concatenate([ge_out_low, ge_out_high], axis=0), 1, 2),
    )


def solution(mesh):
    rows = P((DP, EXP), None)
    tiles = P((DP, EXP), HID)
    return jax.shard_map(
        block,
        mesh=mesh,
        in_specs=(
            tiles, rows, rows, rows, rows, rows, tiles,
            P(None, None, HID),
            P(None, None, HID),
            P(HID, None),
            P(None, HID),
            P(HID, None),
            P(EXP, None, HID),
            P(EXP, HID, None),
        ),
        out_specs=(
            tiles,
            tiles,
            P((DP, EXP), None, HID),
            P((DP, EXP), None, HID),
            P(HID, (DP, EXP)),
            P((DP, EXP), HID),
            P(HID, (DP, EXP)),
            P(EXP, DP, HID),
            P(EXP, HID, DP),
        ),
        check_vma=False,
    )
```

```python
import functools

import jax
import jax.numpy as jnp
from jax import lax
from jax.experimental import pallas as pl
from jax.experimental.pallas import tpu as pltpu
from jax.sharding import PartitionSpec as P


D = 768
HEAD_DIM = 64
EXP_DEV = 4
CAP = 384
EPSILON = 1e-06
NEG_FILL = -1e30
DP, EXP, HID = "dp", "expert", "hidden"
BF = jnp.bfloat16
F32 = jnp.float32
GELU_C = 0.7978845608028654
GELU_A = 0.044715


def kernel_params():
    return pltpu.CompilerParams(vmem_limit_bytes=60 * 1024 * 1024)


def dot(a, b, lhs=1, rhs=0):
    return lax.dot_general(a, b, (((lhs,), (rhs,)), ((), ())), preferred_element_type=F32)


def gelu_pair(values):
    square = values * values
    inner = GELU_C * values * (1.0 + GELU_A * square)
    bent = jnp.tanh(inner)
    half = 0.5 * (1.0 + bent)
    slope = half + (0.5 * values) * (1.0 - bent * bent) * (GELU_C * (1.0 + (3.0 * GELU_A) * square))
    return values * half, slope


def normalize(values):
    centre = values - jnp.mean(values, axis=-1, keepdims=True)
    spread = lax.rsqrt(jnp.mean(centre * centre, axis=-1, keepdims=True) + EPSILON)
    return centre * spread, spread


def norm_back(upstream, unit, spread):
    return spread * (
        upstream
        - jnp.mean(upstream, axis=-1, keepdims=True)
        - unit * jnp.mean(upstream * unit, axis=-1, keepdims=True)
    )


def image_hot(image_col, count):
    lanes = lax.broadcasted_iota(jnp.int32, (image_col.shape[0], count), 1)
    return (image_col == lanes).astype(BF)


def probs_of(queries, keys, same):
    scores = dot(queries, keys, 1, 1) * (HEAD_DIM ** -0.5)
    scores = jnp.where(same, scores, NEG_FILL)
    raised = jnp.exp(scores - jnp.max(scores, axis=-1, keepdims=True))
    return raised * (1.0 / jnp.sum(raised, axis=-1, keepdims=True))


def attn_fwd_kernel(
    x_ref, img_ref, mod_ref, segc_ref, segr_ref, core_ref, *rest, shards, extras,
):
    w_in, rest = rest[:shards], rest[shards + extras:]
    n1_ref, qkv_ref, ctx_ref, attn_ref, mid_ref, n2_ref, w_ref, sems = rest
    step = pl.program_id(0)
    fetch_weights(w_in, w_ref, core_ref[0], sems)
    feat = ctx_ref.shape[2]
    images = mod_ref.shape[1]

    def mod(k):
        return dot(image_hot(img_ref[...], images), mod_ref[k])

    @pl.when(step == 0)
    def _():
        unit, _ = normalize(x_ref[...].astype(F32))
        n1_ref[...] = (unit * (1.0 + mod(1)) + mod(0)).astype(BF)
        attn_ref[...] = jnp.zeros_like(attn_ref)

    qkv = dot(n1_ref[...], w_ref[step, :, : 3 * feat]).astype(BF)
    qkv_ref[0] = qkv
    same = segc_ref[...] == segr_ref[...]
    parts = []
    for a in range(feat // HEAD_DIM):
        lo = a * HEAD_DIM
        probs = probs_of(qkv[:, lo:lo + HEAD_DIM], qkv[:, feat + lo:feat + lo + HEAD_DIM], same)
        parts.append(dot(probs.astype(BF), qkv[:, 2 * feat + lo:2 * feat + lo + HEAD_DIM]).astype(BF))
    context = jnp.concatenate(parts, axis=1)
    ctx_ref[0] = context
    attn_ref[...] += dot(context, w_ref[step, :, 3 * feat:], 1, 1)

    @pl.when(step == pl.num_programs(0) - 1)
    def _():
        mid = x_ref[...].astype(F32) + mod(2) * attn_ref[...]
        mid_ref[...] = mid
        unit, _ = normalize(mid)
        n2_ref[...] = (unit * (1.0 + mod(4)) + mod(3)).astype(BF)


def fixed(*shape):
    return pl.BlockSpec(shape, lambda m: (0,) * len(shape))


def stepped(*shape):
    return pl.BlockSpec((1,) + shape, lambda m: (m,) + (0,) * len(shape))


def attn_forward(core, x_rows, img_col, mod, seg_col, seg_row, weights, extras, parts):
    rows = x_rows.shape[0]
    feat = D // parts
    return pl.pallas_call(
        functools.partial(attn_fwd_kernel, shards=len(weights), extras=len(extras)),
        grid=(parts,),
        in_specs=[
            fixed(rows, D), fixed(rows, 1), fixed(*mod.shape), fixed(rows, 1), fixed(1, rows), smem(),
        ] + [hbm()] * (len(weights) + len(extras)),
        out_specs=[
            fixed(rows, D), stepped(rows, 3 * feat), stepped(rows, feat),
            fixed(rows, D), fixed(rows, D), fixed(rows, D),
        ],
        out_shape=[
            jax.ShapeDtypeStruct((rows, D), BF),
            jax.ShapeDtypeStruct((parts, rows, 3 * feat), BF),
            jax.ShapeDtypeStruct((parts, rows, feat), BF),
            jax.ShapeDtypeStruct((rows, D), F32),
            jax.ShapeDtypeStruct((rows, D), F32),
            jax.ShapeDtypeStruct((rows, D), BF),
        ],
        scratch_shapes=[pltpu.VMEM((parts, D, 4 * feat), BF), pltpu.SemaphoreType.DMA((len(weights),))],
        compiler_params=kernel_params(),
    )(x_rows, img_col, mod, seg_col, seg_row, core, *weights, *extras)


def image_sum(hot, values):
    high = values.astype(BF)
    rest = values - high.astype(F32)
    middle = rest.astype(BF)
    low = (rest - middle.astype(F32)).astype(BF)
    return dot(hot, high, 0, 0) + (dot(hot, middle, 0, 0) + dot(hot, low, 0, 0))


def attn_bwd_kernel(
    gn2_ref, mid_ref, attn_ref, go_ref, x_ref, n1_ref, qkv_ref, ctx_ref, img_ref, mod_ref,
    segc_ref, segr_ref, core_ref, *rest, shards,
):
    w_in, (gpatch_ref, gmod_ref), rest = rest[:shards], rest[shards:shards + 2], rest[shards + 2:]
    grad_refs, (gmid_ref, gattn_ref, gn1_ref, w_ref, sems) = rest[:-5], rest[-5:]
    step = pl.program_id(0)
    fetch_weights(w_in, w_ref, core_ref[0], sems)
    feat = ctx_ref.shape[2]
    images = mod_ref.shape[1]
    scale = HEAD_DIM ** -0.5

    def hot():
        return image_hot(img_ref[...], images)

    def mod(k):
        return dot(hot(), mod_ref[k])

    @pl.when(step == 0)
    def _():
        unit, spread = normalize(mid_ref[...])
        gn2 = gn2_ref[...]
        gmid = go_ref[...].astype(F32) + norm_back(gn2 * (1.0 + mod(4)), unit, spread)
        gmid_ref[...] = gmid
        gattn_ref[...] = (mod(2) * gmid).astype(BF)
        gmod_ref[2] = image_sum(hot(), gmid * attn_ref[...])
        gmod_ref[3] = image_sum(hot(), gn2)
        gmod_ref[4] = image_sum(hot(), gn2 * unit)
        gn1_ref[...] = jnp.zeros_like(gn1_ref)

    gattn = gattn_ref[...]
    gctx = dot(gattn, w_ref[step, :, 3 * feat:]).astype(BF)
    same = segc_ref[...] == segr_ref[...]
    gq, gk, gv = [], [], []
    for a in range(feat // HEAD_DIM):
        lo = a * HEAD_DIM
        queries = qkv_ref[0, :, lo:lo + HEAD_DIM]
        keys = qkv_ref[0, :, feat + lo:feat + lo + HEAD_DIM]
        values = qkv_ref[0, :, 2 * feat + lo:2 * feat + lo + HEAD_DIM]
        gc = gctx[:, lo:lo + HEAD_DIM]
        probs = probs_of(queries, keys, same)
        gv.append(dot(probs.astype(BF), gc, 0, 0).astype(BF))
        gp = dot(gc, values, 1, 1)
        inner = jnp.sum(probs * gp, axis=-1, keepdims=True)
        gs = (probs * (gp - inner)).astype(BF)
        gq.append((dot(gs, keys) * scale).astype(BF))
        gk.append((dot(gs, queries, 0, 0) * scale).astype(BF))
    grows = jnp.concatenate(gq + gk + gv, axis=1)
    store_rows(grad_refs, core_ref, dot(n1_ref[...], grows, 0, 0), slice(0, 3 * feat))
    store_rows(grad_refs, core_ref, dot(gattn, ctx_ref[0], 0, 0), slice(3 * feat, 4 * feat))
    gn1_ref[...] += dot(grows, w_ref[step, :, : 3 * feat], 1, 1)

    @pl.when(step == pl.num_programs(0) - 1)
    def _():
        unit, spread = normalize(x_ref[...].astype(F32))
        gn1 = gn1_ref[...]
        back = norm_back(gn1 * (1.0 + mod(1)), unit, spread)
        gpatch_ref[...] = (gmid_ref[...] + back).astype(BF)
        gmod_ref[0] = image_sum(hot(), gn1)
        gmod_ref[1] = image_sum(hot(), gn1 * unit)


def store_rows(refs, core_ref, values, cols):
    if len(refs) == 1:
        refs[0][0, :, cols] = values
        return
    mine, theirs = refs
    pieces, rows = mine.shape[1], mine.shape[2]
    for p in range(pieces):
        low = values[2 * p * rows:(2 * p + 1) * rows]
        high = values[(2 * p + 1) * rows:(2 * p + 2) * rows]
        mine[0, p ^ core_ref[1], :, cols] = jnp.where(core_ref[0] == 0, low, high)
        theirs[0, p ^ core_ref[1], :, cols] = jnp.where(core_ref[0] == 0, high, low).astype(theirs.dtype)


def row_specs(parts, pieces, width, index, away):
    rows = D // (2 * pieces)
    if rows % 8:
        shape = (D, width)
        count = 1
    else:
        shape = (pieces, rows, width)
        count = 2
    spec = pl.BlockSpec((1,) + shape, lambda m: (index(m),) + (0,) * len(shape))
    return [spec] * count, [jax.ShapeDtypeStruct((parts,) + shape, kind) for kind in (F32, away)[:count]]


def smem():
    return pl.BlockSpec(memory_space=pltpu.SMEM)


def hbm():
    return pl.BlockSpec(memory_space=pl.ANY)


def fetch(refs, targets, sems):
    copies = [pltpu.make_async_copy(refs[i], targets[i], sems.at[i]) for i in range(len(refs))]
    for copy in copies:
        copy.start()
    for copy in copies:
        copy.wait()


def laid_out(refs, target):
    places, start = [], 0
    for ref in refs:
        places.append(target.at[pl.ds(start, ref.shape[0])])
        start += ref.shape[0]
    return places


def weight_copies(refs, w_ref, core, sems):
    half = D // 2
    mine = pl.multiple_of(core * half, half)
    theirs = pl.multiple_of((1 - core) * half, half)
    places = [(0, w_ref.at[0])]
    for base in (mine, theirs):
        for m in (1, 2):
            places.append((m, w_ref.at[m, pl.ds(base, half)]))
        for k in (0, 1):
            places.append((3, w_ref.at[3, pl.ds(pl.multiple_of(base + k * (half // 2), half // 2), half // 2)]))
    return [(m, pltpu.make_async_copy(ref, place, sems.at[i])) for i, (ref, (m, place)) in enumerate(zip(refs, places))]


def fetch_weights(refs, w_ref, core, sems):
    step = pl.program_id(0)
    copies = weight_copies(refs, w_ref, core, sems)

    @pl.when(step == 0)
    def _():
        for _, copy in copies:
            copy.start()

    for shard in range(w_ref.shape[0]):
        @pl.when(step == shard)
        def _():
            for m, copy in copies:
                if m == shard:
                    copy.wait()


def attn_backward(core, pieces, gn2, mid, attn, go, x_rows, n1, qkv, ctx, img_col, mod, seg_col, seg_row, weights):
    rows = x_rows.shape[0]
    parts = qkv.shape[0]
    feat = D // parts
    images = mod.shape[1]
    whole = fixed(rows, D)
    specs, shapes = row_specs(parts, pieces, 4 * feat, lambda m: m, BF)
    return pl.pallas_call(
        functools.partial(attn_bwd_kernel, shards=len(weights)),
        grid=(parts,),
        in_specs=[
            whole, whole, whole, whole, whole, whole,
            stepped(rows, 3 * feat), stepped(rows, feat),
            fixed(rows, 1), fixed(*mod.shape), fixed(rows, 1), fixed(1, rows),
            smem(),
        ] + [hbm()] * len(weights),
        out_specs=[whole, fixed(5, images, D)] + specs,
        out_shape=[
            jax.ShapeDtypeStruct((rows, D), BF),
            jax.ShapeDtypeStruct((5, images, D), F32),
        ] + shapes,
        scratch_shapes=[
            pltpu.VMEM((rows, D), F32), pltpu.VMEM((rows, D), BF), pltpu.VMEM((rows, D), F32),
            pltpu.VMEM((parts, D, 4 * feat), BF), pltpu.SemaphoreType.DMA((len(weights),)),
        ],
        compiler_params=kernel_params(),
    )(gn2, mid, attn, go, x_rows, n1, qkv, ctx, img_col, mod, seg_col, seg_row, core, *weights)


def finish_kernel(mid_ref, mlp_ref, go_ref, img_ref, gate_ref, out_ref, gmod_ref):
    hot = image_hot(img_ref[...], gate_ref.shape[1])
    mlp = mlp_ref[...]
    out_ref[...] = (mid_ref[...] + dot(hot, gate_ref[0]) * mlp).astype(BF)
    gmod_ref[...] = image_sum(hot, go_ref[...].astype(F32) * mlp)


def gate_spec(mod):
    return pl.BlockSpec((1,) + mod.shape[1:], lambda m: (5, 0, 0))


def finish(mid, mlp, go, img_col, mod):
    rows = mid.shape[0]
    whole = fixed(rows, D)
    return pl.pallas_call(
        finish_kernel,
        grid=(1,),
        in_specs=[whole, whole, whole, fixed(rows, 1), gate_spec(mod)],
        out_specs=[whole, fixed(*mod.shape[1:])],
        out_shape=[
            jax.ShapeDtypeStruct(mid.shape, BF),
            jax.ShapeDtypeStruct(mod.shape[1:], F32),
        ],
        compiler_params=kernel_params(),
    )(mid, mlp, go, img_col, mod)


def tables_kernel(own_ref, far_ref, image_ref, ids_ref, row_ref, col_ref, img_ref, segc_ref, segr_ref):
    core, me = ids_ref[0], ids_ref[2]
    tokens = own_ref.shape[1]
    parts = 4
    size = tokens // parts
    segs = image_ref.shape[1] // parts
    hots, gates, images, seg_rows = [], [], [], []
    for j, ref in enumerate((own_ref, far_ref)):
        tiles, pictures = [], []
        for m in range(parts):
            tile = ref[:, pl.ds(pl.multiple_of((me ^ m) * size, size), size)]
            seg = tile[4:5]
            image = jnp.zeros_like(seg)
            for k in range(segs):
                image = jnp.where(seg == float(k), image_ref[j, (me ^ m) * segs + k].astype(F32), image)
            tiles.append(tile)
            pictures.append(image)
        table = jnp.concatenate(tiles, axis=1)
        images.append(jnp.concatenate(pictures, axis=1))
        seg_rows.append(table[4:5])
        experts = (lax.broadcasted_iota(jnp.int32, (EXP_DEV, tokens), 0) + core * EXP_DEV).astype(F32)
        first, second = table[0:1] == experts, table[1:2] == experts
        hots.append(jnp.where(first | second, 1.0, 0.0))
        gates.append(jnp.where(first, table[2:3], jnp.where(second, table[3:4], 0.0)))
    hot = jnp.concatenate(hots, axis=0)
    before = lax.broadcasted_iota(jnp.int32, (tokens, tokens), 0) <= lax.broadcasted_iota(jnp.int32, (tokens, tokens), 1)
    slot = dot(hot.astype(BF), before.astype(BF))
    pos = jnp.where(hot > 0.5, slot - 1.0, -1.0)
    rest = jnp.concatenate(images + seg_rows + [jnp.zeros((4, tokens), F32)], axis=0)
    rows = jnp.concatenate([pos] + gates + [rest], axis=0)
    row_ref[...] = rows
    cols = rows.T
    col_ref[...] = cols
    img_ref[...] = cols[:, 4 * EXP_DEV:4 * EXP_DEV + 1].astype(jnp.int32)
    segc_ref[...] = cols[:, 4 * EXP_DEV + 2:4 * EXP_DEV + 3]
    segr_ref[...] = rows[4 * EXP_DEV + 2:4 * EXP_DEV + 3]


def tables(own, far, images, ids):
    tokens = own.shape[1]
    return pl.pallas_call(
        tables_kernel,
        in_specs=[pl.BlockSpec(own.shape, lambda: (0, 0)), pl.BlockSpec(far.shape, lambda: (0, 0)), smem(), smem()],
        out_shape=[
            jax.ShapeDtypeStruct((24, tokens), F32),
            jax.ShapeDtypeStruct((tokens, 24), F32),
            jax.ShapeDtypeStruct((tokens, 1), jnp.int32),
            jax.ShapeDtypeStruct((tokens, 1), F32),
            jax.ShapeDtypeStruct((1, tokens), F32),
        ],
        compiler_params=kernel_params(),
    )(own, far, images, ids)


def store_split(ref, values):
    pieces, rows = ref.shape[0], ref.shape[2]
    for p in range(pieces):
        ref[p, 0] = values[p * rows:(p + 1) * rows].astype(ref.dtype)


def expert_one_kernel(row_ref, win_ref, mod_ref, gate_far_ref, *rest, tiles, first, kept):
    pieces_in, rest = rest[:tiles], rest[tiles + kept:]
    rows_ref, act_ref, slope_ref, gslot_ref, gw_ref, n2_ref, go_ref, gm_ref, sems = rest
    local = first + pl.program_id(0)
    tokens = n2_ref.shape[1]
    images = gm_ref.shape[1]
    each = tiles // 4

    @pl.when(pl.program_id(0) == 0)
    def _():
        targets = []
        for i, (ref, j) in enumerate(((n2_ref, 0), (n2_ref, 1), (go_ref, 0), (go_ref, 1))):
            targets += laid_out(pieces_in[i * each:(i + 1) * each], ref.at[j])
        sources = list(pieces_in) + [mod_ref.at[5], gate_far_ref]
        fetch(sources, targets + [gm_ref.at[0], gm_ref.at[1]], sems)

    def block(j, carry):
        where_ = row_ref[pl.ds(j * EXP_DEV + local, 1), :].astype(jnp.int32)
        mask = lax.broadcasted_iota(jnp.int32, (CAP, tokens), 0) == where_
        pick = mask.astype(BF)
        rows = dot(pick, n2_ref[j]).astype(BF)
        slots = pl.ds(pl.multiple_of(j * CAP, CAP), CAP)
        rows_ref[0, slots, :] = rows
        gates = row_ref[pl.ds(2 * EXP_DEV + j * EXP_DEV + local, 1), :]
        gate = jnp.sum(jnp.where(mask, gates, 0.0), axis=1, keepdims=True)
        image = jnp.sum(jnp.where(mask, row_ref[pl.ds(4 * EXP_DEV + j, 1), :], 0.0), axis=1, keepdims=True)
        hot = image_hot(image.astype(jnp.int32), images)
        grad = dot(hot, gm_ref[j]) * dot(pick, go_ref[j])
        gslot_ref[0, slots, :] = (gate * grad).astype(BF)
        value, slope = gelu_pair(dot(rows, win_ref[0]))
        act_ref[0, slots, :] = value.astype(BF)
        slope_ref[0, slots, :] = slope
        return carry

    lax.fori_loop(0, 2, block, 0)
    store_split(gw_ref, dot(gslot_ref[0], act_ref[0], 0, 0))


def expert_one(rows, mod, gate_far, w_in, tiles, pieces, first, count, kept):
    tokens = rows.shape[1]
    slots = 2 * CAP
    ff = w_in.shape[2]

    def shifted(*shape):
        return pl.BlockSpec((1,) + shape, lambda m: (m + first,) + (0,) * len(shape))

    fixed_ins = 4
    return pl.pallas_call(
        functools.partial(expert_one_kernel, tiles=len(tiles), first=first, kept=len(kept)),
        grid=(count,),
        in_specs=[fixed(*rows.shape), shifted(D, ff)] + [hbm()] * (2 + len(tiles) + len(kept)),
        out_specs=[
            shifted(slots, D), shifted(slots, ff), shifted(slots, ff), shifted(slots, D),
            pl.BlockSpec((pieces, 1, D // pieces, ff), lambda m: (0, m, 0, 0)),
        ],
        out_shape=[
            jax.ShapeDtypeStruct((EXP_DEV, slots, D), BF),
            jax.ShapeDtypeStruct((EXP_DEV, slots, ff), BF),
            jax.ShapeDtypeStruct((EXP_DEV, slots, ff), F32),
            jax.ShapeDtypeStruct((EXP_DEV, slots, D), BF),
            jax.ShapeDtypeStruct((pieces, count, D // pieces, ff), BF),
        ],
        scratch_shapes=[
            pltpu.VMEM((2, tokens, D), BF), pltpu.VMEM((2, tokens, D), BF), pltpu.VMEM((2,) + mod.shape[1:], BF),
            pltpu.SemaphoreType.DMA((len(tiles) + 2,)),
        ],
        input_output_aliases={fixed_ins + len(tiles) + i: i for i in range(len(kept))},
        compiler_params=kernel_params(),
    )(rows, w_in, mod, gate_far, *tiles, *kept)


def picked(col_ref, j, local):
    lanes = lax.broadcasted_iota(jnp.int32, col_ref.shape, 1)
    place = jnp.sum(jnp.where(lanes == j * EXP_DEV + local, col_ref[...], 0.0), axis=1, keepdims=True)
    slots = lax.broadcasted_iota(jnp.int32, (col_ref.shape[0], CAP), 1)
    return (slots == place.astype(jnp.int32)).astype(BF)


def expert_two_kernel(
    col_ref, rows_ref, slope_ref, gslot_ref, win_ref, wout_ref,
    gw_ref, gn_ref, gn_far_ref, gpre_ref, gn_acc,
):
    local = pl.program_id(0)

    @pl.when(local == 0)
    def _():
        gn_ref[...] = jnp.zeros_like(gn_ref)
        gn_acc[...] = jnp.zeros_like(gn_acc)

    for j, total in enumerate((gn_ref, gn_acc)):
        slots = slice(j * CAP, (j + 1) * CAP)
        grad_pre = (slope_ref[0, slots, :] * dot(gslot_ref[0, slots, :], wout_ref[0], 1, 1)).astype(BF)
        gpre_ref[slots, :] = grad_pre
        grad_in = dot(grad_pre, win_ref[0], 1, 1).astype(BF)
        total[...] += dot(picked(col_ref, j, local), grad_in)
    store_split(gw_ref, dot(rows_ref[0], gpre_ref[...], 0, 0))

    @pl.when(local == pl.num_programs(0) - 1)
    def _():
        gn_far_ref[...] = gn_acc[...].astype(BF)


def expert_two(cols, rows, slope, gslot, w_in, w_out, pieces):
    tokens = cols.shape[0]
    slots = 2 * CAP
    ff = w_in.shape[2]
    whole = fixed(tokens, D)
    return pl.pallas_call(
        expert_two_kernel,
        grid=(EXP_DEV,),
        in_specs=[
            fixed(*cols.shape), stepped(slots, D), stepped(slots, ff), stepped(slots, D),
            stepped(D, ff), stepped(ff, D),
        ],
        out_specs=[pl.BlockSpec((pieces, 1, D // pieces, ff), lambda m: (0, m, 0, 0)), whole, whole],
        out_shape=[
            jax.ShapeDtypeStruct((pieces, EXP_DEV, D // pieces, ff), BF),
            jax.ShapeDtypeStruct((tokens, D), F32),
            jax.ShapeDtypeStruct((tokens, D), BF),
        ],
        scratch_shapes=[pltpu.VMEM((slots, ff), BF), pltpu.VMEM((tokens, D), F32)],
        compiler_params=kernel_params(),
    )(cols, rows, slope, gslot, w_in, w_out)


def expert_mix_kernel(col_ref, act_ref, wout_ref, mix_ref, mix_far_ref, mix_acc):
    local = pl.program_id(0)
    lanes = lax.broadcasted_iota(jnp.int32, col_ref.shape, 1)

    @pl.when(local == 0)
    def _():
        mix_ref[...] = jnp.zeros_like(mix_ref)
        mix_acc[...] = jnp.zeros_like(mix_acc)

    for j, total in enumerate((mix_ref, mix_acc)):
        result = dot(act_ref[0, j * CAP:(j + 1) * CAP, :], wout_ref[0]).astype(BF)
        here = lanes == 2 * EXP_DEV + j * EXP_DEV + local
        gate = jnp.sum(jnp.where(here, col_ref[...], 0.0), axis=1, keepdims=True)
        total[...] += gate * dot(picked(col_ref, j, local), result)

    @pl.when(local == pl.num_programs(0) - 1)
    def _():
        mix_far_ref[...] = mix_acc[...].astype(BF)


def expert_mix(cols, act, w_out):
    tokens = cols.shape[0]
    ff = w_out.shape[1]
    whole = fixed(tokens, D)
    return pl.pallas_call(
        expert_mix_kernel,
        grid=(EXP_DEV,),
        in_specs=[fixed(*cols.shape), stepped(2 * CAP, ff), stepped(ff, D)],
        out_specs=[whole, whole],
        out_shape=[jax.ShapeDtypeStruct((tokens, D), F32), jax.ShapeDtypeStruct((tokens, D), BF)],
        scratch_shapes=[pltpu.VMEM((tokens, D), F32)],
        compiler_params=kernel_params(),
    )(cols, act, w_out)


def shared_kernel(img_ref, gm_ref, win_ref, wout_ref, core_ref, *rest, tiles):
    pieces_in, out_ref, gn_ref = rest[:tiles], rest[tiles + 1], rest[tiles + 2]
    gw_refs, rest = rest[tiles + 3:-6], rest[-6:]
    n2_ref, go_ref, act_ref, gs_ref, gpre_ref, sems = rest
    step = pl.program_id(0)
    ff = win_ref.shape[1]
    rows = out_ref.shape[0]
    here = pl.ds(pl.multiple_of(step * rows, rows), rows)

    @pl.when(step == 0)
    def _():
        each = tiles // 2
        fetch(pieces_in, laid_out(pieces_in[:each], n2_ref) + laid_out(pieces_in[each:], go_ref), sems)

    value, slope = gelu_pair(dot(n2_ref[here, :], win_ref[...]))
    act = value.astype(BF)
    act_ref[here, :] = act
    out_ref[...] = dot(act, wout_ref[...])
    gate = dot(image_hot(img_ref[...], gm_ref.shape[1]), gm_ref[0])
    grad = (gate * go_ref[here, :].astype(F32)).astype(BF)
    gs_ref[here, :] = grad
    gpre = (slope * dot(grad, wout_ref[...], 1, 1)).astype(BF)
    gpre_ref[here, :] = gpre
    gn_ref[...] = dot(gpre, win_ref[...], 1, 1)

    @pl.when(step == pl.num_programs(0) - 1)
    def _():
        store_rows(gw_refs, core_ref, dot(n2_ref[...], gpre_ref[...], 0, 0), slice(0, ff))
        store_rows(gw_refs, core_ref, dot(gs_ref[...], act_ref[...], 0, 0), slice(ff, 2 * ff))


def shared_both(core, pieces, tiles, img_col, mod, w_in, w_out, after):
    rows = tiles[0].shape[0]
    tokens = img_col.shape[0]
    steps = tokens // rows
    ff = w_in.shape[1]
    moving = pl.BlockSpec((rows, D), lambda m: (m, 0))
    specs, shapes = row_specs(1, pieces, 2 * ff, lambda m: 0, F32)
    return pl.pallas_call(
        functools.partial(shared_kernel, tiles=len(tiles)),
        grid=(steps,),
        in_specs=[
            pl.BlockSpec((rows, 1), lambda m: (m, 0)),
            gate_spec(mod), fixed(D, ff), fixed(ff, D), smem(),
        ] + [hbm()] * (len(tiles) + 1),
        out_specs=[moving, moving] + specs,
        out_shape=[
            jax.ShapeDtypeStruct((tokens, D), F32),
            jax.ShapeDtypeStruct((tokens, D), F32),
        ] + shapes,
        scratch_shapes=[
            pltpu.VMEM((tokens, D), BF), pltpu.VMEM((tokens, D), BF),
            pltpu.VMEM((tokens, ff), BF), pltpu.VMEM((tokens, D), BF), pltpu.VMEM((tokens, ff), BF),
            pltpu.SemaphoreType.DMA((len(tiles),)),
        ],
        compiler_params=kernel_params(),
    )(img_col, mod, w_in, w_out, core, *tiles, after)


def block(
    patches, cond, seg_ids, seg_image, routes, gates, grad_out,
    w_ada, w_qkv, w_out, w_shared_in, w_shared_out, w_expert_in, w_expert_out,
):
    tokens, feat = patches.shape
    parts = D // feat
    rows = tokens // parts
    pieces = lax.axis_size(DP)
    me = lax.axis_index(HID)
    core = lax.axis_index(EXP)
    bit_low = (me & 1) == 1
    bit_high = (me & 2) == 2

    def turned(items):
        a, b, c, d = items
        a, b = jnp.where(bit_low, b, a), jnp.where(bit_low, a, b)
        c, d = jnp.where(bit_low, d, c), jnp.where(bit_low, c, d)
        return [
            jnp.where(bit_high, c, a), jnp.where(bit_high, d, b),
            jnp.where(bit_high, a, c), jnp.where(bit_high, b, d),
        ]

    def across(value, mask):
        return lax.ppermute(value, HID, [(i, i ^ mask) for i in range(parts)])

    def other_core(value):
        return lax.ppermute(value, EXP, [(0, 1), (1, 0)])

    def exchanged(items):
        return [items[0]] + [across(items[m], m) for m in range(1, parts)]

    def gathered(value):
        return [value] + [across(value, m) for m in range(1, parts)]

    def passed_on(value):
        one, two = across(value, 1), across(value, 2)
        cut = value.shape[0] // 2
        return [one, two, across(one[:cut], 2), across(two[cut:], 1)]

    def blocks(value):
        return [value[i * rows:(i + 1) * rows] for i in range(parts)]

    def to_cols(value):
        cuts = [value[:, i * feat:(i + 1) * feat] for i in range(parts)]
        return jnp.concatenate(turned(exchanged(turned(cuts))), axis=0)

    packed = jnp.concatenate([w_qkv.reshape(D, 3 * feat), w_out.T], axis=1)
    half = lax.dynamic_slice_in_dim(packed, core * (D // 2), D // 2, axis=0)
    halves = passed_on(half)
    weights = [packed] + halves + [other_core(part) for part in halves]
    flip = lax.axis_index(DP) if pieces == 4 else jnp.zeros((), jnp.int32)
    core_id = jnp.stack([core, flip, me]).astype(jnp.int32)

    def both_rows(left, right):
        cuts = exchanged(turned(blocks(jnp.concatenate([left, right], axis=1))))
        cuts = turned(cuts)
        return [jnp.concatenate([cut[:, i * feat:(i + 1) * feat] for cut in cuts], axis=1) for i in range(2)]

    x_rows, go_rows = both_rows(patches, grad_out)
    silu_cond = jax.nn.silu(cond.astype(F32)).astype(BF)
    mod_own = jnp.einsum("id,dkc->kic", silu_cond, w_ada, preferred_element_type=F32).astype(BF)
    mod = jnp.concatenate(turned(gathered(mod_own)), axis=2)
    go_own = [go_rows] + passed_on(go_rows)
    gate_far = other_core(mod[5])
    go_far = [other_core(tile) for tile in go_own]

    images_flat = seg_image.reshape(1, -1).astype(F32)
    raw = jnp.concatenate(
        [
            routes.T.astype(F32), gates.T, seg_ids.reshape(1, tokens).astype(F32),
            jnp.pad(images_flat, ((0, 0), (0, tokens - images_flat.shape[1]))),
        ],
        axis=0,
    )
    raw_far = other_core(raw)
    image_ids = jnp.concatenate([images_flat, raw_far[5:, : images_flat.shape[1]]], axis=0).astype(jnp.int32)
    table_rows, table_cols, img_col, seg_col, seg_row = tables(raw, raw_far, image_ids, core_id)

    ada_rows = D // (2 * pieces)
    place = lax.axis_index(DP) * 2 + core

    def images_and_silu(grads, silu):
        if pieces != 4:
            images = lax.all_gather(grads, (DP, EXP), axis=0, tiled=False)
            silu = lax.all_gather(silu, (DP, EXP), axis=0, tiled=False)
            return images, lax.dynamic_slice_in_dim(silu, place * ada_rows, ada_rows, axis=2)
        count, feat_own = grads.shape[1:]
        wide = 2 * ada_rows
        own = []
        for m in range(pieces):
            cols = lax.dynamic_slice_in_dim(silu, (flip ^ m) * wide, wide, axis=1)
            part = jnp.concatenate([grads.reshape(6 * count, feat_own), cols], axis=0)
            own.append(lax.ppermute(part, DP, [(i, i ^ m) for i in range(pieces)]) if m else part)
        own = jnp.stack(own)
        every = jnp.concatenate([own, other_core(own)], axis=0)
        cols = every[:, 6 * count:]
        cols = jnp.where(core == 0, cols[..., :ada_rows], cols[..., ada_rows:])
        return every[:, :6 * count].reshape(2 * pieces, 6, count, feat_own), cols

    n1, qkv, ctx, attn, mid, n2 = attn_forward(
        core_id, x_rows, img_col, mod, seg_col, seg_row, weights, [], parts,
    )
    n2_own = [n2] + passed_on(n2)
    n2_far = [other_core(tile) for tile in n2_own]
    tiles = n2_own + n2_far + go_own + go_far
    *kept, gw_out_low = expert_one(table_rows, mod, gate_far, w_expert_in, tiles, pieces, 0, 1, [])
    *kept, gw_out_high = expert_one(
        table_rows, mod, gate_far, w_expert_in, tiles, pieces, 1, EXP_DEV - 1, kept
    )
    shared_out, gn_shared, *gw_shared = shared_both(
        core_id, pieces, n2_own + go_own, img_col, mod, w_shared_in, w_shared_out, gw_out_high
    )

    def core_half(parts_of):
        if len(parts_of) == 1:
            values = parts_of[0]
            cut = values.reshape(values.shape[0], pieces, 2, D // (2 * pieces), values.shape[2])
            low, high = cut[:, :, 0], cut[:, :, 1]
            parts_of = jnp.where(core == 0, low, high), jnp.where(core == 0, high, low)
        return parts_of[0], other_core(parts_of[1])

    def over_dp(values):
        return lax.psum_scatter(values, DP, scatter_dimension=0, tiled=False).astype(F32)

    def pieces_over_dp(values):
        if pieces != 4:
            return over_dp(values.astype(BF))
        total = values[0]
        for m in range(1, pieces):
            moved = lax.ppermute(values[m].astype(BF), DP, [(i, i ^ m) for i in range(pieces)])
            total = total + moved.astype(F32)
        return total

    mine, theirs = core_half(gw_shared)
    half_shared = mine[0] + theirs[0]
    grad_shared = pieces_over_dp(half_shared)

    ge_out_low = over_dp(gw_out_low)
    ge_out_high = over_dp(gw_out_high)
    slot_rows, act, slope, gslot = kept
    gw_in, gn_near, gn_far = expert_two(table_cols, slot_rows, slope, gslot, w_expert_in, w_expert_out, pieces)
    grad_expert_in = over_dp(gw_in)
    mix_near, mix_far = expert_mix(table_cols, act, w_expert_out)

    def row_total(near, far, extra):
        from_core = other_core(far).astype(F32)
        cut = blocks(near + extra + from_core)
        out = cut[0]
        for m in range(1, parts):
            moved = across(cut[m].astype(BF), m)
            out = out + moved.astype(F32)
        return out

    gn2 = row_total(gn_near, gn_far, gn_shared)
    mlp = row_total(mix_near, mix_far, shared_out)

    gpatch, gmod_five, *gw_attn = attn_backward(
        core_id, pieces, gn2, mid, attn, go_rows, x_rows, n1, qkv, ctx, img_col, mod, seg_col, seg_row, weights
    )
    out_rows, gmod_last = finish(mid, mlp, go_rows, img_col, mod)
    block_out = to_cols(out_rows)
    grad_patches = to_cols(gpatch)

    gmod = jnp.concatenate([gmod_five, gmod_last[None]], axis=0)
    cuts = turned([gmod[:, :, i * feat:(i + 1) * feat] for i in range(parts)])
    got = exchanged(cuts)
    grad_image = (got[0] + got[1] + got[2] + got[3]).astype(BF)
    image_all, silu_mine = images_and_silu(grad_image, silu_cond)
    grad_ada = jnp.einsum("gid,gkic->dkc", silu_mine, image_all, preferred_element_type=F32)

    mine, theirs = core_half(gw_attn)
    attn_half = mine + theirs.astype(F32)
    attn_sum = attn_half[0]
    for m in range(1, parts):
        moved = across(attn_half[m].astype(BF), m)
        attn_sum = attn_sum + moved.astype(F32)
    grad_attn = pieces_over_dp(attn_sum)
    ff = w_shared_in.shape[1]
    grad_expert_out = jnp.swapaxes(jnp.concatenate([ge_out_low, ge_out_high], axis=0), 1, 2)
    return (
        block_out,
        grad_patches,
        grad_ada,
        grad_attn[:, : 3 * feat].reshape(ada_rows, 3, feat),
        grad_attn[:, 3 * feat:].T,
        grad_shared[:, :ff],
        grad_shared[:, ff:].T,
        grad_expert_in,
        grad_expert_out,
    )


def solution(mesh):
    rows = P((DP, EXP), None)
    tiles = P((DP, EXP), HID)
    return jax.shard_map(
        block,
        mesh=mesh,
        in_specs=(
            tiles, rows, rows, rows, rows, rows, tiles,
            P(None, None, HID),
            P(None, None, HID),
            P(HID, None),
            P(None, HID),
            P(HID, None),
            P(EXP, None, HID),
            P(EXP, HID, None),
        ),
        out_specs=(
            tiles,
            tiles,
            P((DP, EXP), None, HID),
            P((DP, EXP), None, HID),
            P(HID, (DP, EXP)),
            P((DP, EXP), HID),
            P(HID, (DP, EXP)),
            P(EXP, DP, HID),
            P(EXP, HID, DP),
        ),
        check_vma=False,
    )
```
